32 devices in a mesh: batch: 2 (over y), wide: 16 (over z, x, core).
Axes of the slice: x: 2, y: 2, z: 4, core: 2. Of those that a mesh axis runs over, the one named last changes fastest.
Arguments:
- inputs: float32 [4, 1536, 512], P('batch', 'wide'), may hold values from -6 to 6
- lengths: int32 [4], P('batch'), may hold values from 384 to 1536, as said below
- cotangent: float32 [4, 1536, 512], P('batch', 'wide'), may hold values from -6 to 6
- qkv_weight: float32 [2, 512, 1536], P(None, 'wide'), may hold values from -0.25 to 0.25
- proj_weight: float32 [2, 512, 512], P(None, 'wide'), may hold values from -3.5 to 3.5
- up_weight: float32 [2, 512, 2048], P(None, 'wide'), may hold values from -0.25 to 0.25
- down_weight: float32 [2, 2048, 512], P(None, 'wide'), may hold values from -0.125 to 0.125
- pool_weight: float32 [2, 512, 1536], P(None, 'wide'), may hold values from -0.1875 to 0.1875
- norm_params: float32 [2, 512, 4], P(None, 'wide')
- qkv_velocity: float32 [2, 512, 1536], P(None, 'wide'), may hold values from -96 to 96
- proj_velocity: float32 [2, 512, 512], P(None, 'wide'), may hold values from -96 to 96
- up_velocity: float32 [2, 512, 2048], P(None, 'wide'), may hold values from -96 to 96
- down_velocity: float32 [2, 2048, 512], P(None, 'wide'), may hold values from -96 to 96
- pool_velocity: float32 [2, 512, 1536], P(None, 'wide'), may hold values from -96 to 96
- norm_velocity: float32 [2, 512, 4], P(None, 'wide'), may hold values from -224 to 224
- qkv_average: float32 [2, 512, 1536], P(None, 'wide'), may hold values from -0.25 to 0.25
- proj_average: float32 [2, 512, 512], P(None, 'wide'), may hold values from -3.5 to 3.5
- up_average: float32 [2, 512, 2048], P(None, 'wide'), may hold values from -0.25 to 0.25
- down_average: float32 [2, 2048, 512], P(None, 'wide'), may hold values from -0.125 to 0.125
- pool_average: float32 [2, 512, 1536], P(None, 'wide'), may hold values from -0.1875 to 0.1875
- norm_average: float32 [2, 512, 4], P(None, 'wide')
Outputs:
- activations: float32 [4, 1536, 512], P('batch', 'wide')
- input_grad: float32 [4, 1536, 512], P('batch', 'wide')
- qkv_grad: float32 [2, 512, 1536], P(None, 'wide')
- proj_grad: float32 [2, 512, 512], P(None, 'wide')
- up_grad: float32 [2, 512, 2048], P(None, 'wide')
- down_grad: float32 [2, 2048, 512], P(None, 'wide')
- pool_grad: float32 [2, 512, 1536], P(None, 'wide')
- norm_grad: float32 [2, 512, 4], P(None, 'wide')
- qkv_momentum: float32 [2, 512, 1536], P(None, 'wide')
- proj_momentum: float32 [2, 512, 512], P(None, 'wide')
- up_momentum: float32 [2, 512, 2048], P(None, 'wide')
- down_momentum: float32 [2, 2048, 512], P(None, 'wide')
- pool_momentum: float32 [2, 512, 1536], P(None, 'wide')
- norm_momentum: float32 [2, 512, 4], P(None, 'wide')
- qkv_smooth: float32 [2, 512, 1536], P(None, 'wide')
- proj_smooth: float32 [2, 512, 512], P(None, 'wide')
- up_smooth: float32 [2, 512, 2048], P(None, 'wide')
- down_smooth: float32 [2, 2048, 512], P(None, 'wide')
- pool_smooth: float32 [2, 512, 1536], P(None, 'wide')
- norm_smooth: float32 [2, 512, 4], P(None, 'wide')
- qkv_updated: float32 [2, 512, 1536], P(None, 'wide')
- proj_updated: float32 [2, 512, 512], P(None, 'wide')
- up_updated: float32 [2, 512, 2048], P(None, 'wide')
- down_updated: float32 [2, 2048, 512], P(None, 'wide')
- pool_updated: float32 [2, 512, 1536], P(None, 'wide')
- norm_updated: float32 [2, 512, 4], P(None, 'wide')
The draws below stay inside these ranges and needn't reach their ends.
Inputs may be any that keep to these rules, and one draw needn't show every extreme that they name: `lengths`: every length is a multiple of 3; one sequence has 1536 used positions and one has 384.
All inputs are finite; a program needn't handle non-finite values.
Results may differ from the reference program's by a relative error of at most 0.0003.
Values sent between devices are 32-bit elements; how exact they have to be, the bound alone decides.
No kernel may reach another device: no remote copies, remote signals or barrier semaphores. Data moves between devices by JAX's collectives and lax.ppermute only.
A program may use at most 256 MiB of HBM per device.

```python
import math
import jax
import jax.numpy as jnp
from jax import lax

D = 512
HEADS = 8
HEAD_DIM = 64
FF = 2048
SEQ = 1536
SEQS = 4


def draw_lengths(key, part):
    lowest = SEQ // 12
    drawn_len = 3 * jax.random.randint(key, (SEQS,), lowest, SEQ // 3 + 1)
    return drawn_len.at[0].set(SEQ).at[1].set(3 * lowest).astype(jnp.int32)


def norm_columns(key):
    gain_cols = jax.random.uniform(jax.random.fold_in(key, 11), (2, D, 2), jnp.float32, 0.5, 1.5)
    shift_cols = 0.3 * jax.random.normal(jax.random.fold_in(key, 12), (2, D, 2), jnp.float32)
    return jnp.stack([gain_cols[..., 0], shift_cols[..., 0], gain_cols[..., 1], shift_cols[..., 1]], axis=-1)


def draw_norm_params(key, part):
    return norm_columns(jax.random.fold_in(key, 3))


def draw_norm_average(key, part):
    return norm_columns(jax.random.fold_in(key, 7))


def block_levels(key, extent, shards, smallest, high):
    def one(axis_at, parts):
        steps = jax.random.uniform(jax.random.fold_in(jax.random.fold_in(key, 6), axis_at), (parts,), jnp.float32, smallest / len(shards), high / len(shards))
        return jnp.repeat(jnp.exp(steps), extent[axis_at] // parts).reshape((-1,) + (1,) * (len(extent) - axis_at - 1))

    factor_of = one(*shards[0])
    for cut in shards[1:]:
        factor_of = factor_of * one(*cut)
    return factor_of


def gaussian(rng, dims, deviation, bound, shards=(), held_as=jnp.bfloat16):
    gain = block_levels(rng, dims, shards, -0.22, 0.18) if shards else 1.0
    array = jax.random.normal(rng, dims, jnp.float32) * deviation * gain
    return jnp.minimum(jnp.maximum(array, -bound), bound).astype(held_as)


def setup_inputs(seed: int = 0) -> dict:
    splits = jax.random.split(jax.random.key(seed), 22)
    return {
        "inputs": gaussian(splits[0], (SEQS, SEQ, D), 1.0, 6.0, ((0, 2), (1, 16)), jnp.float32),
        "lengths": draw_lengths(jax.random.fold_in(splits[21], 71), 0),
        "cotangent": gaussian(splits[2], (SEQS, SEQ, D), 1.0, 6.0, ((0, 2), (1, 16)), jnp.float32),
        "qkv_weight": gaussian(splits[3], (2, D, 3 * D), D ** -0.5, 0.25, ((1, 16),), jnp.float32),
        "proj_weight": gaussian(splits[4], (2, D, D), ((SEQ / (9 * D)) ** 0.5), 3.5, ((1, 16),), jnp.float32),
        "up_weight": gaussian(splits[5], (2, D, FF), D ** -0.5, 0.25, ((1, 16),), jnp.float32),
        "down_weight": gaussian(splits[6], (2, FF, D), FF ** -0.5, 0.125, ((1, 16),), jnp.float32),
        "pool_weight": gaussian(splits[7], (2, D, 3 * D), (2 * D) ** -0.5, 0.1875, ((1, 16),), jnp.float32),
        "norm_params": draw_norm_params(jax.random.fold_in(splits[21], 71), 0),
        "qkv_velocity": gaussian(splits[9], (2, D, 3 * D), (0.2 * (SEQS * SEQ) ** 0.5), 96.0, ((1, 16),), jnp.float32),
        "proj_velocity": gaussian(splits[10], (2, D, D), (0.2 * (SEQS * SEQ) ** 0.5), 96.0, ((1, 16),), jnp.float32),
        "up_velocity": gaussian(splits[11], (2, D, FF), (0.2 * (SEQS * SEQ) ** 0.5), 96.0, ((1, 16),), jnp.float32),
        "down_velocity": gaussian(splits[12], (2, FF, D), (0.2 * (SEQS * SEQ) ** 0.5), 96.0, ((1, 16),), jnp.float32),
        "pool_velocity": gaussian(splits[13], (2, D, 3 * D), (0.2 * (SEQS * SEQ) ** 0.5), 96.0, ((1, 16),), jnp.float32),
        "norm_velocity": gaussian(splits[14], (2, D, 4), (0.5 * (SEQS * SEQ) ** 0.5), 224.0, ((1, 16),), jnp.float32),
        "qkv_average": gaussian(splits[15], (2, D, 3 * D), D ** -0.5, 0.25, ((1, 16),), jnp.float32),
        "proj_average": gaussian(splits[16], (2, D, D), ((SEQ / (9 * D)) ** 0.5), 3.5, ((1, 16),), jnp.float32),
        "up_average": gaussian(splits[17], (2, D, FF), D ** -0.5, 0.25, ((1, 16),), jnp.float32),
        "down_average": gaussian(splits[18], (2, FF, D), FF ** -0.5, 0.125, ((1, 16),), jnp.float32),
        "pool_average": gaussian(splits[19], (2, D, 3 * D), (2 * D) ** -0.5, 0.1875, ((1, 16),), jnp.float32),
        "norm_average": draw_norm_average(jax.random.fold_in(splits[21], 71), 0),
    }


HIGHEST = lax.Precision.HIGHEST
norm_eps = 1e-05
masked_score = -1e+30
momentum_decay = 0.9
average_decay = 0.9

@jax.custom_vjp
def low(v):
    return lax.optimization_barrier(v.astype(jnp.bfloat16)).astype(jnp.float32)

@jax.custom_vjp
def low_back(v):
    return v

def low_keep(v):
    return (low(v), None)

def low_pass(kept, grad):
    return (grad,)

def back_keep(v):
    return (v, None)

def back_low(kept, grad):
    return (low(grad),)
low.defvjp(low_keep, low_pass)
low_back.defvjp(back_keep, back_low)

def layer_norm(values, gain_col, shift_col):
    centred = values - lax.optimization_barrier(jnp.mean(values, axis=-1, keepdims=True))
    variance = lax.optimization_barrier(jnp.mean(centred * centred, axis=-1, keepdims=True))
    return centred * lax.rsqrt(variance + norm_eps) * gain_col + shift_col

def rotate(tensor, positions):
    half_dim = tensor.shape[-1] // 2
    inv_freq = 10000.0 ** (-2.0 * jnp.arange(half_dim, dtype=jnp.float32) / tensor.shape[-1])
    angles = positions.astype(jnp.float32)[:, None] * inv_freq[None, :]
    cosine = jnp.cos(angles)[:, None, :]
    sine_part = jnp.sin(angles)[:, None, :]
    lower_half = tensor[..., :half_dim]
    upper_half = tensor[..., half_dim:]
    return jnp.concatenate([lower_half * cosine - upper_half * sine_part, lower_half * sine_part + upper_half * cosine], axis=-1)

def attend(queries, key_heads, value_heads, length):
    seq_len = queries.shape[0]
    q_block = math.gcd(seq_len, 512)
    block_count = seq_len // q_block
    score_scale = queries.shape[-1] ** (-0.5)
    query_blocks = queries.reshape(block_count, q_block, HEADS, HEAD_DIM)
    block_starts = jnp.arange(block_count, dtype=jnp.int32) * q_block
    key_pos = jnp.arange(seq_len, dtype=jnp.int32)

    @jax.checkpoint
    def one_block(members):
        query_blk, block_start = members
        query_pos = block_start + jnp.arange(q_block, dtype=jnp.int32)
        scores = jnp.einsum('qhe,khe->hqk', query_blk, key_heads, precision=HIGHEST) * score_scale
        allowed = (key_pos[None, :] <= query_pos[:, None]) & (key_pos[None, :] < length)
        scores = jnp.where(allowed[None], scores, masked_score)
        probs = jax.nn.softmax(scores, axis=-1)
        return jnp.einsum('hqk,khe->qhe', probs, value_heads, precision=HIGHEST)
    result = lax.map(one_block, (query_blocks, block_starts))
    return result.reshape(seq_len, HEADS * HEAD_DIM)

def block(stream, qkv_mat, proj_mat, up_mat, down_mat, norm_cols, positions, length):
    row_count = stream.shape[0]
    normed = layer_norm(stream, norm_cols[:, 0], norm_cols[:, 1])
    packed = jnp.dot(normed, qkv_mat, precision=HIGHEST).reshape(row_count, 3, HEADS, HEAD_DIM)
    queries = rotate(packed[:, 0], positions)
    key_heads = rotate(packed[:, 1], positions)
    attended = attend(queries, key_heads, packed[:, 2], length)
    mixed = stream + jnp.dot(attended, proj_mat, precision=HIGHEST)
    normed_two = layer_norm(mixed, norm_cols[:, 2], norm_cols[:, 3])
    hidden = jax.nn.gelu(jnp.dot(normed_two, up_mat, precision=HIGHEST), approximate=True)
    return mixed + jnp.dot(hidden, down_mat, precision=HIGHEST)

def hourglass(stream, length, params):
    qkv_weight, proj_weight, up_weight, down_weight, pool_weight, norm_params = params
    seq_len = stream.shape[0]
    model_width = stream.shape[1]
    full_out = block(stream, qkv_weight[0], proj_weight[0], up_weight[0], down_weight[0], norm_params[0], jnp.arange(seq_len, dtype=jnp.int32), length)
    shifted = jnp.concatenate([jnp.zeros((2, model_width), stream.dtype), full_out[:-2]], axis=0)
    shortened = jnp.einsum('jid,die->je', shifted.reshape(seq_len // 3, 3, model_width), pool_weight[0].reshape(model_width, 3, model_width), precision=HIGHEST)
    short_out = block(shortened, qkv_weight[1], proj_weight[1], up_weight[1], down_weight[1], norm_params[1], jnp.arange(seq_len // 3, dtype=jnp.int32), length // 3)
    return full_out + jnp.dot(short_out, pool_weight[1], precision=HIGHEST).reshape(seq_len, model_width)

def update(grad, weight, velocity, average, rate):
    momentum = momentum_decay * velocity + grad
    updated = weight - rate * (grad + momentum_decay * momentum)
    smooth = average_decay * average + (1.0 - average_decay) * updated
    return (momentum, smooth, updated)

def reference(inputs, lengths, cotangent, qkv_weight, proj_weight, up_weight, down_weight, pool_weight, norm_params, qkv_velocity, proj_velocity, up_velocity, down_velocity, pool_velocity, norm_velocity, qkv_average, proj_average, up_average, down_average, pool_average, norm_average):
    params = (qkv_weight, proj_weight, up_weight, down_weight, pool_weight, norm_params)

    def forward(stream_all, weights):
        return lax.map(lambda members: hourglass(members[0], members[1], weights), (stream_all, lengths))
    activations, pullback = jax.vjp(forward, inputs, params)
    seq_len = inputs.shape[1]
    valid = (jnp.arange(seq_len, dtype=jnp.int32)[None, :] < lengths[:, None]).astype(inputs.dtype)
    input_grad, grads = pullback(cotangent * valid[..., None])
    rate = 0.5 / math.sqrt(D * SEQS * SEQ)
    velocities = (qkv_velocity, proj_velocity, up_velocity, down_velocity, pool_velocity, norm_velocity)
    averages = (qkv_average, proj_average, up_average, down_average, pool_average, norm_average)
    results = [update(grads[number], params[number], velocities[number], averages[number], rate) for number in range(6)]
    return (activations, input_grad, grads[0], grads[1], grads[2], grads[3], grads[4], grads[5], results[0][0], results[1][0], results[2][0], results[3][0], results[4][0], results[5][0], results[0][1], results[1][1], results[2][1], results[3][1], results[4][1], results[5][1], results[0][2], results[1][2], results[2][2], results[3][2], results[4][2], results[5][2])
```

```python
import functools
import math

import jax
import jax.numpy as jnp
import numpy as np
from jax import lax
from jax.experimental import pallas as pl
from jax.experimental.pallas import tpu as pltpu
from jax.sharding import Mesh, PartitionSpec as P

HEADS = 8
HEAD_DIM = 64
D = HEADS * HEAD_DIM
HIGH = lax.Precision.HIGH
norm_eps = 1e-05
masked_score = -1e30
momentum_decay = 0.9
average_decay = 0.9
F32 = jnp.float32
BF16 = jnp.bfloat16
VMEM_LIMIT = 56 << 20


def matmul(left, right):
    return jnp.dot(left, right, precision=HIGH)


def layer_norm(values, gain, shift):
    centred = values - jnp.mean(values, axis=-1, keepdims=True)
    variance = jnp.mean(centred * centred, axis=-1, keepdims=True)
    return centred * lax.rsqrt(variance + norm_eps) * gain + shift


def split(value):
    high = value.astype(BF16)
    return high, (value - high.astype(F32)).astype(BF16)


def dot(a, b, dims):
    return lax.dot_general(a, b, (dims, ((), ())), preferred_element_type=F32)


NN = ((1,), (0,))
NT = ((1,), (1,))
TN = ((0,), (0,))


def rope_tables(rows):
    half = HEAD_DIM // 2
    freq = (10000.0 ** (-2.0 * np.arange(half, dtype=np.float32) / HEAD_DIM)).astype(np.float32)
    angles = np.arange(rows, dtype=np.float32)[:, None] * freq[None, :]
    cosine = np.cos(angles).astype(np.float32)
    sine = np.sin(angles).astype(np.float32)
    both = np.concatenate([cosine, cosine], axis=1)
    signed = np.concatenate([-sine, sine], axis=1)
    return (
        np.concatenate([both, both], axis=1),
        np.concatenate([signed, signed], axis=1),
        np.ascontiguousarray(cosine.T),
        np.ascontiguousarray(sine.T),
    )


def swap_halves(pair):
    half = HEAD_DIM // 2
    width = pair.shape[1]
    lane = lax.broadcasted_iota(jnp.int32, pair.shape, 1) % HEAD_DIM
    ahead = pltpu.roll(pair, width - half, 1)
    behind = pltpu.roll(pair, half, 1)
    return jnp.where(lane < half, ahead, behind)


def allowed_keys(first_row, rows, keys, length):
    key_pos = lax.broadcasted_iota(jnp.int32, (keys, rows), 0)
    query_pos = lax.broadcasted_iota(jnp.int32, (keys, rows), 1) + first_row
    return (key_pos <= query_pos) & (key_pos < length)


def attend_rows(raw, length, cos_ref, sin_ref, out_refs, rows, step, half_rows):
    packed_ref, turned_ref, lse_ref, qcat_ref, kcat_ref, vcat_ref = out_refs
    scale = HEAD_DIM ** (-0.5)
    for start in range(0, rows, step):
        part = slice(start, start + step)
        pair = raw[part, : 2 * HEAD_DIM]
        pair = pair * cos_ref[part, :] + swap_halves(pair) * sin_ref[part, :]
        lane = lax.broadcasted_iota(jnp.int32, pair.shape, 1)
        pair = jnp.where(lane < HEAD_DIM, pair * scale, pair)
        high, low = split(pair)
        qh, kh = high[:, :HEAD_DIM], high[:, HEAD_DIM:]
        ql, kl = low[:, :HEAD_DIM], low[:, HEAD_DIM:]
        vh, vl = split(raw[part, 2 * HEAD_DIM :])
        qcat_ref[part, :] = jnp.concatenate([qh, ql, qh], axis=1)
        kcat_ref[part, :] = jnp.concatenate([kh, kh, kl], axis=1)
        vcat_ref[part, :] = jnp.concatenate([vh, vh, vl], axis=1)
    value_pair = jnp.transpose(vcat_ref[:, HEAD_DIM:].astype(F32)).astype(BF16)
    value_high = value_pair[:HEAD_DIM]
    for start in range(0, rows, step):
        part = slice(start, start + step)
        keys = start + step
        scores = dot(kcat_ref[:keys, :], qcat_ref[part, :], NT)
        scores = jnp.where(allowed_keys(start, step, keys, length), scores, masked_score)
        row_max = jnp.max(scores, axis=0, keepdims=True)
        weights = jnp.exp(scores - row_max)
        total = jnp.sum(weights, axis=0, keepdims=True)
        wh, wl = split(weights)
        summed = dot(value_pair[:, :keys], wh, NN)
        summed = summed[:HEAD_DIM] + summed[HEAD_DIM:] + dot(value_high[:, :keys], wl, NN)
        turned = summed / total
        lse_ref[:, part] = jnp.broadcast_to(row_max + jnp.log(total), (8, step))
        turned_ref[:, part] = turned
    attended = jnp.transpose(
        jnp.concatenate([turned_ref[...], turned_ref[...]], axis=0)
    ).reshape(rows // (2 * half_rows), 2, half_rows, 2 * HEAD_DIM)
    lane = lax.broadcasted_iota(jnp.int32, attended[:, 0].shape, 2)
    packed_ref[...] = jnp.where(lane < HEAD_DIM, attended[:, 0], attended[:, 1])


def first_attend_kernel(
    half_rows, step, slots, len_ref, chip_ref, xa_ref, xb_ref, w_ref, cos_ref, sin_ref, *refs
):
    out_refs, norm_ref, raw = refs[:6], refs[6], refs[7]
    chips = xa_ref.shape[0]
    rows = chips * 2 * half_rows
    total = jnp.sum(xa_ref[:, half_rows:, :], axis=0) + jnp.sum(xb_ref[:, half_rows:, :], axis=0)
    norm_ref[...] = total
    gain, shift = total[0:1], total[1:2]
    wh, wl = split(w_ref[...])
    for chip in range(chips):
        for side, ref in enumerate((xa_ref, xb_ref)):
            slot = slots[side](chip_ref[0] ^ chip)
            hh, hl = split(layer_norm(ref[slot, :half_rows, :], gain, shift))
            first = (chip * 2 + side) * half_rows
            raw[first : first + half_rows, :] = dot(hh, wh, NN) + dot(hh, wl, NN) + dot(hl, wh, NN)
    attend_rows(raw, len_ref[0], cos_ref, sin_ref, out_refs, rows, step, half_rows)


def unpack_rows(packed_ref, raw, half_rows, width):
    chips = packed_ref.shape[0]
    for chip in range(chips):
        for side in range(2):
            first = (chip * 2 + side) * half_rows
            raw[first : first + half_rows, :] = packed_ref[
                chip, :, side * width : (side + 1) * width
            ]


def second_attend_kernel(half_rows, step, len_ref, packed_ref, cos_ref, sin_ref, *refs):
    out_refs, raw = refs[:6], refs[6]
    rows = packed_ref.shape[0] * 2 * half_rows
    unpack_rows(packed_ref, raw, half_rows, 3 * HEAD_DIM)
    attend_rows(raw, len_ref[0], cos_ref, sin_ref, out_refs, rows, step, half_rows)


def attend_grad(
    rows, step, half_rows, length, refs, grad_ref, tables, out_ref, scratch
):
    qcat_ref, kcat_ref, vcat_ref, turned_ref, lse_ref = refs
    cos_ref, sin_ref, cos_t_ref, sin_t_ref = tables
    grad_rows, dk_acc, dv_acc, dq_t, dqkv = scratch
    scale = HEAD_DIM ** (-0.5)
    unpack_rows(grad_ref, grad_rows, half_rows, HEAD_DIM)
    key_pair = jnp.transpose(kcat_ref[:, HEAD_DIM:].astype(F32)).astype(BF16)
    key_high = key_pair[:HEAD_DIM]
    dk_acc[...] = jnp.zeros_like(dk_acc)
    dv_acc[...] = jnp.zeros_like(dv_acc)
    for start in range(0, rows, step):
        part = slice(start, start + step)
        keys = start + step
        grad = grad_rows[part, :]
        gh, gl = split(grad)
        gcat = jnp.concatenate([gh, gl, gh], axis=1)
        grad_t = jnp.transpose(jnp.concatenate([grad, grad], axis=1))[:HEAD_DIM]
        delta = jnp.sum(grad_t * turned_ref[:, part], axis=0, keepdims=True)
        scores = dot(kcat_ref[:keys, :], qcat_ref[part, :], NT)
        probs = jnp.where(
            allowed_keys(start, step, keys, length), jnp.exp(scores - lse_ref[0:1, part]), 0.0
        )
        grad_probs = dot(vcat_ref[:keys, :], gcat, NT)
        grad_scores = probs * (grad_probs - delta)
        ph, pw = split(probs)
        sh, sl = split(grad_scores)
        dv_acc[:keys, :] += dot(ph, gcat[:, : 2 * HEAD_DIM], NN)
        dv_acc[:keys, :HEAD_DIM] += dot(pw, gh, NN)
        dk_acc[:keys, :] += dot(sh, qcat_ref[part, : 2 * HEAD_DIM], NN)
        dk_acc[:keys, :HEAD_DIM] += dot(sl, qcat_ref[part, :HEAD_DIM], NN)
        turned = dot(key_pair[:, :keys], sh, NN)
        turned = turned[:HEAD_DIM] + turned[HEAD_DIM:] + dot(key_high[:, :keys], sl, NN)
        dq_t[:, part] = turned * scale
    half = HEAD_DIM // 2
    low, high = dq_t[:half, :], dq_t[half:, :]
    back_low = low * cos_t_ref[...] + high * sin_t_ref[...]
    back_high = high * cos_t_ref[...] - low * sin_t_ref[...]
    dq = jnp.transpose(jnp.concatenate([back_low, back_high, back_low, back_high], axis=0))
    for start in range(0, rows, step):
        part = slice(start, start + step)
        dk = dk_acc[part, :HEAD_DIM] + dk_acc[part, HEAD_DIM:]
        dk = jnp.concatenate([dk, dk], axis=1)
        dk = dk * cos_ref[part, :] - swap_halves(dk) * sin_ref[part, :]
        dv = dv_acc[part, :HEAD_DIM] + dv_acc[part, HEAD_DIM:]
        dqkv[part, :] = jnp.concatenate([dq[part, :HEAD_DIM], dk[:, :HEAD_DIM], dv], axis=1)
    chips = out_ref.shape[0]
    for chip in range(chips):
        first = chip * 2 * half_rows
        out_ref[chip, :, :] = jnp.concatenate(
            [dqkv[first : first + half_rows, :], dqkv[first + half_rows : first + 2 * half_rows, :]],
            axis=1,
        )


def second_grad_kernel(
    half_rows, step, len_ref, q_ref, k_ref, v_ref, t_ref, l_ref, g_ref, c, s, ct, st, out_ref, *scratch
):
    rows = q_ref.shape[0]
    refs = (q_ref, k_ref, v_ref, t_ref, l_ref)
    attend_grad(rows, step, half_rows, len_ref[0], refs, g_ref, (c, s, ct, st), out_ref, scratch)


def first_grad_kernel(
    half_rows,
    step,
    slots,
    len_ref,
    chip_ref,
    xa_ref,
    xb_ref,
    q_ref,
    k_ref,
    v_ref,
    t_ref,
    l_ref,
    g_ref,
    c,
    s,
    ct,
    st,
    out_ref,
    m_ref,
    *scratch,
):
    rows = q_ref.shape[0]
    refs = (q_ref, k_ref, v_ref, t_ref, l_ref)
    attend_grad(rows, step, half_rows, len_ref[0], refs, g_ref, (c, s, ct, st), out_ref, scratch[:5])
    dqkv, nh_ref, nl_ref = scratch[4:]
    chips = xa_ref.shape[0]
    for chip in range(chips):
        for side, ref in enumerate((xa_ref, xb_ref)):
            slot = slots[side](chip_ref[0] ^ chip)
            nh, nl = split(layer_norm(ref[slot, :half_rows, :], 1.0, 0.0))
            first = (chip * 2 + side) * half_rows
            nh_ref[first : first + half_rows, :] = nh
            nl_ref[first : first + half_rows, :] = nl
    dh, dl = split(dqkv[...])
    nh = nh_ref[...]
    product = dot(nh, dh, TN) + dot(nh, dl, TN) + dot(nl_ref[...], dh, TN)
    owners, rows_each = m_ref.shape[0], m_ref.shape[1] - 8
    column = jnp.sum(dqkv[...], axis=0, keepdims=True)
    m_ref[:, :rows_each, :] = product.reshape(owners, rows_each, 3 * HEAD_DIM)
    m_ref[:, rows_each:, :] = jnp.broadcast_to(column[None], (owners, 8, 3 * HEAD_DIM))


SMEM = pl.BlockSpec(memory_space=pltpu.SMEM)
VMEM = pl.BlockSpec(memory_space=pltpu.VMEM)


def attend_outs(rows, half_rows):
    width = 3 * HEAD_DIM
    return [
        jax.ShapeDtypeStruct((rows // (2 * half_rows), half_rows, 2 * HEAD_DIM), F32),
        jax.ShapeDtypeStruct((HEAD_DIM, rows), F32),
        jax.ShapeDtypeStruct((8, rows), F32),
        jax.ShapeDtypeStruct((rows, width), BF16),
        jax.ShapeDtypeStruct((rows, width), BF16),
        jax.ShapeDtypeStruct((rows, width), BF16),
    ]


def call(kernel, outs, scratch, scalars, flops, *args):
    size = sum(math.prod(a.shape) * a.dtype.itemsize for a in list(args) + list(outs))
    return pl.pallas_call(
        kernel,
        out_shape=outs,
        in_specs=[SMEM] * scalars + [VMEM] * (len(args) - scalars),
        out_specs=[VMEM] * len(outs),
        scratch_shapes=scratch,
        compiler_params=pltpu.CompilerParams(vmem_limit_bytes=VMEM_LIMIT),
        cost_estimate=pl.CostEstimate(flops=flops, bytes_accessed=size, transcendentals=0),
    )(*args)


def query_step(rows):
    return math.gcd(rows, 256)


def bit_count(size):
    return size.bit_length() - 1


def swap_with(value, axis, size, mask):
    return lax.ppermute(value, axis, [(i, i ^ mask) for i in range(size)])


class Layout:
    def __init__(self, groups, ranks, cores):
        self.groups = groups
        self.ranks = ranks
        self.cores = cores
        self.chips = HEADS * ranks
        self.devices = self.chips * cores
        self.chip_axes = ("h", "r") if ranks > 1 else ("h",)

    def chip(self):
        return lax.axis_index("h") * self.ranks + lax.axis_index("r")

    def swap_chip(self, value, mask):
        if self.ranks == 1:
            return swap_with(value, "h", HEADS, mask)
        route = [(i, i ^ mask) for i in range(self.chips)]
        return lax.ppermute(value, ("h", "r"), route)

    def shift_chip(self, value, distance):
        chips = range(self.chips)
        route = [(i - distance, i) for i in chips if i - distance in chips]
        return lax.ppermute(value, ("h", "r") if self.ranks > 1 else "h", route)

    def gather_chips(self, value, masks):
        held = value[None]
        for mask in masks:
            held = jnp.concatenate([held, self.swap_chip(held, mask)], axis=0)
        return held

    def slot_of(self, masks):
        def slot(distance):
            found = 0
            for place, mask in enumerate(masks):
                bit = mask.bit_length() - 1
                found = found + (((distance >> bit) & 1) << place)
            return found

        return slot

    def heads_to_rows(self, value):
        value = value.reshape((HEADS, self.ranks) + value.shape[1:])
        mine = lax.dynamic_index_in_dim(value, lax.axis_index("r"), 1, keepdims=False)
        return lax.all_to_all(mine, "h", 0, 0, tiled=True)

    def rows_to_heads(self, value):
        got = lax.all_to_all(value, "h", 0, 0, tiled=True)
        if self.ranks > 1:
            got = lax.all_gather(got, "r", axis=1, tiled=False)
            got = got.reshape((self.chips,) + value.shape[1:])
        return got

    def reduce_owned(self, grads, first_batch):
        bits = bit_count(self.chips)
        rows = grads.shape[1]
        state = grads.reshape((2,) * bits + (self.cores, rows, D))
        core = lax.axis_index("s")
        chip = self.chip()
        group = lax.axis_index("b")

        def halve(state, place, bit, send):
            keep = lax.dynamic_index_in_dim(state, bit, place, keepdims=False)
            away = lax.dynamic_index_in_dim(state, 1 - bit, place, keepdims=False)
            return keep + send(away)

        state = halve(state, bits, core, lambda v: swap_with(v, "s", 2, 1))

        def batch_stages(state):
            for place in range(bit_count(self.groups)):
                dim = state.ndim - 2
                count = state.shape[dim]
                state = state.reshape(state.shape[:dim] + (2, count // 2, D))
                state = halve(
                    state,
                    dim,
                    (group >> place) & 1,
                    lambda v, place=place: swap_with(v, "b", self.groups, 1 << place),
                )
            return state

        for number in range(bits):
            if number == first_batch:
                state = batch_stages(state)
            state = halve(
                state,
                bits - 1 - number,
                (chip >> number) & 1,
                lambda v, number=number: self.swap_chip(v, 1 << number),
            )
        if first_batch >= bits:
            state = batch_stages(state)
        for place in reversed(range(bit_count(self.groups))):
            other = swap_with(state, "b", self.groups, 1 << place)
            bit = (group >> place) & 1
            state = jnp.where(
                bit == 0,
                jnp.concatenate([state, other], axis=0),
                jnp.concatenate([other, state], axis=0),
            )
        return state

    def sum_batch(self, value):
        for place in range(bit_count(self.groups)):
            value = value + swap_with(value, "b", self.groups, 1 << place)
        return value


def column_blocks(mat):
    return [mat[:, i * D : (i + 1) * D] for i in range(mat.shape[1] // D)]


def owner_blocks(mat, owners):
    return [b.reshape(owners, -1, D) for b in column_blocks(mat)]


class Packed:
    def __init__(self, gathered):
        self.gathered = gathered
        self.at = 0

    def take(self, rows):
        block = self.gathered[:, self.at : self.at + rows, :]
        self.at += rows
        return block.reshape(-1, D)

    def columns(self, rows, count):
        return jnp.concatenate([self.take(rows) for _ in range(count)], axis=1)


class Unpacked:
    def __init__(self, owned):
        self.owned = owned
        self.at = 0

    def take(self, rows):
        block = self.owned[self.at : self.at + rows]
        self.at += rows
        return block

    def columns(self, rows, count):
        return jnp.concatenate([self.take(rows) for _ in range(count)], axis=1)


def update(grad, weight, velocity, average, rate):
    momentum = momentum_decay * velocity + grad
    updated = weight - rate * (grad + momentum_decay * momentum)
    smooth = average_decay * average + (1.0 - average_decay) * updated
    return (momentum, smooth, updated)


def from_heads(got, half_rows, parts):
    value = got.reshape(HEADS, half_rows, 2, parts, HEAD_DIM)
    return jnp.transpose(value, (2, 1, 3, 0, 4)).reshape(2 * half_rows, parts * D)


def to_heads(value, half_rows, parts):
    value = value.reshape(2, half_rows, parts, HEADS, HEAD_DIM)
    return jnp.transpose(value, (3, 1, 0, 2, 4)).reshape(
        HEADS, half_rows, 2 * parts * HEAD_DIM
    )


def finish_block(stream, attended, proj, up, down, gain, shift):
    mixed = stream + matmul(attended, proj)
    normed = layer_norm(mixed, gain, shift)
    return mixed + matmul(jax.nn.gelu(matmul(normed, up), approximate=True), down)


def norm_rows(vectors, owners):
    each = D // owners
    block = jnp.stack(vectors).reshape(len(vectors), owners, each)
    block = jnp.transpose(block, (1, 0, 2))
    return jnp.pad(block, ((0, 0), (0, 16 - len(vectors)), (0, D - each)))


def shards(layout, rate, args):
    inputs, lengths, cotangent = args[:3]
    weights, velocities, averages = args[3:9], args[9:15], args[15:21]
    qkv_w, proj_w, up_w, down_w, pool_w, norm_w = weights
    half = inputs.shape[1]
    short_half = half // 3
    each = qkv_w.shape[1]
    ff_each = down_w.shape[1]
    up_blocks = up_w.shape[2] // D
    owners = layout.devices
    chip = layout.chip()
    core = lax.axis_index("s")
    owner = chip * layout.cores + core
    length = lax.dynamic_slice_in_dim(lengths, core, 1, 0)
    chip_arg = chip.reshape(1).astype(jnp.int32)
    seq = layout.chips * 2 * half
    short_seq = seq // 3

    norm_local = jnp.transpose(norm_w, (0, 2, 1)).reshape(8, each)
    norm_lanes = lax.dynamic_update_slice(
        jnp.zeros((8, D), F32), norm_local, (0, owner * each)
    )
    carried = jnp.concatenate([inputs, jnp.broadcast_to(norm_lanes, (2, 8, D))], axis=1)
    carried = lax.all_to_all(carried, "s", 0, 0, tiled=True)
    stream = carried[:, :half].reshape(2 * half, D)
    top = layout.chips // 2
    bits = bit_count(layout.chips)
    masks_a = tuple(1 << i for i in reversed(range(bits)))
    masks_b = (1,) + tuple(1 << i for i in reversed(range(1, bits)))
    slots = (layout.slot_of(masks_a), layout.slot_of(masks_b))
    xa = layout.gather_chips(carried[0], masks_a)
    xb = layout.gather_chips(carried[1], masks_b)

    head_cols = jnp.transpose(qkv_w[0].reshape(each, 3, HEADS, HEAD_DIM), (2, 0, 1, 3))
    head_cols = head_cols.reshape(HEADS, each, 3 * HEAD_DIM)
    head_cols = jnp.repeat(head_cols, layout.ranks * layout.cores, axis=0)
    head_w = lax.all_to_all(head_cols, layout.chip_axes + ("s",), 0, 0, tiled=True)
    head_w = head_w.reshape(D, 3 * HEAD_DIM)

    down_local = down_w
    first_pack = jnp.concatenate(
        [proj_w[0]]
        + column_blocks(up_w[0])
        + [down_local[0]]
        + column_blocks(pool_w[0])
        + column_blocks(qkv_w[1])
        + [proj_w[1]]
        + column_blocks(qkv_w[0]),
        axis=0,
    )
    second_pack = jnp.concatenate(
        column_blocks(up_w[1]) + [down_local[1]] + column_blocks(pool_w[1]), axis=0
    )
    wide_axes = layout.chip_axes + ("s",)
    first = Packed(lax.all_gather(first_pack, wide_axes, axis=0, tiled=False))
    second = Packed(lax.all_gather(second_pack, wide_axes, axis=0, tiled=False))
    proj0 = first.take(each)
    up0 = first.columns(each, up_blocks)
    down0 = first.take(ff_each)
    pool0 = jnp.concatenate([first.take(each) for _ in range(3)], axis=0)
    qkv1 = first.columns(each, 3)
    proj1 = first.take(each)
    qkv0 = first.columns(each, 3)
    up1 = second.columns(each, up_blocks)
    down1 = second.take(ff_each)
    pool1 = second.columns(each, 3)

    cos, sin, cos_t, sin_t = rope_tables(seq)
    tables = (cos, sin)
    tables_t = (cos_t, sin_t)
    short_tables = (cos[:short_seq], sin[:short_seq])
    short_tables_t = (cos_t[:, :short_seq], sin_t[:, :short_seq])
    step = query_step(seq)
    short_step = query_step(short_seq)

    outs = call(
        functools.partial(first_attend_kernel, half, step, slots),
        attend_outs(seq, half) + [jax.ShapeDtypeStruct((8, D), F32)],
        [pltpu.VMEM((seq, 3 * HEAD_DIM), F32)],
        2,
        seq * seq * HEAD_DIM * 12 + seq * D * 192 * 6,
        length,
        chip_arg,
        xa,
        xb,
        head_w,
        *tables,
    )
    packed, saved0, norm = outs[0], outs[1:6], outs[6]
    attended0 = from_heads(layout.heads_to_rows(packed), half, 1)
    full, finish0 = jax.vjp(
        finish_block, stream, attended0, proj0, up0, down0, norm[2], norm[3]
    )

    tails = layout.shift_chip(full[-2:], 1)
    shifted = jnp.concatenate([tails, full[:-2]], axis=0).reshape(2 * short_half, 3 * D)
    shortened = matmul(shifted, pool0)
    short_rows = 2 * short_half

    def project(rows, mat, gain, shift):
        return matmul(layer_norm(rows, gain, shift), mat)

    packed_qkv, project1 = jax.vjp(project, shortened, qkv1, norm[4], norm[5])
    got = layout.rows_to_heads(to_heads(packed_qkv, short_half, 3))
    short_length = length // 3
    outs = call(
        functools.partial(second_attend_kernel, short_half, short_step),
        attend_outs(short_seq, short_half),
        [pltpu.VMEM((short_seq, 3 * HEAD_DIM), F32)],
        1,
        short_seq * short_seq * HEAD_DIM * 12,
        short_length,
        got,
        *short_tables,
    )
    packed, saved1 = outs[0], outs[1:6]
    attended1 = from_heads(layout.heads_to_rows(packed), short_half, 1)
    short_out, finish1 = jax.vjp(
        finish_block, shortened, attended1, proj1, up1, down1, norm[6], norm[7]
    )
    activations = full + matmul(short_out, pool1).reshape(2 * half, D)

    positions = chip * 2 * half + jnp.arange(2 * half, dtype=jnp.int32)
    turned = lax.all_to_all(cotangent, "s", 0, 0, tiled=True).reshape(2 * half, D)
    grad_out = turned * (positions < length[0]).astype(F32)[:, None]
    grad_groups = grad_out.reshape(short_rows, 3 * D)
    grad_short = lax.dot_general(grad_groups, pool1, (((1,), (1,)), ((), ())), precision=HIGH)
    grad_pool1 = lax.dot_general(short_out, grad_groups, (((0,), (0,)), ((), ())), precision=HIGH)

    grad_shortened, grad_att1, grad_proj1, grad_up1, grad_down1, g6, g7 = finish1(grad_short)
    own_a = layout.reduce_owned(
        jnp.concatenate(
            owner_blocks(grad_up1, owners) + [grad_down1.reshape(owners, ff_each, D)], axis=1
        ),
        0,
    )
    own_b = None
    got = layout.rows_to_heads(to_heads(grad_att1, short_half, 1))
    scratch = lambda rows: [
        pltpu.VMEM((rows, HEAD_DIM), F32),
        pltpu.VMEM((rows, 2 * HEAD_DIM), F32),
        pltpu.VMEM((rows, 2 * HEAD_DIM), F32),
        pltpu.VMEM((HEAD_DIM, rows), F32),
        pltpu.VMEM((rows, 3 * HEAD_DIM), F32),
    ]
    dqkv_shape = lambda hr: jax.ShapeDtypeStruct((layout.chips, hr, 6 * HEAD_DIM), F32)
    (packed,) = call(
        functools.partial(second_grad_kernel, short_half, short_step),
        [dqkv_shape(short_half)],
        scratch(short_seq),
        1,
        short_seq * short_seq * HEAD_DIM * 30,
        short_length,
        saved1[2],
        saved1[3],
        saved1[4],
        saved1[0],
        saved1[1],
        got,
        *short_tables,
        *short_tables_t,
    )
    grad_packed1 = from_heads(layout.heads_to_rows(packed), short_half, 3)
    grad_inner, grad_qkv1, g4, g5 = project1(grad_packed1)
    grad_shortened = grad_shortened + grad_inner
    grad_shifted = lax.dot_general(
        grad_shortened, pool0, (((1,), (1,)), ((), ())), precision=HIGH
    ).reshape(2 * half, D)
    grad_pool0 = lax.dot_general(shifted, grad_shortened, (((0,), (0,)), ((), ())), precision=HIGH)
    pool0_blocks = [b.reshape(owners, each, D) for b in jnp.split(grad_pool0, 3, axis=0)]
    own_b = layout.reduce_owned(
        jnp.concatenate(
            pool0_blocks
            + owner_blocks(grad_pool1, owners)
            + owner_blocks(grad_qkv1, owners)
            + owner_blocks(grad_proj1, owners)
            + [norm_rows([g4, g5, g6, g7], owners)],
            axis=1,
        ),
        1,
    )
    heads_back = layout.shift_chip(grad_shifted[:2], -1)
    grad_full = grad_out + jnp.concatenate([grad_shifted[2:], heads_back], axis=0)

    grad_stream, grad_att0, grad_proj0, grad_up0, grad_down0, g2, g3 = finish0(grad_full)
    got = layout.rows_to_heads(to_heads(grad_att0, half, 1))
    own_c = layout.reduce_owned(
        jnp.concatenate(
            owner_blocks(grad_up0, owners) + [norm_rows([g2, g3], owners)], axis=1
        ),
        0,
    )
    own_d = layout.reduce_owned(
        jnp.concatenate(
            [grad_down0.reshape(owners, ff_each, D)] + owner_blocks(grad_proj0, owners), axis=1
        ),
        1,
    )
    packed, product = call(
        functools.partial(first_grad_kernel, half, step, slots),
        [
            dqkv_shape(half),
            jax.ShapeDtypeStruct((owners, each + 8, 3 * HEAD_DIM), F32),
        ],
        scratch(seq) + [pltpu.VMEM((seq, D), BF16), pltpu.VMEM((seq, D), BF16)],
        2,
        seq * seq * HEAD_DIM * 30 + seq * D * 192 * 6,
        length,
        chip_arg,
        xa,
        xb,
        saved0[2],
        saved0[3],
        saved0[4],
        saved0[0],
        saved0[1],
        got,
        *tables,
        *tables_t,
    )
    grad_packed0 = from_heads(layout.heads_to_rows(packed), half, 3)
    grad_normed = lax.dot_general(grad_packed0, qkv0, (((1,), (1,)), ((), ())), precision=HIGH)
    unused, norm_pull = jax.vjp(lambda rows: layer_norm(rows, norm[0], norm[1]), stream)
    input_grad = grad_stream + norm_pull(grad_normed)[0]
    input_grad = lax.all_to_all(input_grad.reshape(2, half, D), "s", 0, 0, tiled=True)
    activations = lax.all_to_all(activations.reshape(2, half, D), "s", 0, 0, tiled=True)

    product = product.reshape(HEADS, layout.ranks, layout.cores, each + 8, 3 * HEAD_DIM)
    product = lax.dynamic_index_in_dim(product, lax.axis_index("r"), 1, keepdims=False)
    keep = lax.dynamic_index_in_dim(product, core, 1, keepdims=False)
    away = lax.dynamic_index_in_dim(product, 1 - core, 1, keepdims=False)
    product = layout.sum_batch(keep + swap_with(away, "s", 2, 1))
    product = lax.all_to_all(product, "h", 0, 0, tiled=True)
    product = jnp.transpose(
        product.reshape(HEADS, each + 8, 3, HEAD_DIM), (1, 2, 0, 3)
    ).reshape(each + 8, 3 * D)
    columns = product[each : each + 1]
    product = product[:each]
    gain, shift = norm_w[0][:, 0:1], norm_w[0][:, 1:2]
    grad_qkv0 = product * gain + shift * columns
    own0 = jnp.sum(qkv_w[0] * product, axis=1)
    own1 = jnp.sum(qkv_w[0] * columns, axis=1)

    a, b, c, d = Unpacked(own_a), Unpacked(own_b), Unpacked(own_c), Unpacked(own_d)
    up_g1 = a.columns(each, up_blocks)
    down_g1 = a.take(ff_each)
    pool_g0 = b.columns(each, 3)
    pool_g1 = b.columns(each, 3)
    qkv_g1 = b.columns(each, 3)
    proj_g1 = b.take(each)
    norm_g1 = b.take(16)
    up_g0 = c.columns(each, up_blocks)
    norm_g0 = c.take(16)
    down_g0 = d.take(ff_each)
    proj_g0 = d.take(each)
    norm_first = jnp.stack([own0, own1, norm_g0[0, :each], norm_g0[1, :each]], axis=1)
    norm_second = jnp.transpose(norm_g1[:4, :each])
    grads = [
        jnp.stack([grad_qkv0, qkv_g1]),
        jnp.stack([proj_g0, proj_g1]),
        jnp.stack([up_g0, up_g1]),
        jnp.stack([down_g0, down_g1]),
        jnp.stack([pool_g0, pool_g1]),
        jnp.stack([norm_first, norm_second]),
    ]
    results = [
        update(grads[i], weights[i], velocities[i], averages[i], rate) for i in range(6)
    ]
    return (
        (activations, input_grad)
        + tuple(grads)
        + tuple(r[0] for r in results)
        + tuple(r[1] for r in results)
        + tuple(r[2] for r in results)
    )


def solution(mesh):
    groups, wide = mesh.shape["batch"], mesh.shape["wide"]

    def program(*args):
        cores = args[0].shape[0] // groups
        ranks = wide // (HEADS * cores)
        layout = Layout(groups, ranks, cores)
        rate = 0.5 / math.sqrt(math.prod(args[0].shape))
        fine = Mesh(mesh.devices.reshape(groups, HEADS, ranks, cores), ("b", "h", "r", "s"))
        rows = ("h", "r", "s")
        stream = P("b", rows, None)
        weight = P(None, rows, None)
        return jax.shard_map(
            lambda *local: shards(layout, rate, local),
            mesh=fine,
            in_specs=(stream, P("b"), stream) + (weight,) * 18,
            out_specs=(stream, stream) + (weight,) * 24,
            check_vma=False,
        )(*args)

    return program
```

```python
import functools
import math

import jax
import jax.numpy as jnp
import numpy as np
from jax import lax
from jax.experimental import pallas as pl
from jax.experimental.pallas import tpu as pltpu
from jax.sharding import Mesh, PartitionSpec as P

HEADS = 8
HEAD_DIM = 64
D = HEADS * HEAD_DIM
norm_eps = 1e-05
masked_score = -1e30
momentum_decay = 0.9
average_decay = 0.9
F32 = jnp.float32
BF16 = jnp.bfloat16
VMEM_LIMIT = 56 << 20
ROOT = math.sqrt(2.0 / math.pi)
CUBE = 0.044715
CHIP, CORE, SIDE, COLUMN, LENGTH, SHORT_LENGTH = range(6)


def split(value):
    high = value.astype(BF16)
    return high, (value - high.astype(F32)).astype(BF16)


def dot(a, b, dims):
    return lax.dot_general(a, b, (dims, ((), ())), preferred_element_type=F32)


NN = ((1,), (0,))
NT = ((1,), (1,))
TN = ((0,), (0,))


def matmul(left, right, dims=NN):
    rows = left.shape[0]
    high, low = split(left)
    right_high, right_low = split(right)
    both = dot(jnp.concatenate([high, low], axis=0), right_high, dims)
    return both[:rows] + both[rows:] + dot(high, right_low, dims)


def outer(left, right):
    columns = right.shape[1]
    high, low = split(left)
    right_high, right_low = split(right)
    both = dot(high, jnp.concatenate([right_high, right_low], axis=1), TN)
    return both[:, :columns] + both[:, columns:] + dot(low, right_high, TN)


def normalized(values):
    centred = values - jnp.mean(values, axis=-1, keepdims=True)
    variance = jnp.mean(centred * centred, axis=-1, keepdims=True)
    scale = lax.rsqrt(variance + norm_eps)
    return centred * scale, scale


def normalized_grad(grad, gain, normed, scale):
    inner = grad * gain
    along = jnp.mean(inner * normed, axis=-1, keepdims=True)
    return scale * (inner - jnp.mean(inner, axis=-1, keepdims=True) - normed * along)


def gelu_parts(u):
    curve = jnp.tanh(ROOT * (u + CUBE * u * u * u))
    return curve, 0.5 * u * (1.0 + curve)


def gelu_slope(u, curve):
    inner = ROOT * (1.0 + 3.0 * CUBE * u * u)
    return 0.5 * (1.0 + curve) + 0.5 * u * (1.0 - curve * curve) * inner


def rope_tables(rows):
    half = HEAD_DIM // 2
    freq = (10000.0 ** (-2.0 * np.arange(half, dtype=np.float32) / HEAD_DIM)).astype(np.float32)
    angles = np.arange(rows, dtype=np.float32)[:, None] * freq[None, :]
    cosine = np.cos(angles).astype(np.float32)
    sine = np.sin(angles).astype(np.float32)
    both = np.concatenate([cosine, cosine], axis=1)
    signed = np.concatenate([-sine, sine], axis=1)
    return (
        np.concatenate([both, both], axis=1),
        np.concatenate([signed, signed], axis=1),
        np.ascontiguousarray(cosine.T),
        np.ascontiguousarray(sine.T),
    )


def swap_halves(pair):
    half = HEAD_DIM // 2
    width = pair.shape[1]
    lane = lax.broadcasted_iota(jnp.int32, pair.shape, 1) % HEAD_DIM
    ahead = pltpu.roll(pair, width - half, 1)
    behind = pltpu.roll(pair, half, 1)
    return jnp.where(lane < half, ahead, behind)


def rows_from_heads(ref, parts):
    pair = 2 * HEAD_DIM
    top, bottom = [], []
    for part in range(parts):
        lanes = slice(part * pair, (part + 1) * pair)
        for k in range(HEADS // 2):
            even, odd = ref[2 * k, :, lanes], ref[2 * k + 1, :, lanes]
            first = lax.broadcasted_iota(jnp.int32, even.shape, 1) < HEAD_DIM
            top.append(jnp.where(first, even, pltpu.roll(odd, HEAD_DIM, 1)))
            bottom.append(jnp.where(first, pltpu.roll(even, HEAD_DIM, 1), odd))
    return jnp.concatenate(
        [jnp.concatenate(top, axis=1), jnp.concatenate(bottom, axis=1)], axis=0
    )


def rows_to_heads(rows, ref, parts):
    pair = 2 * HEAD_DIM
    half = rows.shape[0] // 2
    for part in range(parts):
        lanes = slice(part * pair, (part + 1) * pair)
        for k in range(HEADS // 2):
            at = part * D + k * pair
            top, bottom = rows[:half, at : at + pair], rows[half:, at : at + pair]
            first = lax.broadcasted_iota(jnp.int32, top.shape, 1) < HEAD_DIM
            ref[2 * k, :, lanes] = jnp.where(first, top, pltpu.roll(bottom, HEAD_DIM, 1))
            ref[2 * k + 1, :, lanes] = jnp.where(first, pltpu.roll(top, HEAD_DIM, 1), bottom)


def allowed_keys(first_row, rows, keys, length):
    key_pos = lax.broadcasted_iota(jnp.int32, (keys, rows), 0)
    query_pos = lax.broadcasted_iota(jnp.int32, (keys, rows), 1) + first_row
    return (key_pos <= query_pos) & (key_pos < length)


def attend_rows(raw, length, cos_ref, sin_ref, out_refs, rows, step, half_rows):
    packed_ref, turned_ref, lse_ref, qcat_ref, kcat_ref, vcat_ref = out_refs
    scale = HEAD_DIM ** (-0.5)
    for start in range(0, rows, step):
        part = slice(start, start + step)
        pair = raw[part, : 2 * HEAD_DIM]
        pair = pair * cos_ref[part, :] + swap_halves(pair) * sin_ref[part, :]
        lane = lax.broadcasted_iota(jnp.int32, pair.shape, 1)
        pair = jnp.where(lane < HEAD_DIM, pair * scale, pair)
        high, low = split(pair)
        qh, kh = high[:, :HEAD_DIM], high[:, HEAD_DIM:]
        ql, kl = low[:, :HEAD_DIM], low[:, HEAD_DIM:]
        vh, vl = split(raw[part, 2 * HEAD_DIM :])
        qcat_ref[part, :] = jnp.concatenate([qh, ql, qh], axis=1)
        kcat_ref[part, :] = jnp.concatenate([kh, kh, kl], axis=1)
        vcat_ref[part, :] = jnp.concatenate([vh, vh, vl], axis=1)
    value_pair = jnp.transpose(vcat_ref[:, HEAD_DIM:].astype(F32)).astype(BF16)
    value_high = value_pair[:HEAD_DIM]
    for start in range(0, rows, step):
        part = slice(start, start + step)
        keys = start + step
        scores = dot(kcat_ref[:keys, :], qcat_ref[part, :], NT)
        scores = jnp.where(allowed_keys(start, step, keys, length), scores, masked_score)
        row_max = jnp.max(scores, axis=0, keepdims=True)
        weights = jnp.exp(scores - row_max)
        total = jnp.sum(weights, axis=0, keepdims=True)
        wh, wl = split(weights)
        summed = dot(value_pair[:, :keys], wh, NN)
        summed = summed[:HEAD_DIM] + summed[HEAD_DIM:] + dot(value_high[:, :keys], wl, NN)
        turned = summed / total
        lse_ref[:, part] = jnp.broadcast_to(row_max + jnp.log(total), (8, step))
        turned_ref[:, part] = turned
    attended = jnp.transpose(
        jnp.concatenate([turned_ref[...], turned_ref[...]], axis=0)
    ).reshape(rows // (2 * half_rows), 2, half_rows, 2 * HEAD_DIM)
    lane = lax.broadcasted_iota(jnp.int32, attended[:, 0].shape, 2)
    packed_ref[...] = jnp.where(lane < HEAD_DIM, attended[:, 0], attended[:, 1])


def gathered_blocks(ids_ref, refs, distances, half_rows):
    for number, ref in enumerate(refs):
        side, part = divmod(number, 2)
        count = ref.shape[0]
        for slot in range(count):
            chip = ids_ref[CHIP] ^ distances[side][part * count + slot]
            first = pl.multiple_of((chip * 2 + side) * half_rows, 8)
            yield ref, slot, first


def first_attend_kernel(half_rows, step, distances, ids_ref, *refs):
    x_refs, (w_ref, cos_ref, sin_ref) = refs[:4], refs[4:7]
    out_refs, norm_ref, raw = refs[7:13], refs[13], refs[14]
    rows = raw.shape[0]
    total = sum(jnp.sum(ref[:, half_rows:, :], axis=0) for ref in x_refs)
    norm_ref[...] = total
    gain, shift = total[0:1], total[1:2]
    wh, wl = split(w_ref[...])
    for ref, slot, first in gathered_blocks(ids_ref, x_refs, distances, half_rows):
        hh, hl = split(normalized(ref[slot, :half_rows, :])[0] * gain + shift)
        raw[pl.ds(first, half_rows), :] = dot(hh, wh, NN) + dot(hh, wl, NN) + dot(hl, wh, NN)
    attend_rows(raw, ids_ref[LENGTH], cos_ref, sin_ref, out_refs, rows, step, half_rows)


def unpack_rows(packed_ref, raw, half_rows, parts):
    chips = packed_ref.shape[0]
    for chip in range(chips):
        for side in range(2):
            first = (chip * 2 + side) * half_rows
            pieces = [
                packed_ref[chip, :, (2 * part + side) * HEAD_DIM : (2 * part + side + 1) * HEAD_DIM]
                for part in range(parts)
            ]
            piece = pieces[0] if parts == 1 else jnp.concatenate(pieces, axis=1)
            raw[first : first + half_rows, :] = piece


def second_attend_kernel(half_rows, step, ids_ref, packed_ref, cos_ref, sin_ref, *refs):
    out_refs, raw = refs[:6], refs[6]
    rows = packed_ref.shape[0] * 2 * half_rows
    unpack_rows(packed_ref, raw, half_rows, 3)
    attend_rows(raw, ids_ref[SHORT_LENGTH], cos_ref, sin_ref, out_refs, rows, step, half_rows)


def attend_grad(
    rows, step, half_rows, length, refs, grad_ref, tables, out_ref, scratch
):
    qcat_ref, kcat_ref, vcat_ref, turned_ref, lse_ref = refs
    cos_ref, sin_ref, cos_t_ref, sin_t_ref = tables
    grad_rows, dk_acc, dv_acc, dq_t, dqkv = scratch
    scale = HEAD_DIM ** (-0.5)
    unpack_rows(grad_ref, grad_rows, half_rows, 1)
    key_pair = jnp.transpose(kcat_ref[:, HEAD_DIM:].astype(F32)).astype(BF16)
    key_high = key_pair[:HEAD_DIM]
    dk_acc[...] = jnp.zeros_like(dk_acc)
    dv_acc[...] = jnp.zeros_like(dv_acc)
    for start in range(0, rows, step):
        part = slice(start, start + step)
        keys = start + step
        grad = grad_rows[part, :]
        gh, gl = split(grad)
        gcat = jnp.concatenate([gh, gl, gh], axis=1)
        grad_t = jnp.transpose(jnp.concatenate([grad, grad], axis=1))[:HEAD_DIM]
        delta = jnp.sum(grad_t * turned_ref[:, part], axis=0, keepdims=True)
        scores = dot(kcat_ref[:keys, :], qcat_ref[part, :], NT)
        probs = jnp.where(
            allowed_keys(start, step, keys, length), jnp.exp(scores - lse_ref[0:1, part]), 0.0
        )
        grad_probs = dot(vcat_ref[:keys, :], gcat, NT)
        grad_scores = probs * (grad_probs - delta)
        ph, pw = split(probs)
        sh, sl = split(grad_scores)
        dv_acc[:keys, :] += dot(ph, gcat[:, : 2 * HEAD_DIM], NN)
        dv_acc[:keys, :HEAD_DIM] += dot(pw, gh, NN)
        dk_acc[:keys, :] += dot(sh, qcat_ref[part, : 2 * HEAD_DIM], NN)
        dk_acc[:keys, :HEAD_DIM] += dot(sl, qcat_ref[part, :HEAD_DIM], NN)
        turned = dot(key_pair[:, :keys], sh, NN)
        turned = turned[:HEAD_DIM] + turned[HEAD_DIM:] + dot(key_high[:, :keys], sl, NN)
        dq_t[:, part] = turned * scale
    half = HEAD_DIM // 2
    low, high = dq_t[:half, :], dq_t[half:, :]
    back_low = low * cos_t_ref[...] + high * sin_t_ref[...]
    back_high = high * cos_t_ref[...] - low * sin_t_ref[...]
    dq = jnp.transpose(jnp.concatenate([back_low, back_high, back_low, back_high], axis=0))
    for start in range(0, rows, step):
        part = slice(start, start + step)
        dk = dk_acc[part, :HEAD_DIM] + dk_acc[part, HEAD_DIM:]
        dk = jnp.concatenate([dk, dk], axis=1)
        dk = dk * cos_ref[part, :] - swap_halves(dk) * sin_ref[part, :]
        dv = dv_acc[part, :HEAD_DIM] + dv_acc[part, HEAD_DIM:]
        dqkv[part, :] = jnp.concatenate([dq[part, :HEAD_DIM], dk[:, :HEAD_DIM], dv], axis=1)
    chips = out_ref.shape[0]
    for chip in range(chips):
        first = chip * 2 * half_rows
        top = dqkv[first : first + half_rows, :]
        bottom = dqkv[first + half_rows : first + 2 * half_rows, :]
        pieces = []
        for part in range(3):
            lanes = slice(part * HEAD_DIM, (part + 1) * HEAD_DIM)
            pieces += [top[:, lanes], bottom[:, lanes]]
        out_ref[chip, :, :] = jnp.concatenate(pieces, axis=1)


def second_grad_kernel(half_rows, step, ids_ref, *refs):
    saved, grad_ref, tables, out_ref, scratch = refs[:5], refs[5], refs[6:10], refs[10], refs[11:]
    rows = saved[0].shape[0]
    length = ids_ref[SHORT_LENGTH]
    attend_grad(rows, step, half_rows, length, saved, grad_ref, tables, out_ref, scratch)


def first_grad_kernel(half_rows, step, distances, ids_ref, *refs):
    x_refs, saved, grad_ref, tables = refs[:4], refs[4:9], refs[9], refs[10:14]
    out_ref, m_ref, scratch = refs[14], refs[15], refs[16:]
    rows = saved[0].shape[0]
    length = ids_ref[LENGTH]
    attend_grad(rows, step, half_rows, length, saved, grad_ref, tables, out_ref, scratch[:5])
    dqkv, nh_ref, nl_ref = scratch[4:]
    for ref, slot, first in gathered_blocks(ids_ref, x_refs, distances, half_rows):
        nh, nl = split(normalized(ref[slot, :half_rows, :])[0])
        nh_ref[pl.ds(first, half_rows), :] = nh
        nl_ref[pl.ds(first, half_rows), :] = nl
    dh, dl = split(dqkv[...])
    nh = nh_ref[...]
    product = dot(nh, dh, TN) + dot(nh, dl, TN) + dot(nl_ref[...], dh, TN)
    owners, rows_each = m_ref.shape[0], m_ref.shape[1] - 8
    column = jnp.sum(dqkv[...], axis=0, keepdims=True)
    m_ref[:, :rows_each, :] = product.reshape(owners, rows_each, 3 * HEAD_DIM)
    m_ref[:, rows_each:, :] = jnp.broadcast_to(column[None], (owners, 8, 3 * HEAD_DIM))


class Loader:
    def __init__(self, ids_ref, sems):
        self.ids_ref = ids_ref
        self.sems = sems
        self.used = 0

    def start(self, src, dst):
        sem = self.sems.at[self.used]
        self.used += 1
        copy = pltpu.make_async_copy(src, dst, sem)
        copy.start()
        return copy

    def columns(self, gathered, unit, dst):
        return [[self.start(gathered.at[:, unit + k], dst.at[k])] for k in range(dst.shape[0])]

    def rows(self, gathered, unit, dst):
        run = dst.shape[0] // 4
        waits = []
        for k in range(4):
            owners = pl.ds(k * run, run)
            waits.append([self.start(gathered.at[owners, unit : unit + 4], dst.at[owners])])
        return waits


def ready(waits):
    for copy in waits:
        copy.wait()


def square(ref):
    return ref[...].reshape(D, D)


def pick(first, zero, one):
    return jnp.where(first, zero, one)


class Halves:
    def __init__(self, ids_ref, keep_ref, send_ref):
        self.zero = ids_ref[CORE] == 0
        self.keep_ref, self.send_ref = keep_ref, send_ref
        self.at = 0

    def put(self, keep, send):
        width = keep.shape[1]
        self.keep_ref[:, self.at : self.at + width] = keep
        self.send_ref[:, self.at : self.at + width] = send
        self.at += width

    def whole(self, value):
        self.put(value, value)

    def halved(self, zero, one):
        self.put(pick(self.zero, zero, one), pick(self.zero, one, zero))

    def granules(self, value, size, at):
        for k in range(value.shape[1] // (2 * size)):
            zero = value[:, 2 * k * size : (2 * k + 1) * size]
            one = value[:, (2 * k + 1) * size : (2 * k + 2) * size]
            lanes = slice(at + k * size, at + (k + 1) * size)
            self.keep_ref[:, lanes] = pick(self.zero, zero, one)
            self.send_ref[:, lanes] = pick(self.zero, one, zero)


def first_dense_kernel(
    ids_ref, stream_ref, got_ref, norm_ref, g_ref, full_ref, mixed_ref, u_ref, proj, up, down, sems
):
    load = Loader(ids_ref, sems)
    proj_wait = load.columns(g_ref, 0, proj)
    up_wait = load.columns(g_ref, 1, up)
    down_wait = load.rows(g_ref, 5, down)
    attended = rows_from_heads(got_ref, 1)
    ready(proj_wait[0])
    mixed = stream_ref[...] + matmul(attended, square(proj))
    mixed_ref[...] = mixed
    inner = normalized(mixed)[0] * norm_ref[2:3, :] + norm_ref[3:4, :]
    run = down.shape[0] // 4
    result = mixed
    for k in range(4):
        ready(up_wait[k])
        u = matmul(inner, up[k].reshape(D, D))
        u_ref[:, k * D : (k + 1) * D] = u
        hidden = gelu_parts(u)[1]
        ready(down_wait[k])
        result = result + matmul(hidden, down[k * run : (k + 1) * run].reshape(D, D))
    full_ref[...] = result


def shorten_kernel(
    ids_ref, full_ref, tail_ref, norm_ref, g_ref, short_ref, packed_ref, pool, qkv, moved, sems
):
    load = Loader(ids_ref, sems)
    pool_wait = load.columns(g_ref, 9, pool)
    qkv_wait = load.columns(g_ref, 12, qkv)
    shift_rows(full_ref, tail_ref, moved)
    rows = short_ref.shape[0]
    short = jnp.zeros((rows, D), F32)
    for i in range(3):
        ready(pool_wait[i])
        short = short + matmul(load_thirds(moved, 6 + i, rows), pool[i].reshape(D, D))
    short_ref[...] = short
    inner = normalized(short)[0] * norm_ref[4:5, :] + norm_ref[5:6, :]
    parts = []
    for i in range(3):
        ready(qkv_wait[i])
        parts.append(matmul(inner, qkv[i].reshape(D, D)))
    rows_to_heads(jnp.concatenate(parts, axis=1), packed_ref, 3)


LANES = 128
LANE_BLOCKS = D // LANES


def shift_rows(full_ref, tail_ref, moved):
    rows = full_ref.shape[0]
    for k in range(LANE_BLOCKS):
        lanes = slice(k * LANES, (k + 1) * LANES)
        moved[k, 6:8, :] = tail_ref[:, lanes]
        moved[k, 8 : 8 + rows, :] = full_ref[:, lanes]


def load_thirds(buffer, start, rows):
    pieces = [buffer[k, pl.ds(start, rows, stride=3), :] for k in range(LANE_BLOCKS)]
    return jnp.concatenate(pieces, axis=1)


def store_thirds(buffer, start, value):
    rows = value.shape[0]
    for k in range(LANE_BLOCKS):
        buffer[k, pl.ds(start, rows, stride=3), :] = value[:, k * LANES : (k + 1) * LANES]


def to_blocks(value, buffer):
    for k in range(LANE_BLOCKS):
        buffer[k] = value[:, k * LANES : (k + 1) * LANES]


def from_blocks(buffer):
    return jnp.concatenate([buffer[k] for k in range(LANE_BLOCKS)], axis=1)


def kept_cotangent(ids_ref, cot_ref):
    rows = cot_ref.shape[0]
    position = lax.broadcasted_iota(jnp.int32, cot_ref.shape, 0) + ids_ref[CHIP] * rows
    return jnp.where(position < ids_ref[LENGTH], cot_ref[...], 0.0)


def ffn_backward(grad, mixed, gain, u_of, curves, up_of, down_of, proj_of, halves, size):
    normed, scale = normalized(mixed)
    halves.whole(normed)
    base = halves.at
    halves.at += 4 * D
    halves.whole(grad)
    inner = jnp.zeros_like(mixed)
    each = D // 2
    for k in range(4):
        u = u_of(k)
        curve, hidden = curves(k, u)
        du = matmul(grad, down_of(k), NT) * gelu_slope(u, curve)
        halves.granules(du, size, base + k * each)
        halves.granules(hidden, size, base + 2 * D + k * each)
        inner = inner + matmul(du, up_of(k), NT)
    grad_mixed = grad + normalized_grad(inner, gain, normed, scale)
    return grad_mixed, matmul(grad_mixed, proj_of(), NT)


def middle_kernel(size, *refs):
    (ids_ref, short_ref, got_ref, norm_ref, full_ref, cot_ref, g_ref), refs = refs[:7], refs[7:]
    late_ref, refs = refs[0], refs[1:]
    (act_ref, grad_ref, mixed_ref, keep_ref, send_ref), refs = refs[:5], refs[5:]
    proj, up, down, pool, kept, act, sems = refs
    load = Loader(ids_ref, sems)
    proj_wait = load.columns(g_ref, 15, proj)
    up_wait = load.columns(late_ref, 0, up)
    down_wait = load.rows(late_ref, 4, down)
    pool_wait = load.columns(g_ref, 16, pool)
    to_blocks(kept_cotangent(ids_ref, cot_ref), kept)
    to_blocks(full_ref[...], act)
    attended = rows_from_heads(got_ref, 1)
    run = down.shape[0] // 4
    rows = short_ref.shape[0]
    up_of = lambda k: up[k].reshape(D, D)
    down_of = lambda k: down[k * run : (k + 1) * run].reshape(D, D)
    ready(proj_wait[0])
    mixed = short_ref[...] + matmul(attended, square(proj))
    gain = norm_ref[6:7, :]
    inner = normalized(mixed)[0] * gain + norm_ref[7:8, :]
    for wait in up_wait:
        ready(wait)
    us = [matmul(inner, up_of(k)) for k in range(4)]
    gelus = [gelu_parts(u) for u in us]
    for wait in down_wait:
        ready(wait)
    result = mixed
    for k in range(4):
        result = result + matmul(gelus[k][1], down_of(k))
    grad = jnp.zeros((rows, D), F32)
    groups = []
    for i in range(3):
        ready(pool_wait[i])
        tap = pool[i].reshape(D, D)
        store_thirds(act, i, load_thirds(act, i, rows) + matmul(result, tap))
        groups.append(load_thirds(kept, i, rows))
        grad = grad + matmul(groups[i], tap, NT)
    act_ref[...] = from_blocks(act)
    halves = Halves(ids_ref, keep_ref, send_ref)
    grad_mixed, grad_attended = ffn_backward(
        grad,
        mixed,
        gain,
        lambda k: us[k],
        lambda k, u: gelus[k],
        up_of,
        down_of,
        lambda: square(proj),
        halves,
        size,
    )
    rows_to_heads(grad_attended, grad_ref, 1)
    mixed_ref[...] = grad_mixed
    halves.whole(attended)
    halves.halved(grad_mixed[:, : D // 2], grad_mixed[:, D // 2 :])
    halves.whole(result)
    wide = jnp.concatenate(groups, axis=1)
    halves.halved(wide[:, : 3 * D // 2], wide[:, 3 * D // 2 :])


def lengthen_grad_kernel(
    ids_ref,
    got_ref,
    short_ref,
    mixed_ref,
    norm_ref,
    full_ref,
    tail_ref,
    g_ref,
    shifted_ref,
    keep_ref,
    send_ref,
    pool,
    qkv,
    moved,
    back,
    sems,
):
    load = Loader(ids_ref, sems)
    qkv_wait = load.columns(g_ref, 12, qkv)
    pool_wait = load.columns(g_ref, 9, pool)
    dqkv = rows_from_heads(got_ref, 3)
    rows = short_ref.shape[0]
    normed, scale = normalized(short_ref[...])
    inner = jnp.zeros((rows, D), F32)
    for i in range(3):
        ready(qkv_wait[i])
        inner = inner + matmul(dqkv[:, i * D : (i + 1) * D], qkv[i].reshape(D, D), NT)
    grad = mixed_ref[...] + normalized_grad(inner, norm_ref[4:5, :], normed, scale)
    for i in range(3):
        ready(pool_wait[i])
        store_thirds(back, i, matmul(grad, pool[i].reshape(D, D), NT))
    shifted_ref[...] = from_blocks(back)
    shift_rows(full_ref, tail_ref, moved)
    halves = Halves(ids_ref, keep_ref, send_ref)
    halves.whole(normed)
    halves.halved(dqkv[:, : 3 * D // 2], dqkv[:, 3 * D // 2 :])
    for i in range(3):
        halves.whole(load_thirds(moved, 6 + i, rows))
    halves.halved(grad[:, : D // 2], grad[:, D // 2 :])


def first_dense_grad_kernel(
    size,
    ids_ref,
    shifted_ref,
    next_ref,
    cot_ref,
    mixed_in_ref,
    u_ref,
    got_ref,
    norm_ref,
    g_ref,
    grad_ref,
    mixed_ref,
    keep_ref,
    send_ref,
    proj,
    up,
    down,
    moved,
    sems,
):
    load = Loader(ids_ref, sems)
    down_wait = load.rows(g_ref, 5, down)
    up_wait = load.columns(g_ref, 1, up)
    proj_wait = load.columns(g_ref, 0, proj)
    rows = cot_ref.shape[0]
    moved[:rows, :] = shifted_ref[...]
    moved[rows : rows + 2, :] = next_ref[...]
    grad = kept_cotangent(ids_ref, cot_ref) + moved[2 : 2 + rows, :]
    run = down.shape[0] // 4

    def up_of(k):
        ready(up_wait[k])
        return up[k].reshape(D, D)

    def down_of(k):
        ready(down_wait[k])
        return down[k * run : (k + 1) * run].reshape(D, D)

    def proj_of():
        ready(proj_wait[0])
        return square(proj)

    halves = Halves(ids_ref, keep_ref, send_ref)
    grad_mixed, grad_attended = ffn_backward(
        grad,
        mixed_in_ref[...],
        norm_ref[2:3, :],
        lambda k: u_ref[:, k * D : (k + 1) * D],
        lambda k, u: gelu_parts(u),
        up_of,
        down_of,
        proj_of,
        halves,
        size,
    )
    rows_to_heads(grad_attended, grad_ref, 1)
    mixed_ref[...] = grad_mixed
    halves.whole(rows_from_heads(got_ref, 1))
    halves.halved(grad_mixed[:, : D // 2], grad_mixed[:, D // 2 :])


def input_grad_kernel(
    ids_ref, got_ref, stream_ref, mixed_ref, norm_ref, g_ref, out_ref, qkv, sems
):
    load = Loader(ids_ref, sems)
    qkv_wait = load.columns(g_ref, 0, qkv)
    dqkv = rows_from_heads(got_ref, 3)
    normed, scale = normalized(stream_ref[...])
    inner = jnp.zeros_like(normed)
    for i in range(3):
        ready(qkv_wait[i])
        inner = inner + matmul(dqkv[:, i * D : (i + 1) * D], qkv[i].reshape(D, D), NT)
    out_ref[...] = mixed_ref[...] + normalized_grad(inner, norm_ref[0:1, :], normed, scale)


class Factors:
    def __init__(self, keep_ref, got_ref):
        self.keep_ref, self.got_ref = keep_ref, got_ref
        self.at = 0

    def take(self, width):
        lanes = slice(self.at, self.at + width)
        self.at += width
        return jnp.concatenate([self.keep_ref[:, lanes], self.got_ref[:, lanes]], axis=0)


def side_halves(ids_ref, value):
    width = value.shape[1] // 2
    zero = ids_ref[SIDE] == 0
    first, second = value[:, :width], value[:, width:]
    return pick(zero, first, second), pick(zero, second, first)


def place_by_column(ids_ref, ref, rows, block, ranks):
    for depth in range(4):
        for column in range(2):
            for rank in range(ranks):
                chip = (depth * 2 + column) * ranks + rank
                ref[column ^ ids_ref[COLUMN], depth * ranks + rank, rows, :] = block(chip)


def packed_rows(rows):
    count = rows.shape[0] // 4
    return jnp.concatenate([rows[i * count : (i + 1) * count] for i in range(4)], axis=1)


def place_blocks(ids_ref, ref, at, product, each, ranks):
    rows = slice(at, at + each)
    place_by_column(
        ids_ref, ref, rows, lambda chip: product[chip * each : (chip + 1) * each], ranks
    )
    return at + each


def place_sums(ids_ref, ref, at, value, ranks):
    total = jnp.broadcast_to(jnp.sum(value, axis=0, keepdims=True), (8, value.shape[1]))
    place_by_column(ids_ref, ref, slice(at, at + 8), lambda chip: total, ranks)
    return at + 8


def place_packed(ids_ref, ref, at, product, each, ranks):
    rows = slice(at, at + each // 4)
    place_by_column(
        ids_ref,
        ref,
        rows,
        lambda chip: packed_rows(product[chip * each : (chip + 1) * each]),
        ranks,
    )
    return at + each // 4


def place_by_side(ids_ref, refs, at, products, each, ranks):
    zero = ids_ref[COLUMN] == 0
    for depth in range(4):
        for rank in range(ranks):
            first = ((depth * 2) * ranks + rank) * each
            second = ((depth * 2 + 1) * ranks + rank) * each
            place = depth * ranks + rank
            for side in range(2):
                far = side ^ ids_ref[SIDE]
                one = products[side][first : first + each]
                two = products[side][second : second + each]
                refs[0][place, far, at : at + each, :] = pick(zero, one, two)
                refs[1][place, far, at : at + each, :] = pick(zero, two, one)
    return at + each


def middle_products_kernel(ranks, size, each, ids_ref, keep_ref, got_ref, *refs):
    up_refs, down_refs = refs[:2], refs[2:]
    factors = Factors(keep_ref, got_ref)
    normed, du, hidden, grad = (factors.take(w * D) for w in (1, 2, 2, 1))
    attended, grad_mixed = factors.take(D), factors.take(D // 2)
    for ref, half, narrow in zip(
        up_refs, side_halves(ids_ref, du), side_halves(ids_ref, grad_mixed)
    ):
        at = place_blocks(ids_ref, ref, 0, outer(normed, half), each, ranks)
        at = place_sums(ids_ref, ref, at, half, ranks)
        place_packed(ids_ref, ref, at, outer(attended, narrow), each, ranks)
    product = outer(hidden, grad).reshape(D // each, 2, size // 2, D)
    sides = [product[:, side].reshape(-1, D) for side in range(2)]
    place_by_side(ids_ref, down_refs, 0, sides, size // 2, ranks)


def first_products_kernel(ranks, size, each, ids_ref, keep_ref, got_ref, *refs):
    factors = Factors(keep_ref, got_ref)
    normed, du, hidden, grad = (factors.take(w * D) for w in (1, 2, 2, 1))
    attended, grad_mixed = factors.take(D), factors.take(D // 2)
    product = outer(hidden, grad).reshape(D // each, 2, size // 2, D)
    zero = ids_ref[SIDE] == 0
    downs = [
        pick(zero, product[:, far], product[:, 1 - far]).reshape(-1, D) for far in range(2)
    ]
    for ref, half, narrow, down in zip(
        refs, side_halves(ids_ref, du), side_halves(ids_ref, grad_mixed), downs
    ):
        at = place_blocks(ids_ref, ref, 0, outer(normed, half), each, ranks)
        at = place_sums(ids_ref, ref, at, half, ranks)
        at = place_blocks(ids_ref, ref, at, down, size // 2, ranks)
        place_packed(ids_ref, ref, at, outer(attended, narrow), each, ranks)


def shorten_products_kernel(
    ranks, each, ids_ref, keep_ref, got_ref, up_keep_ref, up_got_ref, *refs
):
    qkv_refs, pool_refs = refs[:2], refs[2:]
    factors = Factors(keep_ref, got_ref)
    normed, dqkv = factors.take(D), factors.take(3 * D // 2)
    shifted = [factors.take(D) for _ in range(3)]
    grad = factors.take(D // 2)
    for ref, half in zip(qkv_refs, side_halves(ids_ref, dqkv)):
        at = place_blocks(ids_ref, ref, 0, outer(normed, half), each, ranks)
        place_sums(ids_ref, ref, at, half, ranks)
    narrow, wide = D // 4, 3 * D // 4
    taps = [
        jnp.concatenate(
            [outer(rows, grad[:, side * narrow : (side + 1) * narrow]) for rows in shifted],
            axis=1,
        )
        for side in range(2)
    ]
    at = place_by_side(ids_ref, pool_refs, 0, taps, each, ranks)
    factors = Factors(up_keep_ref, up_got_ref)
    factors.at = 15 * D // 2
    short, groups = factors.take(D), factors.take(3 * D // 2)
    taps = [outer(short, groups[:, side * wide : (side + 1) * wide]) for side in range(2)]
    place_by_side(ids_ref, pool_refs, at, taps, each, ranks)


PER_US = 3.3e+09
SMEM = pl.BlockSpec(memory_space=pltpu.SMEM)
VMEM = pl.BlockSpec(memory_space=pltpu.VMEM)
ANY = pl.BlockSpec(memory_space=pl.ANY)


def attend_outs(rows, half_rows):
    width = 3 * HEAD_DIM
    return [
        shape(rows // (2 * half_rows), half_rows, 2 * HEAD_DIM),
        shape(HEAD_DIM, rows),
        shape(8, rows),
        jax.ShapeDtypeStruct((rows, width), BF16),
        jax.ShapeDtypeStruct((rows, width), BF16),
        jax.ShapeDtypeStruct((rows, width), BF16),
    ]


def shape(*dims):
    return jax.ShapeDtypeStruct(dims, F32)


def call(time, kernel, outs, scratch, ids, args, weights=(), copies=0):
    scratch = list(scratch)
    if copies:
        scratch.append(pltpu.SemaphoreType.DMA((copies,)))
    return pl.pallas_call(
        kernel,
        out_shape=list(outs),
        in_specs=[SMEM] + [VMEM] * len(args) + [ANY] * len(weights),
        out_specs=[VMEM] * len(outs),
        scratch_shapes=scratch,
        compiler_params=pltpu.CompilerParams(vmem_limit_bytes=VMEM_LIMIT),
        cost_estimate=pl.CostEstimate(
            flops=int(time * PER_US), bytes_accessed=0, transcendentals=0
        ),
    )(ids, *args, *weights)


def query_step(rows):
    return math.gcd(rows, 256)


def bit_count(size):
    return size.bit_length() - 1


def swap_with(value, axis, size, mask):
    return lax.ppermute(value, axis, [(i, i ^ mask) for i in range(size)])


def by_bit(bit, own, other):
    return jnp.where(bit == 0, jnp.stack([own, other]), jnp.stack([other, own]))


class Layout:
    def __init__(self, groups, ranks, cores):
        self.groups = groups
        self.ranks = ranks
        self.cores = cores
        self.chips = HEADS * ranks
        self.devices = self.chips * cores
        self.chip_axes = ("z", "x", "r") if ranks > 1 else ("z", "x")

    def chip(self):
        return lax.axis_index(("z", "x", "r"))

    def swap_chip(self, value, mask):
        return swap_with(value, self.chip_axes, self.chips, mask)

    def swap_core(self, value):
        return swap_with(value, "s", 2, 1)

    def shift_chip(self, value, distance):
        chips = range(self.chips)
        route = [(i - distance, i) for i in chips if i - distance in chips]
        return lax.ppermute(value, self.chip_axes, route)

    def gather_chips(self, value, masks):
        held = value[None]
        for mask in masks[:-1]:
            held = jnp.concatenate([held, self.swap_chip(held, mask)], axis=0)
        return [held, self.swap_chip(held, masks[-1])]

    def distances(self, masks):
        found = [0]
        for mask in masks:
            found = found + [d ^ mask for d in found]
        return found

    def heads_to_rows(self, value):
        value = value.reshape((HEADS, self.ranks) + value.shape[1:])
        mine = lax.dynamic_index_in_dim(value, lax.axis_index("r"), 1, keepdims=False)
        return lax.all_to_all(mine, ("z", "x"), 0, 0, tiled=True)

    def rows_to_heads(self, value):
        got = lax.all_to_all(value, ("z", "x"), 0, 0, tiled=True)
        if self.ranks > 1:
            got = lax.all_gather(got, "r", axis=1, tiled=False)
            got = got.reshape((self.chips,) + value.shape[1:])
        return got

    def join_sides(self, value):
        return by_bit(lax.axis_index("b") % 2, value, swap_with(value, "b", self.groups, 1))

    def join_cores(self, value, each):
        core = lax.axis_index("s")
        both = value[:, 2 * each :]

        def rows_of(owner):
            rows = lax.dynamic_slice_in_dim(value, owner * each, each, 1)
            return jnp.concatenate([rows, both], axis=1)

        return by_bit(core, rows_of(core), self.swap_core(rows_of(1 - core)))

    def sum_batch(self, value):
        for place in range(bit_count(self.groups)):
            value = value + swap_with(value, "b", self.groups, 1 << place)
        return value


class Reduction:
    def __init__(self, layout, batch_first, keep, send):
        self.layout = layout
        self.batch_first = batch_first
        self.keep, self.send = keep, send
        self.stage = 0

    def step(self):
        groups = self.layout.groups
        axis, size = ("b", groups) if self.batch_first == (self.stage == 0) else ("x", 2)
        if self.stage < 2:
            got = swap_with(self.send, axis, size, 1)
        if self.stage == 0 and self.batch_first:
            self.keep, self.send = self.keep[0] + got[0], self.keep[1] + got[1]
        elif self.stage == 0:
            self.keep, self.send = self.keep[:, 0] + got[:, 0], self.keep[:, 1] + got[:, 1]
        elif self.stage == 1:
            self.send = self.keep + got
            self.keep = self.send
        else:
            self.keep = self.over_depth()
        self.stage += 1

    def over_depth(self):
        ranks = self.layout.ranks
        got = lax.all_to_all(self.send, "z", 0, 0, tiled=True)
        own = lax.broadcasted_iota(jnp.int32, got.shape, 0) // ranks == lax.axis_index("z")
        value = jnp.where(own, self.keep, got)
        value = jnp.sum(value.reshape((4, ranks) + value.shape[1:]), axis=0)
        if ranks > 1:
            rank = lax.axis_index("r")
            keep = lax.dynamic_index_in_dim(value, rank, 0, keepdims=False)
            send = lax.dynamic_index_in_dim(value, 1 - rank, 0, keepdims=False)
            value = keep + swap_with(send, "r", 2, 1)
        else:
            value = value[0]
        for place in range(1, bit_count(self.layout.groups)):
            value = value + swap_with(value, "b", self.layout.groups, 1 << place)
        return value

    def finish(self):
        while self.stage < 3:
            self.step()
        return self.keep


def tied(value, *reductions):
    value, kept = lax.optimization_barrier((value, [r.keep for r in reductions]))
    for r, keep in zip(reductions, kept):
        r.keep = keep
    return value


def column_blocks(mat):
    return [mat[:, i * D : (i + 1) * D] for i in range(mat.shape[1] // D)]


def update(grad, weight, velocity, average, rate):
    momentum = momentum_decay * velocity + grad
    updated = weight - rate * (grad + momentum_decay * momentum)
    smooth = average_decay * average + (1.0 - average_decay) * updated
    return (momentum, smooth, updated)


def with_norm(product, columns, gain, shift, weight):
    grad = gain * product + shift * columns
    return grad, jnp.sum(weight * product, axis=1), jnp.sum(weight * columns, axis=1)


def shards(layout, rate, args):
    inputs, lengths, cotangent = args[:3]
    weights, velocities, averages = args[3:9], args[9:15], args[15:21]
    qkv_w, proj_w, up_w, down_w, pool_w, norm_w = weights
    half = inputs.shape[1]
    rows = 2 * half
    short_half, short_rows = half // 3, rows // 3
    each = qkv_w.shape[1]
    ff_each = down_w.shape[1]
    owners, chips, ranks = layout.devices, layout.chips, layout.ranks
    chip = layout.chip()
    core = lax.axis_index("s")
    side = lax.axis_index("b") % 2
    owner = chip * layout.cores + core
    length = lengths[core]
    ids = jnp.stack([chip, core, side, lax.axis_index("x"), length, length // 3]).astype(jnp.int32)
    seq = chips * rows
    short_seq = seq // 3
    bits = bit_count(chips)

    norm_local = jnp.transpose(norm_w, (0, 2, 1)).reshape(8, each)
    norm_lanes = lax.dynamic_update_slice(
        jnp.zeros((8, D), F32), norm_local, (0, owner * each)
    )
    carried = jnp.concatenate([inputs, jnp.broadcast_to(norm_lanes, (2, 8, D))], axis=1)
    carried = lax.all_to_all(carried, "s", 0, 0, tiled=True)
    stream = carried[:, :half].reshape(rows, D)
    masks_a = tuple(1 << i for i in reversed(range(bits)))
    masks_b = (1,) + tuple(1 << i for i in reversed(range(1, bits)))
    distances = (layout.distances(masks_a), layout.distances(masks_b))
    blocks = layout.gather_chips(carried[0], masks_a) + layout.gather_chips(carried[1], masks_b)

    head_cols = jnp.transpose(qkv_w[0].reshape(each, 3, HEADS, HEAD_DIM), (2, 0, 1, 3))
    head_cols = head_cols.reshape(HEADS, each, 3 * HEAD_DIM)
    head_cols = jnp.repeat(head_cols, ranks * layout.cores, axis=0)
    wide_axes = layout.chip_axes + ("s",)
    head_w = lax.all_to_all(head_cols, wide_axes, 0, 0, tiled=True)
    head_w = head_w.reshape(D, 3 * HEAD_DIM)

    units = lambda pieces: jnp.concatenate(pieces, axis=0).reshape(-1, each, D)
    packed = units(
        [proj_w[0]]
        + column_blocks(up_w[0])
        + [down_w[0]]
        + column_blocks(pool_w[0])
        + column_blocks(qkv_w[1])
        + [proj_w[1]]
        + column_blocks(pool_w[1])
    )
    gathered = lax.all_gather(packed, wide_axes, axis=0, tiled=False)
    second = units(column_blocks(up_w[1]) + [down_w[1]])
    second = lax.all_gather(second, wide_axes, axis=0, tiled=False)
    last = units(column_blocks(qkv_w[0]))
    last = lax.all_gather(last, wide_axes, axis=0, tiled=False)

    cos, sin, cos_t, sin_t = rope_tables(seq)
    tables = (cos, sin)
    tables_t = (cos_t, sin_t)
    short_tables = (cos[:short_seq], sin[:short_seq])
    short_tables_t = (cos_t[:, :short_seq], sin_t[:, :short_seq])
    step = query_step(seq)
    short_step = query_step(short_seq)
    vmem = lambda *dims: pltpu.VMEM(dims, F32)
    column_buffer = lambda count: vmem(count, owners, each, D)
    row_buffer = vmem(owners, 4, each, D)
    blocks_of = lambda count: vmem(LANE_BLOCKS, count, LANES)

    outs = call(
        10,
        functools.partial(first_attend_kernel, half, step, distances),
        attend_outs(seq, half) + [shape(8, D)],
        [vmem(seq, 3 * HEAD_DIM)],
        ids,
        [*blocks, head_w, *tables],
    )
    saved0, norm = (outs[3], outs[4], outs[5], outs[1], outs[2]), outs[6]
    got0 = layout.heads_to_rows(outs[0])
    full, mixed0, u0 = call(
        8,
        first_dense_kernel,
        [shape(rows, D), shape(rows, D), shape(rows, 4 * D)],
        [column_buffer(1), column_buffer(4), row_buffer],
        ids,
        [stream, got0, norm],
        [gathered],
        9,
    )

    tail = layout.shift_chip(full[-2:], 1)
    shortened, to_send = call(
        5,
        shorten_kernel,
        [shape(short_rows, D), shape(HEADS, short_half, 6 * HEAD_DIM)],
        [column_buffer(3), column_buffer(3), blocks_of(rows + 8)],
        ids,
        [full, tail, norm],
        [gathered],
        6,
    )
    outs = call(
        3,
        functools.partial(second_attend_kernel, short_half, short_step),
        attend_outs(short_seq, short_half),
        [vmem(short_seq, 3 * HEAD_DIM)],
        ids,
        [layout.rows_to_heads(to_send), *short_tables],
    )
    saved1 = (outs[3], outs[4], outs[5], outs[1], outs[2])
    got1 = layout.heads_to_rows(outs[0])
    cot = lax.all_to_all(cotangent, "s", 0, 0, tiled=True).reshape(rows, D)
    middle_wide = 10 * D
    activations, grad_att1, grad_mixed1, keep_a, send_a = call(
        13,
        functools.partial(middle_kernel, ff_each),
        [
            shape(rows, D),
            shape(HEADS, short_half, 2 * HEAD_DIM),
            shape(short_rows, D),
            shape(short_rows, middle_wide),
            shape(short_rows, middle_wide),
        ],
        [column_buffer(1), column_buffer(4), row_buffer, column_buffer(3)]
        + [blocks_of(rows), blocks_of(rows)],
        ids,
        [shortened, got1, norm, full, cot],
        [gathered, second],
        12,
    )

    depth = 4 * ranks
    pair = 2 * each
    up_rows = pair + 8
    up_out = shape(2, depth, up_rows + each // 2, D)
    down_out = shape(depth, 2, ff_each // 2, D)
    got_a = layout.swap_core(send_a)
    up_keep, up_send, down_keep, down_send = call(
        6,
        functools.partial(middle_products_kernel, ranks, ff_each, pair),
        [up_out, up_out, down_out, down_out],
        [],
        ids,
        [keep_a, got_a],
    )
    red_up1 = Reduction(layout, True, up_keep, up_send)
    red_down1 = Reduction(layout, False, down_keep, down_send)

    scratch = lambda count: [
        vmem(count, HEAD_DIM),
        vmem(count, 2 * HEAD_DIM),
        vmem(count, 2 * HEAD_DIM),
        vmem(HEAD_DIM, count),
        vmem(count, 3 * HEAD_DIM),
    ]
    got = layout.rows_to_heads(grad_att1)
    got = tied(got, red_up1, red_down1)
    (to_send,) = call(
        4,
        functools.partial(second_grad_kernel, short_half, short_step),
        [shape(chips, short_half, 6 * HEAD_DIM)],
        scratch(short_seq),
        ids,
        [*saved1, got, *short_tables, *short_tables_t],
    )
    got = layout.heads_to_rows(to_send)
    grad_shifted, keep_b, send_b = call(
        6.5,
        lengthen_grad_kernel,
        [shape(rows, D), shape(short_rows, 6 * D), shape(short_rows, 6 * D)],
        [column_buffer(3), column_buffer(3), blocks_of(rows + 8), blocks_of(rows)],
        ids,
        [got, shortened, grad_mixed1, norm, full, tail],
        [gathered],
        6,
    )
    head = layout.shift_chip(grad_shifted[:2], -1)
    qkv_out = shape(2, depth, up_rows, 3 * D // 4)
    pool_out = shape(depth, 2, 2 * pair, 3 * D // 4)
    qkv_keep, qkv_send, pool_keep, pool_send = call(
        7,
        functools.partial(shorten_products_kernel, ranks, pair),
        [qkv_out, qkv_out, pool_out, pool_out],
        [],
        ids,
        [keep_b, layout.swap_core(send_b), keep_a, got_a],
    )
    red_qkv1 = Reduction(layout, True, qkv_keep, qkv_send)
    red_pool = Reduction(layout, False, pool_keep, pool_send)
    red_up1.step()
    head = tied(head, red_qkv1, red_pool)
    first_wide = 15 * D // 2
    grad_att0, grad_mixed0, keep_c, send_c = call(
        12.5,
        functools.partial(first_dense_grad_kernel, ff_each),
        [
            shape(HEADS, half, 2 * HEAD_DIM),
            shape(rows, D),
            shape(rows, first_wide),
            shape(rows, first_wide),
        ],
        [column_buffer(1), column_buffer(4), row_buffer, vmem(rows + 8, D)],
        ids,
        [grad_shifted, head, cot, mixed0, u0, got0, norm],
        [gathered],
        9,
    )
    all_out = shape(2, depth, up_rows + ff_each // 2 + each // 2, D)
    all_keep, all_send = call(
        9,
        functools.partial(first_products_kernel, ranks, ff_each, pair),
        [all_out, all_out],
        [],
        ids,
        [keep_c, layout.swap_core(send_c)],
    )
    red_first = Reduction(layout, True, all_keep, all_send)
    got = layout.rows_to_heads(grad_att0)
    red_up1.step()
    red_down1.step()
    red_qkv1.step()
    got = tied(got, red_first)
    to_send, product = call(
        16,
        functools.partial(first_grad_kernel, half, step, distances),
        [shape(chips, half, 6 * HEAD_DIM), shape(owners, each + 8, 3 * HEAD_DIM)],
        scratch(seq) + [pltpu.VMEM((seq, D), BF16), pltpu.VMEM((seq, D), BF16)],
        ids,
        [*blocks, *saved0, got, *tables, *tables_t],
    )
    got = layout.heads_to_rows(to_send)
    red_up1.step()
    red_down1.step()
    red_qkv1.step()
    red_first.step()
    red_pool.step()
    (input_grad,) = call(
        5,
        input_grad_kernel,
        [shape(rows, D)],
        [column_buffer(3)],
        ids,
        [got, stream, grad_mixed0, norm],
        [last],
        3,
    )
    input_grad = lax.all_to_all(input_grad.reshape(2, half, D), "s", 0, 0, tiled=True)
    activations = lax.all_to_all(activations.reshape(2, half, D), "s", 0, 0, tiled=True)

    product = product.reshape(HEADS, ranks, layout.cores, each + 8, 3 * HEAD_DIM)
    product = lax.dynamic_index_in_dim(product, lax.axis_index("r"), 1, keepdims=False)
    keep = lax.dynamic_index_in_dim(product, core, 1, keepdims=False)
    away = lax.dynamic_index_in_dim(product, 1 - core, 1, keepdims=False)
    product = layout.sum_batch(keep + layout.swap_core(away))
    product = lax.all_to_all(product, ("z", "x"), 0, 0, tiled=True)
    product = jnp.transpose(
        product.reshape(HEADS, each + 8, 3, HEAD_DIM), (1, 2, 0, 3)
    ).reshape(each + 8, 3 * D)

    def up_columns(joined):
        value = joined.reshape(2, 2, each + 8, D // ff_each, ff_each)
        return jnp.transpose(value, (2, 1, 3, 0, 4)).reshape(each + 8, 4 * D)

    def plain_columns(joined):
        return jnp.transpose(joined, (2, 0, 1, 3)).reshape(joined.shape[2], -1)

    def packed_columns(value):
        value = value.reshape(2, each // 2, 4, D // 4)
        value = jnp.transpose(value, (0, 2, 1, 3)).reshape(2, pair, D // 4)
        return plain_columns(layout.join_cores(value, each))

    half_ff = ff_each // 2
    joined = layout.join_sides(
        jnp.concatenate([red_up1.finish(), red_down1.finish()], axis=0)
    )
    up_g1 = up_columns(layout.join_cores(joined[:, :up_rows], each))
    proj_g1 = packed_columns(joined[:, up_rows : up_rows + each // 2])
    down_g1 = joined[:, up_rows + each // 2 :].reshape(ff_each, D)
    joined = layout.join_sides(jnp.concatenate([red_qkv1.finish(), red_pool.finish()], axis=0))
    qkv_g1 = plain_columns(layout.join_cores(joined[:, :up_rows], each))
    taps = layout.join_cores(joined[:, up_rows : up_rows + pair], each)
    taps = taps.reshape(2, 2, each, 3, D // 4)
    pool_g0 = jnp.transpose(taps, (2, 3, 0, 1, 4)).reshape(each, 3 * D)
    pool_g1 = plain_columns(layout.join_cores(joined[:, up_rows + pair :], each))
    joined = layout.join_sides(red_first.finish())
    up_g0 = up_columns(layout.join_cores(joined[:, :up_rows], each))
    down_g0 = joined[:, up_rows : up_rows + half_ff].reshape(ff_each, D)
    proj_g0 = packed_columns(joined[:, up_rows + half_ff :])

    def own(block, number):
        return norm_w[block][:, number : number + 1]

    qkv_g0, own0, own1 = with_norm(
        product[:each], product[each : each + 1], own(0, 0), own(0, 1), qkv_w[0]
    )
    up_g0, own2, own3 = with_norm(
        up_g0[:each], up_g0[each : each + 1], own(0, 2), own(0, 3), up_w[0]
    )
    qkv_g1, own4, own5 = with_norm(
        qkv_g1[:each], qkv_g1[each : each + 1], own(1, 0), own(1, 1), qkv_w[1]
    )
    up_g1, own6, own7 = with_norm(
        up_g1[:each], up_g1[each : each + 1], own(1, 2), own(1, 3), up_w[1]
    )
    norm_g0 = jnp.stack([own0, own1, own2, own3], axis=1)
    norm_g1 = jnp.stack([own4, own5, own6, own7], axis=1)
    grads = [
        jnp.stack(pair)
        for pair in (
            (qkv_g0, qkv_g1),
            (proj_g0, proj_g1),
            (up_g0, up_g1),
            (down_g0, down_g1),
            (pool_g0, pool_g1),
            (norm_g0, norm_g1),
        )
    ]
    results = [
        update(grads[i], weights[i], velocities[i], averages[i], rate) for i in range(6)
    ]
    return (
        (activations, input_grad)
        + tuple(grads)
        + tuple(r[0] for r in results)
        + tuple(r[1] for r in results)
        + tuple(r[2] for r in results)
    )


def solution(mesh):
    groups, wide = mesh.shape["batch"], mesh.shape["wide"]

    def program(*args):
        cores = args[0].shape[0] // groups
        ranks = wide // (HEADS * cores)
        layout = Layout(groups, ranks, cores)
        rate = 0.5 / math.sqrt(math.prod(args[0].shape))
        dims = (groups, 4, 2, ranks, cores)
        fine = Mesh(mesh.devices.reshape(dims), ("b", "z", "x", "r", "s"))
        rows = ("z", "x", "r", "s")
        stream = P("b", rows, None)
        weight = P(None, rows, None)
        return jax.shard_map(
            lambda *local: shards(layout, rate, local),
            mesh=fine,
            in_specs=(stream, P("b"), stream) + (weight,) * 18,
            out_specs=(stream, stream) + (weight,) * 24,
            check_vma=False,
        )(*args)

    return program
```

```python
import functools
import math

import jax
import jax.numpy as jnp
import numpy as np
from jax import lax
from jax.experimental import pallas as pl
from jax.experimental.pallas import tpu as pltpu
from jax.sharding import Mesh, PartitionSpec as P

HEADS = 8
HEAD_DIM = 64
D = HEADS * HEAD_DIM
norm_eps = 1e-05
masked_score = -1e30
momentum_decay = 0.9
average_decay = 0.9
F32 = jnp.float32
BF16 = jnp.bfloat16
VMEM_LIMIT = 56 << 20
ROOT = math.sqrt(2.0 / math.pi)
CUBE = 0.044715
CHIP, CORE, SIDE, COLUMN, DEPTH, LENGTH, SHORT_LENGTH = range(7)


def split(value):
    high = value.astype(BF16)
    return high, (value - high.astype(F32)).astype(BF16)


def dot(a, b, dims):
    return lax.dot_general(a, b, (dims, ((), ())), preferred_element_type=F32)


NN = ((1,), (0,))
NT = ((1,), (1,))
TN = ((0,), (0,))


def matmul(left, right, dims=NN):
    rows = left.shape[0]
    high, low = split(left)
    right_high, right_low = split(right)
    both = dot(jnp.concatenate([high, low], axis=0), right_high, dims)
    return both[:rows] + both[rows:] + dot(high, right_low, dims)


def outer(left, right):
    columns = right.shape[1]
    high, low = split(left)
    right_high, right_low = split(right)
    both = dot(high, jnp.concatenate([right_high, right_low], axis=1), TN)
    return both[:, :columns] + both[:, columns:] + dot(low, right_high, TN)


def normalized(values):
    centred = values - jnp.mean(values, axis=-1, keepdims=True)
    variance = jnp.mean(centred * centred, axis=-1, keepdims=True)
    scale = lax.rsqrt(variance + norm_eps)
    return centred * scale, scale


def normalized_grad(grad, gain, normed, scale):
    inner = grad * gain
    along = jnp.mean(inner * normed, axis=-1, keepdims=True)
    return scale * (inner - jnp.mean(inner, axis=-1, keepdims=True) - normed * along)


def gelu_parts(u):
    curve = jnp.tanh(ROOT * (u + CUBE * u * u * u))
    return curve, 0.5 * u * (1.0 + curve)


def gelu_slope(u, curve):
    inner = ROOT * (1.0 + 3.0 * CUBE * u * u)
    return 0.5 * (1.0 + curve) + 0.5 * u * (1.0 - curve * curve) * inner


def rope_tables(rows):
    half = HEAD_DIM // 2
    freq = (10000.0 ** (-2.0 * np.arange(half, dtype=np.float32) / HEAD_DIM)).astype(np.float32)
    angles = np.arange(rows, dtype=np.float32)[:, None] * freq[None, :]
    cosine = np.cos(angles).astype(np.float32)
    sine = np.sin(angles).astype(np.float32)
    both = np.concatenate([cosine, cosine], axis=1)
    signed = np.concatenate([-sine, sine], axis=1)
    return (
        np.concatenate([both, both], axis=1),
        np.concatenate([signed, signed], axis=1),
        np.ascontiguousarray(cosine.T),
        np.ascontiguousarray(sine.T),
    )


def swap_halves(pair):
    half = HEAD_DIM // 2
    width = pair.shape[1]
    lane = lax.broadcasted_iota(jnp.int32, pair.shape, 1) % HEAD_DIM
    ahead = pltpu.roll(pair, width - half, 1)
    behind = pltpu.roll(pair, half, 1)
    return jnp.where(lane < half, ahead, behind)


def rows_from_heads(ref, parts):
    pair = 2 * HEAD_DIM
    top, bottom = [], []
    for part in range(parts):
        lanes = slice(part * pair, (part + 1) * pair)
        for k in range(HEADS // 2):
            even, odd = ref[2 * k, :, lanes], ref[2 * k + 1, :, lanes]
            first = lax.broadcasted_iota(jnp.int32, even.shape, 1) < HEAD_DIM
            top.append(jnp.where(first, even, pltpu.roll(odd, HEAD_DIM, 1)))
            bottom.append(jnp.where(first, pltpu.roll(even, HEAD_DIM, 1), odd))
    return jnp.concatenate(
        [jnp.concatenate(top, axis=1), jnp.concatenate(bottom, axis=1)], axis=0
    )


def rows_to_heads(rows, ref, parts):
    pair = 2 * HEAD_DIM
    half = rows.shape[0] // 2
    for part in range(parts):
        lanes = slice(part * pair, (part + 1) * pair)
        for k in range(HEADS // 2):
            at = part * D + k * pair
            top, bottom = rows[:half, at : at + pair], rows[half:, at : at + pair]
            first = lax.broadcasted_iota(jnp.int32, top.shape, 1) < HEAD_DIM
            ref[2 * k, :, lanes] = jnp.where(first, top, pltpu.roll(bottom, HEAD_DIM, 1))
            ref[2 * k + 1, :, lanes] = jnp.where(first, pltpu.roll(top, HEAD_DIM, 1), bottom)


def allowed_keys(first_row, rows, keys, length):
    key_pos = lax.broadcasted_iota(jnp.int32, (keys, rows), 0)
    query_pos = lax.broadcasted_iota(jnp.int32, (keys, rows), 1) + first_row
    return (key_pos <= query_pos) & (key_pos < length)


def attend_rows(raw, length, cos_ref, sin_ref, out_refs, rows, step, half_rows):
    packed_ref, turned_ref, lse_ref, qcat_ref, kcat_ref, vcat_ref = out_refs
    scale = HEAD_DIM ** (-0.5)
    for start in range(0, rows, step):
        part = slice(start, start + step)
        pair = raw[part, : 2 * HEAD_DIM]
        pair = pair * cos_ref[part, :] + swap_halves(pair) * sin_ref[part, :]
        lane = lax.broadcasted_iota(jnp.int32, pair.shape, 1)
        pair = jnp.where(lane < HEAD_DIM, pair * scale, pair)
        high, low = split(pair)
        qh, kh = high[:, :HEAD_DIM], high[:, HEAD_DIM:]
        ql, kl = low[:, :HEAD_DIM], low[:, HEAD_DIM:]
        vh, vl = split(raw[part, 2 * HEAD_DIM :])
        qcat_ref[part, :] = jnp.concatenate([qh, ql, qh], axis=1)
        kcat_ref[part, :] = jnp.concatenate([kh, kh, kl], axis=1)
        vcat_ref[part, :] = jnp.concatenate([vh, vh, vl], axis=1)
    value_pair = jnp.transpose(vcat_ref[:, HEAD_DIM:].astype(F32)).astype(BF16)
    value_high = value_pair[:HEAD_DIM]
    for start in range(0, rows, step):
        part = slice(start, start + step)
        keys = start + step
        scores = dot(kcat_ref[:keys, :], qcat_ref[part, :], NT)
        scores = jnp.where(allowed_keys(start, step, keys, length), scores, masked_score)
        row_max = jnp.max(scores, axis=0, keepdims=True)
        weights = jnp.exp(scores - row_max)
        total = jnp.sum(weights, axis=0, keepdims=True)
        wh, wl = split(weights)
        summed = dot(value_pair[:, :keys], wh, NN)
        summed = summed[:HEAD_DIM] + summed[HEAD_DIM:] + dot(value_high[:, :keys], wl, NN)
        turned = summed / total
        lse_ref[:, part] = jnp.broadcast_to(row_max + jnp.log(total), (8, step))
        turned_ref[:, part] = turned
    attended = jnp.transpose(
        jnp.concatenate([turned_ref[...], turned_ref[...]], axis=0)
    ).reshape(rows // (2 * half_rows), 2, half_rows, 2 * HEAD_DIM)
    lane = lax.broadcasted_iota(jnp.int32, attended[:, 0].shape, 2)
    packed_ref[...] = jnp.where(lane < HEAD_DIM, attended[:, 0], attended[:, 1])


def gathered_blocks(ids_ref, refs, distances, half_rows):
    for number, ref in enumerate(refs):
        side, part = divmod(number, 2)
        count = ref.shape[0]
        for slot in range(count):
            chip = ids_ref[CHIP] ^ distances[side][part * count + slot]
            first = pl.multiple_of((chip * 2 + side) * half_rows, 8)
            yield ref, slot, first


def first_attend_kernel(half_rows, step, distances, ids_ref, *refs):
    x_refs, (w_ref, cos_ref, sin_ref) = refs[:4], refs[4:7]
    out_refs, norm_ref, raw = refs[7:13], refs[13], refs[14]
    rows = raw.shape[0]
    total = sum(jnp.sum(ref[:, half_rows:, :], axis=0) for ref in x_refs)
    norm_ref[...] = total
    gain, shift = total[0:1], total[1:2]
    wh, wl = split(w_ref[...])
    for ref, slot, first in gathered_blocks(ids_ref, x_refs, distances, half_rows):
        hh, hl = split(normalized(ref[slot, :half_rows, :])[0] * gain + shift)
        raw[pl.ds(first, half_rows), :] = dot(hh, wh, NN) + dot(hh, wl, NN) + dot(hl, wh, NN)
    attend_rows(raw, ids_ref[LENGTH], cos_ref, sin_ref, out_refs, rows, step, half_rows)


def unpack_rows(packed_ref, raw, half_rows, parts):
    chips = packed_ref.shape[0]
    for chip in range(chips):
        for side in range(2):
            first = (chip * 2 + side) * half_rows
            pieces = [
                packed_ref[chip, :, (2 * part + side) * HEAD_DIM : (2 * part + side + 1) * HEAD_DIM]
                for part in range(parts)
            ]
            piece = pieces[0] if parts == 1 else jnp.concatenate(pieces, axis=1)
            raw[first : first + half_rows, :] = piece


def second_attend_kernel(half_rows, step, ids_ref, packed_ref, cos_ref, sin_ref, *refs):
    out_refs, raw = refs[:6], refs[6]
    rows = packed_ref.shape[0] * 2 * half_rows
    unpack_rows(packed_ref, raw, half_rows, 3)
    attend_rows(raw, ids_ref[SHORT_LENGTH], cos_ref, sin_ref, out_refs, rows, step, half_rows)


def attend_grad(
    rows, step, half_rows, length, refs, grad_ref, tables, out_ref, scratch
):
    qcat_ref, kcat_ref, vcat_ref, turned_ref, lse_ref = refs
    cos_ref, sin_ref, cos_t_ref, sin_t_ref = tables
    grad_rows, dk_acc, dv_acc, dq_t, dqkv = scratch
    scale = HEAD_DIM ** (-0.5)
    unpack_rows(grad_ref, grad_rows, half_rows, 1)
    key_pair = jnp.transpose(kcat_ref[:, HEAD_DIM:].astype(F32)).astype(BF16)
    key_high = key_pair[:HEAD_DIM]
    dk_acc[...] = jnp.zeros_like(dk_acc)
    dv_acc[...] = jnp.zeros_like(dv_acc)
    for start in range(0, rows, step):
        part = slice(start, start + step)
        keys = start + step
        grad = grad_rows[part, :]
        gh, gl = split(grad)
        gcat = jnp.concatenate([gh, gl, gh], axis=1)
        grad_t = jnp.transpose(jnp.concatenate([grad, grad], axis=1))[:HEAD_DIM]
        delta = jnp.sum(grad_t * turned_ref[:, part], axis=0, keepdims=True)
        scores = dot(kcat_ref[:keys, :], qcat_ref[part, :], NT)
        probs = jnp.where(
            allowed_keys(start, step, keys, length), jnp.exp(scores - lse_ref[0:1, part]), 0.0
        )
        grad_probs = dot(vcat_ref[:keys, :], gcat, NT)
        grad_scores = probs * (grad_probs - delta)
        ph, pw = split(probs)
        sh, sl = split(grad_scores)
        dv_acc[:keys, :] += dot(ph, gcat[:, : 2 * HEAD_DIM], NN)
        dv_acc[:keys, :HEAD_DIM] += dot(pw, gh, NN)
        dk_acc[:keys, :] += dot(sh, qcat_ref[part, : 2 * HEAD_DIM], NN)
        dk_acc[:keys, :HEAD_DIM] += dot(sl, qcat_ref[part, :HEAD_DIM], NN)
        turned = dot(key_pair[:, :keys], sh, NN)
        turned = turned[:HEAD_DIM] + turned[HEAD_DIM:] + dot(key_high[:, :keys], sl, NN)
        dq_t[:, part] = turned * scale
    half = HEAD_DIM // 2
    low, high = dq_t[:half, :], dq_t[half:, :]
    back_low = low * cos_t_ref[...] + high * sin_t_ref[...]
    back_high = high * cos_t_ref[...] - low * sin_t_ref[...]
    dq = jnp.transpose(jnp.concatenate([back_low, back_high, back_low, back_high], axis=0))
    for start in range(0, rows, step):
        part = slice(start, start + step)
        dk = dk_acc[part, :HEAD_DIM] + dk_acc[part, HEAD_DIM:]
        dk = jnp.concatenate([dk, dk], axis=1)
        dk = dk * cos_ref[part, :] - swap_halves(dk) * sin_ref[part, :]
        dv = dv_acc[part, :HEAD_DIM] + dv_acc[part, HEAD_DIM:]
        dqkv[part, :] = jnp.concatenate([dq[part, :HEAD_DIM], dk[:, :HEAD_DIM], dv], axis=1)
    chips = out_ref.shape[0]
    for chip in range(chips):
        first = chip * 2 * half_rows
        top = dqkv[first : first + half_rows, :]
        bottom = dqkv[first + half_rows : first + 2 * half_rows, :]
        pieces = []
        for part in range(3):
            lanes = slice(part * HEAD_DIM, (part + 1) * HEAD_DIM)
            pieces += [top[:, lanes], bottom[:, lanes]]
        out_ref[chip, :, :] = jnp.concatenate(pieces, axis=1)


def second_grad_kernel(half_rows, step, ids_ref, *refs):
    saved, grad_ref, tables, out_ref, scratch = refs[:5], refs[5], refs[6:10], refs[10], refs[11:]
    rows = saved[0].shape[0]
    length = ids_ref[SHORT_LENGTH]
    attend_grad(rows, step, half_rows, length, saved, grad_ref, tables, out_ref, scratch)


def first_grad_kernel(half_rows, step, distances, ids_ref, *refs):
    x_refs, saved, grad_ref, tables = refs[:4], refs[4:9], refs[9], refs[10:14]
    out_ref, m_ref, scratch = refs[14], refs[15], refs[16:]
    rows = saved[0].shape[0]
    length = ids_ref[LENGTH]
    attend_grad(rows, step, half_rows, length, saved, grad_ref, tables, out_ref, scratch[:5])
    dqkv, nh_ref, nl_ref = scratch[4:]
    for ref, slot, first in gathered_blocks(ids_ref, x_refs, distances, half_rows):
        nh, nl = split(normalized(ref[slot, :half_rows, :])[0])
        nh_ref[pl.ds(first, half_rows), :] = nh
        nl_ref[pl.ds(first, half_rows), :] = nl
    dh, dl = split(dqkv[...])
    nh = nh_ref[...]
    product = dot(nh, dh, TN) + dot(nh, dl, TN) + dot(nl_ref[...], dh, TN)
    owners, rows_each = m_ref.shape[0], m_ref.shape[1] - 8
    column = jnp.sum(dqkv[...], axis=0, keepdims=True)
    m_ref[:, :rows_each, :] = product.reshape(owners, rows_each, 3 * HEAD_DIM)
    m_ref[:, rows_each:, :] = jnp.broadcast_to(column[None], (owners, 8, 3 * HEAD_DIM))


class Loader:
    def __init__(self, ids_ref, sems):
        self.ids_ref = ids_ref
        self.sems = sems
        self.used = 0

    def start(self, src, dst):
        sem = self.sems.at[self.used]
        self.used += 1
        copy = pltpu.make_async_copy(src, dst, sem)
        copy.start()
        return copy

    def columns(self, gathered, unit, dst):
        return [[self.start(gathered.at[:, unit + k], dst.at[k])] for k in range(dst.shape[0])]

    def rows(self, gathered, unit, dst):
        run = dst.shape[0] // 4
        waits = []
        for k in range(4):
            owners = pl.ds(k * run, run)
            waits.append([self.start(gathered.at[owners, unit : unit + 4], dst.at[owners])])
        return waits


def ready(waits):
    for copy in waits:
        copy.wait()


def square(ref):
    return ref[...].reshape(D, D)


def pick(first, zero, one):
    return jnp.where(first, zero, one)


class Halves:
    def __init__(self, ids_ref, keep_ref, send_ref):
        self.zero = ids_ref[CORE] == 0
        self.keep_ref, self.send_ref = keep_ref, send_ref
        self.at = 0

    def put(self, keep, send):
        width = keep.shape[1]
        self.keep_ref[:, self.at : self.at + width] = keep
        self.send_ref[:, self.at : self.at + width] = send
        self.at += width

    def whole(self, value):
        self.put(value, value)

    def halved(self, zero, one):
        self.put(pick(self.zero, zero, one), pick(self.zero, one, zero))

    def granules(self, value, size, at):
        for k in range(value.shape[1] // (2 * size)):
            zero = value[:, 2 * k * size : (2 * k + 1) * size]
            one = value[:, (2 * k + 1) * size : (2 * k + 2) * size]
            lanes = slice(at + k * size, at + (k + 1) * size)
            self.keep_ref[:, lanes] = pick(self.zero, zero, one)
            self.send_ref[:, lanes] = pick(self.zero, one, zero)


def first_dense_kernel(
    ids_ref, stream_ref, got_ref, norm_ref, g_ref, full_ref, mixed_ref, u_ref, proj, up, down, sems
):
    load = Loader(ids_ref, sems)
    proj_wait = load.columns(g_ref, 0, proj)
    up_wait = load.columns(g_ref, 1, up)
    down_wait = load.rows(g_ref, 5, down)
    attended = rows_from_heads(got_ref, 1)
    ready(proj_wait[0])
    mixed = stream_ref[...] + matmul(attended, square(proj))
    mixed_ref[...] = mixed
    inner = normalized(mixed)[0] * norm_ref[2:3, :] + norm_ref[3:4, :]
    run = down.shape[0] // 4
    result = mixed
    for k in range(4):
        ready(up_wait[k])
        u = matmul(inner, up[k].reshape(D, D))
        u_ref[:, k * D : (k + 1) * D] = u
        hidden = gelu_parts(u)[1]
        ready(down_wait[k])
        result = result + matmul(hidden, down[k * run : (k + 1) * run].reshape(D, D))
    full_ref[...] = result


def shorten_kernel(
    ids_ref, full_ref, tail_ref, norm_ref, g_ref, short_ref, packed_ref, pool, qkv, moved, sems
):
    load = Loader(ids_ref, sems)
    pool_wait = load.columns(g_ref, 9, pool)
    qkv_wait = load.columns(g_ref, 12, qkv)
    shift_rows(full_ref, tail_ref, moved)
    rows = short_ref.shape[0]
    short = jnp.zeros((rows, D), F32)
    for i in range(3):
        ready(pool_wait[i])
        short = short + matmul(load_thirds(moved, 6 + i, rows), pool[i].reshape(D, D))
    short_ref[...] = short
    inner = normalized(short)[0] * norm_ref[4:5, :] + norm_ref[5:6, :]
    parts = []
    for i in range(3):
        ready(qkv_wait[i])
        parts.append(matmul(inner, qkv[i].reshape(D, D)))
    rows_to_heads(jnp.concatenate(parts, axis=1), packed_ref, 3)


LANES = 128
LANE_BLOCKS = D // LANES


def shift_rows(full_ref, tail_ref, moved):
    rows = full_ref.shape[0]
    for k in range(LANE_BLOCKS):
        lanes = slice(k * LANES, (k + 1) * LANES)
        moved[k, 6:8, :] = tail_ref[:, lanes]
        moved[k, 8 : 8 + rows, :] = full_ref[:, lanes]


def load_thirds(buffer, start, rows):
    pieces = [buffer[k, pl.ds(start, rows, stride=3), :] for k in range(LANE_BLOCKS)]
    return jnp.concatenate(pieces, axis=1)


def store_thirds(buffer, start, value):
    rows = value.shape[0]
    for k in range(LANE_BLOCKS):
        buffer[k, pl.ds(start, rows, stride=3), :] = value[:, k * LANES : (k + 1) * LANES]


def to_blocks(value, buffer):
    for k in range(LANE_BLOCKS):
        buffer[k] = value[:, k * LANES : (k + 1) * LANES]


def from_blocks(buffer):
    return jnp.concatenate([buffer[k] for k in range(LANE_BLOCKS)], axis=1)


def kept_cotangent(ids_ref, cot_ref):
    rows = cot_ref.shape[0]
    position = lax.broadcasted_iota(jnp.int32, cot_ref.shape, 0) + ids_ref[CHIP] * rows
    return jnp.where(position < ids_ref[LENGTH], cot_ref[...], 0.0)


def ffn_backward(grad, mixed, gain, u_of, curves, up_of, down_of, proj_of, halves, size):
    normed, scale = normalized(mixed)
    halves.whole(normed)
    base = halves.at
    halves.at += 4 * D
    halves.whole(grad)
    inner = jnp.zeros_like(mixed)
    each = D // 2
    for k in range(4):
        u = u_of(k)
        curve, hidden = curves(k, u)
        du = matmul(grad, down_of(k), NT) * gelu_slope(u, curve)
        halves.granules(du, size, base + k * each)
        halves.granules(hidden, size, base + 2 * D + k * each)
        inner = inner + matmul(du, up_of(k), NT)
    grad_mixed = grad + normalized_grad(inner, gain, normed, scale)
    return grad_mixed, matmul(grad_mixed, proj_of(), NT)


def middle_kernel(size, *refs):
    (ids_ref, short_ref, got_ref, norm_ref, full_ref, cot_ref, g_ref), refs = refs[:7], refs[7:]
    late_ref, refs = refs[0], refs[1:]
    (act_ref, grad_ref, mixed_ref, keep_ref, send_ref), refs = refs[:5], refs[5:]
    proj, up, down, pool, kept, act, sems = refs
    load = Loader(ids_ref, sems)
    proj_wait = load.columns(g_ref, 15, proj)
    up_wait = load.columns(late_ref, 0, up)
    down_wait = load.rows(late_ref, 4, down)
    pool_wait = load.columns(g_ref, 16, pool)
    to_blocks(kept_cotangent(ids_ref, cot_ref), kept)
    to_blocks(full_ref[...], act)
    attended = rows_from_heads(got_ref, 1)
    run = down.shape[0] // 4
    rows = short_ref.shape[0]
    up_of = lambda k: up[k].reshape(D, D)
    down_of = lambda k: down[k * run : (k + 1) * run].reshape(D, D)
    ready(proj_wait[0])
    mixed = short_ref[...] + matmul(attended, square(proj))
    gain = norm_ref[6:7, :]
    inner = normalized(mixed)[0] * gain + norm_ref[7:8, :]
    for wait in up_wait:
        ready(wait)
    us = [matmul(inner, up_of(k)) for k in range(4)]
    gelus = [gelu_parts(u) for u in us]
    for wait in down_wait:
        ready(wait)
    result = mixed
    for k in range(4):
        result = result + matmul(gelus[k][1], down_of(k))
    grad = jnp.zeros((rows, D), F32)
    groups = []
    for i in range(3):
        ready(pool_wait[i])
        tap = pool[i].reshape(D, D)
        store_thirds(act, i, load_thirds(act, i, rows) + matmul(result, tap))
        groups.append(load_thirds(kept, i, rows))
        grad = grad + matmul(groups[i], tap, NT)
    act_ref[...] = from_blocks(act)
    halves = Halves(ids_ref, keep_ref, send_ref)
    grad_mixed, grad_attended = ffn_backward(
        grad,
        mixed,
        gain,
        lambda k: us[k],
        lambda k, u: gelus[k],
        up_of,
        down_of,
        lambda: square(proj),
        halves,
        size,
    )
    rows_to_heads(grad_attended, grad_ref, 1)
    mixed_ref[...] = grad_mixed
    halves.whole(attended)
    halves.halved(grad_mixed[:, : D // 2], grad_mixed[:, D // 2 :])
    halves.whole(result)
    wide = jnp.concatenate(groups, axis=1)
    halves.halved(wide[:, : 3 * D // 2], wide[:, 3 * D // 2 :])


def lengthen_grad_kernel(
    ids_ref,
    got_ref,
    short_ref,
    mixed_ref,
    norm_ref,
    full_ref,
    tail_ref,
    g_ref,
    shifted_ref,
    keep_ref,
    send_ref,
    pool,
    qkv,
    moved,
    back,
    sems,
):
    load = Loader(ids_ref, sems)
    qkv_wait = load.columns(g_ref, 12, qkv)
    pool_wait = load.columns(g_ref, 9, pool)
    dqkv = rows_from_heads(got_ref, 3)
    rows = short_ref.shape[0]
    normed, scale = normalized(short_ref[...])
    inner = jnp.zeros((rows, D), F32)
    for i in range(3):
        ready(qkv_wait[i])
        inner = inner + matmul(dqkv[:, i * D : (i + 1) * D], qkv[i].reshape(D, D), NT)
    grad = mixed_ref[...] + normalized_grad(inner, norm_ref[4:5, :], normed, scale)
    for i in range(3):
        ready(pool_wait[i])
        store_thirds(back, i, matmul(grad, pool[i].reshape(D, D), NT))
    shifted_ref[...] = from_blocks(back)
    shift_rows(full_ref, tail_ref, moved)
    halves = Halves(ids_ref, keep_ref, send_ref)
    halves.whole(normed)
    halves.halved(dqkv[:, : 3 * D // 2], dqkv[:, 3 * D // 2 :])
    for i in range(3):
        halves.whole(load_thirds(moved, 6 + i, rows))
    halves.halved(grad[:, : D // 2], grad[:, D // 2 :])


def first_dense_grad_kernel(
    size,
    ids_ref,
    shifted_ref,
    next_ref,
    cot_ref,
    mixed_in_ref,
    u_ref,
    got_ref,
    norm_ref,
    g_ref,
    grad_ref,
    mixed_ref,
    keep_ref,
    send_ref,
    proj,
    up,
    down,
    moved,
    sems,
):
    load = Loader(ids_ref, sems)
    down_wait = load.rows(g_ref, 5, down)
    up_wait = load.columns(g_ref, 1, up)
    proj_wait = load.columns(g_ref, 0, proj)
    rows = cot_ref.shape[0]
    moved[:rows, :] = shifted_ref[...]
    moved[rows : rows + 2, :] = next_ref[...]
    grad = kept_cotangent(ids_ref, cot_ref) + moved[2 : 2 + rows, :]
    run = down.shape[0] // 4

    def up_of(k):
        ready(up_wait[k])
        return up[k].reshape(D, D)

    def down_of(k):
        ready(down_wait[k])
        return down[k * run : (k + 1) * run].reshape(D, D)

    def proj_of():
        ready(proj_wait[0])
        return square(proj)

    halves = Halves(ids_ref, keep_ref, send_ref)
    grad_mixed, grad_attended = ffn_backward(
        grad,
        mixed_in_ref[...],
        norm_ref[2:3, :],
        lambda k: u_ref[:, k * D : (k + 1) * D],
        lambda k, u: gelu_parts(u),
        up_of,
        down_of,
        proj_of,
        halves,
        size,
    )
    rows_to_heads(grad_attended, grad_ref, 1)
    mixed_ref[...] = grad_mixed
    halves.whole(rows_from_heads(got_ref, 1))
    halves.halved(grad_mixed[:, : D // 2], grad_mixed[:, D // 2 :])


def input_grad_kernel(
    ids_ref, got_ref, stream_ref, mixed_ref, norm_ref, g_ref, out_ref, qkv, sems
):
    load = Loader(ids_ref, sems)
    qkv_wait = load.columns(g_ref, 0, qkv)
    dqkv = rows_from_heads(got_ref, 3)
    normed, scale = normalized(stream_ref[...])
    inner = jnp.zeros_like(normed)
    for i in range(3):
        ready(qkv_wait[i])
        inner = inner + matmul(dqkv[:, i * D : (i + 1) * D], qkv[i].reshape(D, D), NT)
    out_ref[...] = mixed_ref[...] + normalized_grad(inner, norm_ref[0:1, :], normed, scale)


class Factors:
    def __init__(self, keep_ref, got_ref):
        self.keep_ref, self.got_ref = keep_ref, got_ref
        self.at = 0

    def take(self, width):
        lanes = slice(self.at, self.at + width)
        self.at += width
        return jnp.concatenate([self.keep_ref[:, lanes], self.got_ref[:, lanes]], axis=0)


def side_halves(ids_ref, value):
    width = value.shape[1] // 2
    zero = ids_ref[SIDE] == 0
    first, second = value[:, :width], value[:, width:]
    return pick(zero, first, second), pick(zero, second, first)


def place_of(ids_ref, depth, rank, ranks):
    distance = depth ^ ids_ref[DEPTH]
    return ((distance & 1) * 2 + (distance >> 1)) * ranks + rank


def place_by_column(ids_ref, ref, rows, block, ranks):
    for depth in range(4):
        for column in range(2):
            for rank in range(ranks):
                chip = (depth * 2 + column) * ranks + rank
                place = place_of(ids_ref, depth, rank, ranks)
                ref[column ^ ids_ref[COLUMN], place, rows, :] = block(chip)


def packed_rows(rows):
    count = rows.shape[0] // 4
    return jnp.concatenate([rows[i * count : (i + 1) * count] for i in range(4)], axis=1)


def place_blocks(ids_ref, ref, at, product, each, ranks):
    rows = slice(at, at + each)
    place_by_column(
        ids_ref, ref, rows, lambda chip: product[chip * each : (chip + 1) * each], ranks
    )
    return at + each


def place_sums(ids_ref, ref, at, value, ranks):
    total = jnp.broadcast_to(jnp.sum(value, axis=0, keepdims=True), (8, value.shape[1]))
    place_by_column(ids_ref, ref, slice(at, at + 8), lambda chip: total, ranks)
    return at + 8


def place_packed(ids_ref, ref, at, product, each, ranks):
    rows = slice(at, at + each // 4)
    place_by_column(
        ids_ref,
        ref,
        rows,
        lambda chip: packed_rows(product[chip * each : (chip + 1) * each]),
        ranks,
    )
    return at + each // 4


def place_by_side(ids_ref, refs, at, products, each, ranks):
    zero = ids_ref[COLUMN] == 0
    for depth in range(4):
        for rank in range(ranks):
            first = ((depth * 2) * ranks + rank) * each
            second = ((depth * 2 + 1) * ranks + rank) * each
            place = place_of(ids_ref, depth, rank, ranks)
            for side in range(2):
                far = side ^ ids_ref[SIDE]
                one = products[side][first : first + each]
                two = products[side][second : second + each]
                refs[0][place, far, at : at + each, :] = pick(zero, one, two)
                refs[1][place, far, at : at + each, :] = pick(zero, two, one)
    return at + each


def dense_products_kernel(ranks, size, each, ids_ref, keep_ref, got_ref, *refs):
    up_refs, down_refs = refs[:2], refs[2:]
    factors = Factors(keep_ref, got_ref)
    normed, du, hidden, grad = (factors.take(w * D) for w in (1, 2, 2, 1))
    attended, grad_mixed = factors.take(D), factors.take(D // 2)
    for ref, half, narrow in zip(
        up_refs, side_halves(ids_ref, du), side_halves(ids_ref, grad_mixed)
    ):
        at = place_blocks(ids_ref, ref, 0, outer(normed, half), each, ranks)
        at = place_sums(ids_ref, ref, at, half, ranks)
        place_packed(ids_ref, ref, at, outer(attended, narrow), each, ranks)
    product = outer(hidden, grad).reshape(D // each, 2, size // 2, D)
    sides = [product[:, side].reshape(-1, D) for side in range(2)]
    place_by_side(ids_ref, down_refs, 0, sides, size // 2, ranks)


def shorten_products_kernel(
    ranks, each, ids_ref, keep_ref, got_ref, up_keep_ref, up_got_ref, *refs
):
    factors = Factors(keep_ref, got_ref)
    normed, dqkv = factors.take(D), factors.take(3 * D // 2)
    shifted = [factors.take(D) for _ in range(3)]
    grad = factors.take(D // 2)
    factors = Factors(up_keep_ref, up_got_ref)
    factors.at = 15 * D // 2
    short, groups = factors.take(D), factors.take(3 * D // 2)
    for ref, half, narrow, wide in zip(
        refs,
        side_halves(ids_ref, dqkv),
        side_halves(ids_ref, grad),
        side_halves(ids_ref, groups),
    ):
        at = place_blocks(ids_ref, ref, 0, outer(normed, half), each, ranks)
        at = place_sums(ids_ref, ref, at, half, ranks)
        taps = jnp.concatenate([outer(rows, narrow) for rows in shifted], axis=1)
        at = place_blocks(ids_ref, ref, at, taps, each, ranks)
        place_blocks(ids_ref, ref, at, outer(short, wide), each, ranks)


PER_US = 1.1e+08
SMEM = pl.BlockSpec(memory_space=pltpu.SMEM)
VMEM = pl.BlockSpec(memory_space=pltpu.VMEM)
ANY = pl.BlockSpec(memory_space=pl.ANY)


def attend_outs(rows, half_rows):
    width = 3 * HEAD_DIM
    return [
        shape(rows // (2 * half_rows), half_rows, 2 * HEAD_DIM),
        shape(HEAD_DIM, rows),
        shape(8, rows),
        jax.ShapeDtypeStruct((rows, width), BF16),
        jax.ShapeDtypeStruct((rows, width), BF16),
        jax.ShapeDtypeStruct((rows, width), BF16),
    ]


def shape(*dims):
    return jax.ShapeDtypeStruct(dims, F32)


def call(time, kernel, outs, scratch, ids, args, weights=(), copies=0):
    scratch = list(scratch)
    if copies:
        scratch.append(pltpu.SemaphoreType.DMA((copies,)))
    return pl.pallas_call(
        kernel,
        out_shape=list(outs),
        in_specs=[SMEM] + [VMEM] * len(args) + [ANY] * len(weights),
        out_specs=[VMEM] * len(outs),
        scratch_shapes=scratch,
        compiler_params=pltpu.CompilerParams(vmem_limit_bytes=VMEM_LIMIT),
        cost_estimate=pl.CostEstimate(
            flops=int(time * PER_US), bytes_accessed=0, transcendentals=0
        ),
    )(ids, *args, *weights)


def query_step(rows):
    return math.gcd(rows, 256)


def bit_count(size):
    return size.bit_length() - 1


def swap_with(value, axis, size, mask):
    return lax.ppermute(value, axis, [(i, i ^ mask) for i in range(size)])


def by_bit(bit, own, other):
    return jnp.where(bit == 0, jnp.stack([own, other]), jnp.stack([other, own]))


class Layout:
    def __init__(self, groups, ranks, cores):
        self.groups = groups
        self.ranks = ranks
        self.cores = cores
        self.chips = HEADS * ranks
        self.devices = self.chips * cores
        self.chip_axes = ("z", "x", "r") if ranks > 1 else ("z", "x")

    def chip(self):
        return lax.axis_index(("z", "x", "r"))

    def swap_chip(self, value, mask):
        return swap_with(value, self.chip_axes, self.chips, mask)

    def swap_core(self, value):
        return swap_with(value, "s", 2, 1)

    def exchange_cores(self, value):
        core = lax.axis_index("s")
        own = lax.dynamic_index_in_dim(value, core, 0, keepdims=False)
        away = lax.dynamic_index_in_dim(value, 1 - core, 0, keepdims=False)
        return by_bit(core, own, self.swap_core(away))

    def shift_chip(self, value, distance):
        chips = range(self.chips)
        route = [(i - distance, i) for i in chips if i - distance in chips]
        return lax.ppermute(value, self.chip_axes, route)

    def gather_chips(self, value, masks):
        held = value[None]
        for mask in masks[:-1]:
            held = jnp.concatenate([held, self.swap_chip(held, mask)], axis=0)
        return [held, self.swap_chip(held, masks[-1])]

    def distances(self, masks):
        found = [0]
        for mask in masks:
            found = found + [d ^ mask for d in found]
        return found

    def heads_to_rows(self, value):
        value = value.reshape((HEADS, self.ranks) + value.shape[1:])
        mine = lax.dynamic_index_in_dim(value, lax.axis_index("r"), 1, keepdims=False)
        return lax.all_to_all(mine, ("z", "x"), 0, 0, tiled=True)

    def rows_to_heads(self, value):
        got = lax.all_to_all(value, ("z", "x"), 0, 0, tiled=True)
        if self.ranks > 1:
            got = lax.all_gather(got, "r", axis=1, tiled=False)
            got = got.reshape((self.chips,) + value.shape[1:])
        return got

    def join_sides(self, value):
        return by_bit(lax.axis_index("b") % 2, value, swap_with(value, "b", self.groups, 1))

    def join_cores(self, value, each):
        core = lax.axis_index("s")
        both = value[:, 2 * each :]

        def rows_of(owner):
            rows = lax.dynamic_slice_in_dim(value, owner * each, each, 1)
            return jnp.concatenate([rows, both], axis=1)

        return by_bit(core, rows_of(core), self.swap_core(rows_of(1 - core)))

    def sum_batch(self, value):
        for place in range(bit_count(self.groups)):
            value = value + swap_with(value, "b", self.groups, 1 << place)
        return value


class Reduction:
    def __init__(self, layout, batch_first, keep, send):
        self.layout = layout
        self.batch_first = batch_first
        self.keep, self.send = keep, send
        self.stage = 0

    def step(self):
        groups, ranks = self.layout.groups, self.layout.ranks
        axes = (("b", groups, 1), ("x", 2, 1), ("z", 4, 1), ("z", 4, 2))
        if not self.batch_first:
            axes = (axes[1], axes[0]) + axes[2:]
        got = swap_with(self.send, *axes[self.stage])
        if self.stage == 0:
            stay, away = (0, 1) if self.batch_first else ((slice(None), 0), (slice(None), 1))
        else:
            count = got.shape[0] // 2
            stay, away = slice(0, count), slice(count, None)
        if self.stage < 3:
            self.keep, self.send = self.keep[stay] + got[stay], self.keep[away] + got[away]
        else:
            self.keep = self.last(self.keep + got)
        self.stage += 1

    def last(self, value):
        if self.layout.ranks > 1:
            rank = lax.axis_index("r")
            keep = lax.dynamic_index_in_dim(value, rank, 0, keepdims=False)
            send = lax.dynamic_index_in_dim(value, 1 - rank, 0, keepdims=False)
            value = keep + swap_with(send, "r", 2, 1)
        else:
            value = value[0]
        for place in range(1, bit_count(self.layout.groups)):
            value = value + swap_with(value, "b", self.layout.groups, 1 << place)
        return value

    def finish(self):
        while self.stage < 4:
            self.step()
        return self.keep


def tied(value, *reductions):
    value, kept = lax.optimization_barrier((value, [r.keep for r in reductions]))
    for r, keep in zip(reductions, kept):
        r.keep = keep
    return value


def column_blocks(mat):
    return [mat[:, i * D : (i + 1) * D] for i in range(mat.shape[1] // D)]


def update(grad, weight, velocity, average, rate):
    momentum = momentum_decay * velocity + grad
    updated = weight - rate * (grad + momentum_decay * momentum)
    smooth = average_decay * average + (1.0 - average_decay) * updated
    return (momentum, smooth, updated)


def with_norm(product, columns, gain, shift, weight):
    grad = gain * product + shift * columns
    return grad, jnp.sum(weight * product, axis=1), jnp.sum(weight * columns, axis=1)


def shards(layout, rate, args):
    inputs, lengths, cotangent = args[:3]
    weights, velocities, averages = args[3:9], args[9:15], args[15:21]
    qkv_w, proj_w, up_w, down_w, pool_w, norm_w = weights
    half = inputs.shape[1]
    rows = 2 * half
    short_half, short_rows = half // 3, rows // 3
    each = qkv_w.shape[1]
    ff_each = down_w.shape[1]
    owners, chips, ranks = layout.devices, layout.chips, layout.ranks
    chip = layout.chip()
    core = lax.axis_index("s")
    side = lax.axis_index("b") % 2
    owner = chip * layout.cores + core
    length = lengths[core]
    places = [chip, core, side, lax.axis_index("x"), lax.axis_index("z")]
    ids = jnp.stack(places + [length, length // 3]).astype(jnp.int32)
    seq = chips * rows
    short_seq = seq // 3
    bits = bit_count(chips)

    norm_local = jnp.transpose(norm_w, (0, 2, 1)).reshape(8, each)
    norm_lanes = lax.dynamic_update_slice(
        jnp.zeros((8, D), F32), norm_local, (0, owner * each)
    )
    carried = jnp.concatenate([inputs, jnp.broadcast_to(norm_lanes, (2, 8, D))], axis=1)
    carried = layout.exchange_cores(carried)
    stream = carried[:, :half].reshape(rows, D)
    masks_a = tuple(1 << i for i in reversed(range(bits)))
    masks_b = (1,) + tuple(1 << i for i in reversed(range(1, bits)))
    distances = (layout.distances(masks_a), layout.distances(masks_b))
    blocks = layout.gather_chips(carried[0], masks_a) + layout.gather_chips(carried[1], masks_b)

    head_cols = jnp.transpose(qkv_w[0].reshape(each, 3, HEADS, HEAD_DIM), (2, 0, 1, 3))
    head_cols = head_cols.reshape(HEADS, each, 3 * HEAD_DIM)
    head_cols = jnp.repeat(head_cols, ranks * layout.cores, axis=0)
    wide_axes = layout.chip_axes + ("s",)
    head_w = lax.all_to_all(head_cols, wide_axes, 0, 0, tiled=True)
    head_w = head_w.reshape(D, 3 * HEAD_DIM)

    units = lambda pieces: jnp.concatenate(pieces, axis=0).reshape(-1, each, D)
    packed = units(
        [proj_w[0]]
        + column_blocks(up_w[0])
        + [down_w[0]]
        + column_blocks(pool_w[0])
        + column_blocks(qkv_w[1])
        + [proj_w[1]]
        + column_blocks(pool_w[1])
    )
    gathered = lax.all_gather(packed, wide_axes, axis=0, tiled=False)
    second = units(column_blocks(up_w[1]) + [down_w[1]])
    second = lax.all_gather(second, wide_axes, axis=0, tiled=False)
    last = units(column_blocks(qkv_w[0]))
    last = lax.all_gather(last, wide_axes, axis=0, tiled=False)

    cos, sin, cos_t, sin_t = rope_tables(seq)
    tables = (cos, sin)
    tables_t = (cos_t, sin_t)
    short_tables = (cos[:short_seq], sin[:short_seq])
    short_tables_t = (cos_t[:, :short_seq], sin_t[:, :short_seq])
    step = query_step(seq)
    short_step = query_step(short_seq)
    vmem = lambda *dims: pltpu.VMEM(dims, F32)
    column_buffer = lambda count: vmem(count, owners, each, D)
    row_buffer = vmem(owners, 4, each, D)
    blocks_of = lambda count: vmem(LANE_BLOCKS, count, LANES)

    outs = call(
        10,
        functools.partial(first_attend_kernel, half, step, distances),
        attend_outs(seq, half) + [shape(8, D)],
        [vmem(seq, 3 * HEAD_DIM)],
        ids,
        [*blocks, head_w, *tables],
    )
    saved0, norm = (outs[3], outs[4], outs[5], outs[1], outs[2]), outs[6]
    got0 = layout.heads_to_rows(outs[0])
    full, mixed0, u0 = call(
        8,
        first_dense_kernel,
        [shape(rows, D), shape(rows, D), shape(rows, 4 * D)],
        [column_buffer(1), column_buffer(4), row_buffer],
        ids,
        [stream, got0, norm],
        [gathered],
        9,
    )

    tail = layout.shift_chip(full[-2:], 1)
    shortened, to_send = call(
        5,
        shorten_kernel,
        [shape(short_rows, D), shape(HEADS, short_half, 6 * HEAD_DIM)],
        [column_buffer(3), column_buffer(3), blocks_of(rows + 8)],
        ids,
        [full, tail, norm],
        [gathered],
        6,
    )
    outs = call(
        3,
        functools.partial(second_attend_kernel, short_half, short_step),
        attend_outs(short_seq, short_half),
        [vmem(short_seq, 3 * HEAD_DIM)],
        ids,
        [layout.rows_to_heads(to_send), *short_tables],
    )
    saved1 = (outs[3], outs[4], outs[5], outs[1], outs[2])
    got1 = layout.heads_to_rows(outs[0])
    cot = layout.exchange_cores(cotangent).reshape(rows, D)
    middle_wide = 10 * D
    activations, grad_att1, grad_mixed1, keep_a, send_a = call(
        13,
        functools.partial(middle_kernel, ff_each),
        [
            shape(rows, D),
            shape(HEADS, short_half, 2 * HEAD_DIM),
            shape(short_rows, D),
            shape(short_rows, middle_wide),
            shape(short_rows, middle_wide),
        ],
        [column_buffer(1), column_buffer(4), row_buffer, column_buffer(3)]
        + [blocks_of(rows), blocks_of(rows)],
        ids,
        [shortened, got1, norm, full, cot],
        [gathered, second],
        12,
    )

    depth = 4 * ranks
    pair = 2 * each
    up_rows = pair + 8
    up_out = shape(2, depth, up_rows + each // 2, D)
    down_out = shape(depth, 2, ff_each // 2, D)
    got_a = layout.swap_core(send_a)
    up_keep, up_send, down_keep, down_send = call(
        6,
        functools.partial(dense_products_kernel, ranks, ff_each, pair),
        [up_out, up_out, down_out, down_out],
        [],
        ids,
        [keep_a, got_a],
    )
    red_up1 = Reduction(layout, True, up_keep, up_send)
    red_down1 = Reduction(layout, False, down_keep, down_send)

    scratch = lambda count: [
        vmem(count, HEAD_DIM),
        vmem(count, 2 * HEAD_DIM),
        vmem(count, 2 * HEAD_DIM),
        vmem(HEAD_DIM, count),
        vmem(count, 3 * HEAD_DIM),
    ]
    got = layout.rows_to_heads(grad_att1)
    got = tied(got, red_up1, red_down1)
    (to_send,) = call(
        4,
        functools.partial(second_grad_kernel, short_half, short_step),
        [shape(chips, short_half, 6 * HEAD_DIM)],
        scratch(short_seq),
        ids,
        [*saved1, got, *short_tables, *short_tables_t],
    )
    got = layout.heads_to_rows(to_send)
    got, red_down1.send = lax.optimization_barrier((got, red_down1.send))
    grad_shifted, keep_b, send_b = call(
        6.5,
        lengthen_grad_kernel,
        [shape(rows, D), shape(short_rows, 6 * D), shape(short_rows, 6 * D)],
        [column_buffer(3), column_buffer(3), blocks_of(rows + 8), blocks_of(rows)],
        ids,
        [got, shortened, grad_mixed1, norm, full, tail],
        [gathered],
        6,
    )
    head = layout.shift_chip(grad_shifted[:2], -1)
    pool_out = shape(2, depth, up_rows + 2 * pair, 3 * D // 4)
    pool_keep, pool_send = call(
        7,
        functools.partial(shorten_products_kernel, ranks, pair),
        [pool_out, pool_out],
        [],
        ids,
        [keep_b, layout.swap_core(send_b), keep_a, got_a],
    )
    red_pool = Reduction(layout, True, pool_keep, pool_send)
    red_up1.step()
    head = tied(head, red_up1)
    head = tied(head, red_pool)
    first_wide = 15 * D // 2
    grad_att0, grad_mixed0, keep_c, send_c = call(
        12.5,
        functools.partial(first_dense_grad_kernel, ff_each),
        [
            shape(HEADS, half, 2 * HEAD_DIM),
            shape(rows, D),
            shape(rows, first_wide),
            shape(rows, first_wide),
        ],
        [column_buffer(1), column_buffer(4), row_buffer, vmem(rows + 8, D)],
        ids,
        [grad_shifted, head, cot, mixed0, u0, got0, norm],
        [gathered],
        9,
    )
    up_keep, up_send, down_keep, down_send = call(
        9,
        functools.partial(dense_products_kernel, ranks, ff_each, pair),
        [up_out, up_out, down_out, down_out],
        [],
        ids,
        [keep_c, layout.swap_core(send_c)],
    )
    red_up0 = Reduction(layout, True, up_keep, up_send)
    red_down0 = Reduction(layout, False, down_keep, down_send)
    got = layout.rows_to_heads(grad_att0)
    got = tied(got, red_up0, red_down0)
    got = tied(got, red_up1, red_down1)
    red_up1.step()
    red_down1.step()
    to_send, product = call(
        16,
        functools.partial(first_grad_kernel, half, step, distances),
        [shape(chips, half, 6 * HEAD_DIM), shape(owners, each + 8, 3 * HEAD_DIM)],
        scratch(seq) + [pltpu.VMEM((seq, D), BF16), pltpu.VMEM((seq, D), BF16)],
        ids,
        [*blocks, *saved0, got, *tables, *tables_t],
    )
    red_pool.step()
    to_send = tied(to_send, red_pool)
    got = layout.heads_to_rows(to_send)
    got, product = lax.optimization_barrier((got, product))
    (input_grad,) = call(
        5,
        input_grad_kernel,
        [shape(rows, D)],
        [column_buffer(3)],
        ids,
        [got, stream, grad_mixed0, norm],
        [last],
        3,
    )
    input_grad = layout.exchange_cores(input_grad.reshape(2, half, D))
    activations = layout.exchange_cores(activations.reshape(2, half, D))

    product = product.reshape(HEADS, ranks, layout.cores, each + 8, 3 * HEAD_DIM)
    product = lax.dynamic_index_in_dim(product, lax.axis_index("r"), 1, keepdims=False)
    keep = lax.dynamic_index_in_dim(product, core, 1, keepdims=False)
    away = lax.dynamic_index_in_dim(product, 1 - core, 1, keepdims=False)
    product = layout.sum_batch(keep + layout.swap_core(away))
    product = lax.all_to_all(product, ("z", "x"), 0, 0, tiled=True)
    product = jnp.transpose(
        product.reshape(HEADS, each + 8, 3, HEAD_DIM), (1, 2, 0, 3)
    ).reshape(each + 8, 3 * D)

    def up_columns(joined):
        value = joined.reshape(2, 2, each + 8, D // ff_each, ff_each)
        return jnp.transpose(value, (2, 1, 3, 0, 4)).reshape(each + 8, 4 * D)

    def plain_columns(joined):
        return jnp.transpose(joined, (2, 0, 1, 3)).reshape(joined.shape[2], -1)

    def packed_columns(value):
        value = value.reshape(2, each // 2, 4, D // 4)
        value = jnp.transpose(value, (0, 2, 1, 3)).reshape(2, pair, D // 4)
        return plain_columns(layout.join_cores(value, each))

    joined = layout.join_sides(
        jnp.concatenate([red_up1.finish(), red_down1.finish()], axis=0)
    )
    up_g1 = up_columns(layout.join_cores(joined[:, :up_rows], each))
    proj_g1 = packed_columns(joined[:, up_rows : up_rows + each // 2])
    down_g1 = joined[:, up_rows + each // 2 :].reshape(ff_each, D)
    joined = layout.join_sides(red_pool.finish())
    qkv_g1 = plain_columns(layout.join_cores(joined[:, :up_rows], each))
    taps = layout.join_cores(joined[:, up_rows : up_rows + pair], each)
    taps = taps.reshape(2, 2, each, 3, D // 4)
    pool_g0 = jnp.transpose(taps, (2, 3, 0, 1, 4)).reshape(each, 3 * D)
    pool_g1 = plain_columns(layout.join_cores(joined[:, up_rows + pair :], each))
    joined = layout.join_sides(
        jnp.concatenate([red_up0.finish(), red_down0.finish()], axis=0)
    )
    up_g0 = up_columns(layout.join_cores(joined[:, :up_rows], each))
    proj_g0 = packed_columns(joined[:, up_rows : up_rows + each // 2])
    down_g0 = joined[:, up_rows + each // 2 :].reshape(ff_each, D)

    def own(block, number):
        return norm_w[block][:, number : number + 1]

    qkv_g0, own0, own1 = with_norm(
        product[:each], product[each : each + 1], own(0, 0), own(0, 1), qkv_w[0]
    )
    up_g0, own2, own3 = with_norm(
        up_g0[:each], up_g0[each : each + 1], own(0, 2), own(0, 3), up_w[0]
    )
    qkv_g1, own4, own5 = with_norm(
        qkv_g1[:each], qkv_g1[each : each + 1], own(1, 0), own(1, 1), qkv_w[1]
    )
    up_g1, own6, own7 = with_norm(
        up_g1[:each], up_g1[each : each + 1], own(1, 2), own(1, 3), up_w[1]
    )
    norm_g0 = jnp.stack([own0, own1, own2, own3], axis=1)
    norm_g1 = jnp.stack([own4, own5, own6, own7], axis=1)
    grads = [
        jnp.stack(pair)
        for pair in (
            (qkv_g0, qkv_g1),
            (proj_g0, proj_g1),
            (up_g0, up_g1),
            (down_g0, down_g1),
            (pool_g0, pool_g1),
            (norm_g0, norm_g1),
        )
    ]
    results = [
        update(grads[i], weights[i], velocities[i], averages[i], rate) for i in range(6)
    ]
    return (
        (activations, input_grad)
        + tuple(grads)
        + tuple(r[0] for r in results)
        + tuple(r[1] for r in results)
        + tuple(r[2] for r in results)
    )


def solution(mesh):
    groups, wide = mesh.shape["batch"], mesh.shape["wide"]

    def program(*args):
        cores = args[0].shape[0] // groups
        ranks = wide // (HEADS * cores)
        layout = Layout(groups, ranks, cores)
        rate = 0.5 / math.sqrt(math.prod(args[0].shape))
        dims = (groups, 4, 2, ranks, cores)
        fine = Mesh(mesh.devices.reshape(dims), ("b", "z", "x", "r", "s"))
        rows = ("z", "x", "r", "s")
        stream = P("b", rows, None)
        weight = P(None, rows, None)
        return jax.shard_map(
            lambda *local: shards(layout, rate, local),
            mesh=fine,
            in_specs=(stream, P("b"), stream) + (weight,) * 18,
            out_specs=(stream, stream) + (weight,) * 24,
            check_vma=False,
        )(*args)

    return program
```

```python
import functools
import math

import jax
import jax.numpy as jnp
import numpy as np
from jax import lax
from jax.experimental import pallas as pl
from jax.experimental.pallas import tpu as pltpu
from jax.sharding import Mesh, PartitionSpec as P

HEADS = 8
HEAD_DIM = 64
D = HEADS * HEAD_DIM
norm_eps = 1e-05
masked_score = -1e30
momentum_decay = 0.9
average_decay = 0.9
F32 = jnp.float32
BF16 = jnp.bfloat16
VMEM_LIMIT = 56 << 20
ROOT = math.sqrt(2.0 / math.pi)
CUBE = 0.044715
CHIP, CORE, SIDE, COLUMN, DEPTH, LENGTH, SHORT_LENGTH = range(7)


def split(value):
    high = value.astype(BF16)
    return high, (value - high.astype(F32)).astype(BF16)


def dot(a, b, dims):
    return lax.dot_general(a, b, (dims, ((), ())), preferred_element_type=F32)


NN = ((1,), (0,))
NT = ((1,), (1,))
TN = ((0,), (0,))


def matmul(left, right, dims=NN):
    rows = left.shape[0]
    high, low = split(left)
    right_high, right_low = split(right)
    both = dot(jnp.concatenate([high, low], axis=0), right_high, dims)
    return both[:rows] + both[rows:] + dot(high, right_low, dims)


def outer(left, right):
    columns = right.shape[1]
    high, low = split(left)
    right_high, right_low = split(right)
    both = dot(high, jnp.concatenate([right_high, right_low], axis=1), TN)
    return both[:, :columns] + both[:, columns:] + dot(low, right_high, TN)


def normalized(values):
    centred = values - jnp.mean(values, axis=-1, keepdims=True)
    variance = jnp.mean(centred * centred, axis=-1, keepdims=True)
    scale = lax.rsqrt(variance + norm_eps)
    return centred * scale, scale


def normalized_grad(grad, gain, normed, scale):
    inner = grad * gain
    along = jnp.mean(inner * normed, axis=-1, keepdims=True)
    return scale * (inner - jnp.mean(inner, axis=-1, keepdims=True) - normed * along)


def gelu_parts(u):
    curve = jnp.tanh(ROOT * (u + CUBE * u * u * u))
    return curve, 0.5 * u * (1.0 + curve)


def gelu_slope(u, curve):
    inner = ROOT * (1.0 + 3.0 * CUBE * u * u)
    return 0.5 * (1.0 + curve) + 0.5 * u * (1.0 - curve * curve) * inner


def rope_tables(rows):
    half = HEAD_DIM // 2
    freq = (10000.0 ** (-2.0 * np.arange(half, dtype=np.float32) / HEAD_DIM)).astype(np.float32)
    angles = np.arange(rows, dtype=np.float32)[:, None] * freq[None, :]
    cosine = np.cos(angles).astype(np.float32)
    sine = np.sin(angles).astype(np.float32)
    both = np.concatenate([cosine, cosine], axis=1)
    signed = np.concatenate([-sine, sine], axis=1)
    return (
        np.concatenate([both, both], axis=1),
        np.concatenate([signed, signed], axis=1),
        np.ascontiguousarray(cosine.T),
        np.ascontiguousarray(sine.T),
    )


def swap_halves(pair):
    half = HEAD_DIM // 2
    width = pair.shape[1]
    lane = lax.broadcasted_iota(jnp.int32, pair.shape, 1) % HEAD_DIM
    ahead = pltpu.roll(pair, width - half, 1)
    behind = pltpu.roll(pair, half, 1)
    return jnp.where(lane < half, ahead, behind)


def rows_from_heads(ref, parts):
    pair = 2 * HEAD_DIM
    top, bottom = [], []
    for part in range(parts):
        lanes = slice(part * pair, (part + 1) * pair)
        for k in range(HEADS // 2):
            even, odd = ref[2 * k, :, lanes], ref[2 * k + 1, :, lanes]
            first = lax.broadcasted_iota(jnp.int32, even.shape, 1) < HEAD_DIM
            top.append(jnp.where(first, even, pltpu.roll(odd, HEAD_DIM, 1)))
            bottom.append(jnp.where(first, pltpu.roll(even, HEAD_DIM, 1), odd))
    return jnp.concatenate(
        [jnp.concatenate(top, axis=1), jnp.concatenate(bottom, axis=1)], axis=0
    )


def rows_to_heads(rows, ref, parts):
    pair = 2 * HEAD_DIM
    half = rows.shape[0] // 2
    for part in range(parts):
        lanes = slice(part * pair, (part + 1) * pair)
        for k in range(HEADS // 2):
            at = part * D + k * pair
            top, bottom = rows[:half, at : at + pair], rows[half:, at : at + pair]
            first = lax.broadcasted_iota(jnp.int32, top.shape, 1) < HEAD_DIM
            ref[2 * k, :, lanes] = jnp.where(first, top, pltpu.roll(bottom, HEAD_DIM, 1))
            ref[2 * k + 1, :, lanes] = jnp.where(first, pltpu.roll(top, HEAD_DIM, 1), bottom)


def allowed_keys(first_row, rows, keys, length):
    key_pos = lax.broadcasted_iota(jnp.int32, (keys, rows), 0)
    query_pos = lax.broadcasted_iota(jnp.int32, (keys, rows), 1) + first_row
    return (key_pos <= query_pos) & (key_pos < length)


def attend_rows(raw, length, cos_ref, sin_ref, out_refs, rows, step, half_rows):
    packed_ref, turned_ref, lse_ref, qcat_ref, kcat_ref, vcat_ref = out_refs
    scale = HEAD_DIM ** (-0.5)
    for start in range(0, rows, step):
        part = slice(start, start + step)
        pair = raw[part, : 2 * HEAD_DIM]
        pair = pair * cos_ref[part, :] + swap_halves(pair) * sin_ref[part, :]
        lane = lax.broadcasted_iota(jnp.int32, pair.shape, 1)
        pair = jnp.where(lane < HEAD_DIM, pair * scale, pair)
        high, low = split(pair)
        qh, kh = high[:, :HEAD_DIM], high[:, HEAD_DIM:]
        ql, kl = low[:, :HEAD_DIM], low[:, HEAD_DIM:]
        vh, vl = split(raw[part, 2 * HEAD_DIM :])
        qcat_ref[part, :] = jnp.concatenate([qh, ql, qh], axis=1)
        kcat_ref[part, :] = jnp.concatenate([kh, kh, kl], axis=1)
        vcat_ref[part, :] = jnp.concatenate([vh, vh, vl], axis=1)
    value_pair = jnp.transpose(vcat_ref[:, HEAD_DIM:].astype(F32)).astype(BF16)
    value_high = value_pair[:HEAD_DIM]
    for start in range(0, rows, step):
        part = slice(start, start + step)
        keys = start + step
        scores = dot(kcat_ref[:keys, :], qcat_ref[part, :], NT)
        scores = jnp.where(allowed_keys(start, step, keys, length), scores, masked_score)
        row_max = jnp.max(scores, axis=0, keepdims=True)
        weights = jnp.exp(scores - row_max)
        total = jnp.sum(weights, axis=0, keepdims=True)
        wh, wl = split(weights)
        summed = dot(value_pair[:, :keys], wh, NN)
        summed = summed[:HEAD_DIM] + summed[HEAD_DIM:] + dot(value_high[:, :keys], wl, NN)
        turned = summed / total
        lse_ref[:, part] = jnp.broadcast_to(row_max + jnp.log(total), (8, step))
        turned_ref[:, part] = turned
    attended = jnp.transpose(
        jnp.concatenate([turned_ref[...], turned_ref[...]], axis=0)
    ).reshape(rows // (2 * half_rows), 2, half_rows, 2 * HEAD_DIM)
    lane = lax.broadcasted_iota(jnp.int32, attended[:, 0].shape, 2)
    packed_ref[...] = jnp.where(lane < HEAD_DIM, attended[:, 0], attended[:, 1])


def gathered_blocks(ids_ref, refs, distances, half_rows):
    for number, ref in enumerate(refs):
        side, part = divmod(number, 2)
        count = ref.shape[0]
        for slot in range(count):
            chip = ids_ref[CHIP] ^ distances[side][part * count + slot]
            first = pl.multiple_of((chip * 2 + side) * half_rows, 8)
            yield ref, slot, first


def first_attend_kernel(half_rows, step, distances, ids_ref, *refs):
    x_refs, (w_ref, cos_ref, sin_ref) = refs[:4], refs[4:7]
    out_refs, norm_ref, raw = refs[7:13], refs[13], refs[14]
    rows = raw.shape[0]
    total = sum(jnp.sum(ref[:, half_rows:, :], axis=0) for ref in x_refs)
    norm_ref[...] = total
    gain, shift = total[0:1], total[1:2]
    wh, wl = split(w_ref[...])
    for ref, slot, first in gathered_blocks(ids_ref, x_refs, distances, half_rows):
        hh, hl = split(normalized(ref[slot, :half_rows, :])[0] * gain + shift)
        raw[pl.ds(first, half_rows), :] = dot(hh, wh, NN) + dot(hh, wl, NN) + dot(hl, wh, NN)
    attend_rows(raw, ids_ref[LENGTH], cos_ref, sin_ref, out_refs, rows, step, half_rows)


def unpack_rows(packed_ref, raw, half_rows, parts):
    chips = packed_ref.shape[0]
    for chip in range(chips):
        for side in range(2):
            first = (chip * 2 + side) * half_rows
            pieces = [
                packed_ref[chip, :, (2 * part + side) * HEAD_DIM : (2 * part + side + 1) * HEAD_DIM]
                for part in range(parts)
            ]
            piece = pieces[0] if parts == 1 else jnp.concatenate(pieces, axis=1)
            raw[first : first + half_rows, :] = piece


def second_attend_kernel(half_rows, step, ids_ref, packed_ref, cos_ref, sin_ref, *refs):
    out_refs, raw = refs[:6], refs[6]
    rows = packed_ref.shape[0] * 2 * half_rows
    unpack_rows(packed_ref, raw, half_rows, 3)
    attend_rows(raw, ids_ref[SHORT_LENGTH], cos_ref, sin_ref, out_refs, rows, step, half_rows)


def attend_grad(
    rows, step, half_rows, length, refs, grad_ref, tables, out_ref, scratch
):
    qcat_ref, kcat_ref, vcat_ref, turned_ref, lse_ref = refs
    cos_ref, sin_ref, cos_t_ref, sin_t_ref = tables
    grad_rows, dk_acc, dv_acc, dq_t, dqkv = scratch
    scale = HEAD_DIM ** (-0.5)
    unpack_rows(grad_ref, grad_rows, half_rows, 1)
    key_pair = jnp.transpose(kcat_ref[:, HEAD_DIM:].astype(F32)).astype(BF16)
    key_high = key_pair[:HEAD_DIM]
    dk_acc[...] = jnp.zeros_like(dk_acc)
    dv_acc[...] = jnp.zeros_like(dv_acc)
    for start in range(0, rows, step):
        part = slice(start, start + step)
        keys = start + step
        grad = grad_rows[part, :]
        gh, gl = split(grad)
        gcat = jnp.concatenate([gh, gl, gh], axis=1)
        grad_t = jnp.transpose(jnp.concatenate([grad, grad], axis=1))[:HEAD_DIM]
        delta = jnp.sum(grad_t * turned_ref[:, part], axis=0, keepdims=True)
        scores = dot(kcat_ref[:keys, :], qcat_ref[part, :], NT)
        probs = jnp.where(
            allowed_keys(start, step, keys, length), jnp.exp(scores - lse_ref[0:1, part]), 0.0
        )
        grad_probs = dot(vcat_ref[:keys, :], gcat, NT)
        grad_scores = probs * (grad_probs - delta)
        ph, pw = split(probs)
        sh, sl = split(grad_scores)
        dv_acc[:keys, :] += dot(ph, gcat[:, : 2 * HEAD_DIM], NN)
        dv_acc[:keys, :HEAD_DIM] += dot(pw, gh, NN)
        dk_acc[:keys, :] += dot(sh, qcat_ref[part, : 2 * HEAD_DIM], NN)
        dk_acc[:keys, :HEAD_DIM] += dot(sl, qcat_ref[part, :HEAD_DIM], NN)
        turned = dot(key_pair[:, :keys], sh, NN)
        turned = turned[:HEAD_DIM] + turned[HEAD_DIM:] + dot(key_high[:, :keys], sl, NN)
        dq_t[:, part] = turned * scale
    half = HEAD_DIM // 2
    low, high = dq_t[:half, :], dq_t[half:, :]
    back_low = low * cos_t_ref[...] + high * sin_t_ref[...]
    back_high = high * cos_t_ref[...] - low * sin_t_ref[...]
    dq = jnp.transpose(jnp.concatenate([back_low, back_high, back_low, back_high], axis=0))
    for start in range(0, rows, step):
        part = slice(start, start + step)
        dk = dk_acc[part, :HEAD_DIM] + dk_acc[part, HEAD_DIM:]
        dk = jnp.concatenate([dk, dk], axis=1)
        dk = dk * cos_ref[part, :] - swap_halves(dk) * sin_ref[part, :]
        dv = dv_acc[part, :HEAD_DIM] + dv_acc[part, HEAD_DIM:]
        dqkv[part, :] = jnp.concatenate([dq[part, :HEAD_DIM], dk[:, :HEAD_DIM], dv], axis=1)
    chips = out_ref.shape[0]
    for chip in range(chips):
        first = chip * 2 * half_rows
        top = dqkv[first : first + half_rows, :]
        bottom = dqkv[first + half_rows : first + 2 * half_rows, :]
        pieces = []
        for part in range(3):
            lanes = slice(part * HEAD_DIM, (part + 1) * HEAD_DIM)
            pieces += [top[:, lanes], bottom[:, lanes]]
        out_ref[chip, :, :] = jnp.concatenate(pieces, axis=1)


def second_grad_kernel(half_rows, step, ids_ref, *refs):
    saved, grad_ref, tables, out_ref, scratch = refs[:5], refs[5], refs[6:10], refs[10], refs[11:]
    rows = saved[0].shape[0]
    length = ids_ref[SHORT_LENGTH]
    attend_grad(rows, step, half_rows, length, saved, grad_ref, tables, out_ref, scratch)


def first_grad_kernel(half_rows, step, distances, ids_ref, *refs):
    x_refs, saved, grad_ref, tables = refs[:4], refs[4:9], refs[9], refs[10:14]
    out_ref, m_ref, scratch = refs[14], refs[15], refs[16:]
    rows = saved[0].shape[0]
    length = ids_ref[LENGTH]
    attend_grad(rows, step, half_rows, length, saved, grad_ref, tables, out_ref, scratch[:5])
    dqkv, nh_ref, nl_ref = scratch[4:]
    for ref, slot, first in gathered_blocks(ids_ref, x_refs, distances, half_rows):
        nh, nl = split(normalized(ref[slot, :half_rows, :])[0])
        nh_ref[pl.ds(first, half_rows), :] = nh
        nl_ref[pl.ds(first, half_rows), :] = nl
    dh, dl = split(dqkv[...])
    nh = nh_ref[...]
    product = dot(nh, dh, TN) + dot(nh, dl, TN) + dot(nl_ref[...], dh, TN)
    owners, rows_each = m_ref.shape[0], m_ref.shape[1] - 8
    column = jnp.sum(dqkv[...], axis=0, keepdims=True)
    m_ref[:, :rows_each, :] = product.reshape(owners, rows_each, 3 * HEAD_DIM)
    m_ref[:, rows_each:, :] = jnp.broadcast_to(column[None], (owners, 8, 3 * HEAD_DIM))


class Loader:
    def __init__(self, ids_ref, sems):
        self.ids_ref = ids_ref
        self.sems = sems
        self.used = 0

    def start(self, src, dst):
        sem = self.sems.at[self.used]
        self.used += 1
        copy = pltpu.make_async_copy(src, dst, sem)
        copy.start()
        return copy

    def columns(self, gathered, unit, dst):
        return [[self.start(gathered.at[:, unit + k], dst.at[k])] for k in range(dst.shape[0])]

    def rows(self, gathered, unit, dst):
        run = dst.shape[0] // 4
        waits = []
        for k in range(4):
            owners = pl.ds(k * run, run)
            waits.append([self.start(gathered.at[owners, unit : unit + 4], dst.at[owners])])
        return waits


def ready(waits):
    for copy in waits:
        copy.wait()


def square(ref):
    return ref[...].reshape(D, D)


def pick(first, zero, one):
    return jnp.where(first, zero, one)


class Halves:
    def __init__(self, ids_ref, keep_ref, send_ref):
        self.zero = ids_ref[CORE] == 0
        self.keep_ref, self.send_ref = keep_ref, send_ref
        self.at = 0

    def put(self, keep, send):
        width = keep.shape[1]
        self.keep_ref[:, self.at : self.at + width] = keep
        self.send_ref[:, self.at : self.at + width] = send
        self.at += width

    def whole(self, value):
        self.put(value, value)

    def halved(self, zero, one):
        self.put(pick(self.zero, zero, one), pick(self.zero, one, zero))

    def granules(self, value, size, at):
        for k in range(value.shape[1] // (2 * size)):
            zero = value[:, 2 * k * size : (2 * k + 1) * size]
            one = value[:, (2 * k + 1) * size : (2 * k + 2) * size]
            lanes = slice(at + k * size, at + (k + 1) * size)
            self.keep_ref[:, lanes] = pick(self.zero, zero, one)
            self.send_ref[:, lanes] = pick(self.zero, one, zero)


def first_dense_kernel(
    ids_ref, stream_ref, got_ref, norm_ref, g_ref, full_ref, mixed_ref, u_ref, proj, up, down, sems
):
    load = Loader(ids_ref, sems)
    proj_wait = load.columns(g_ref, 0, proj)
    up_wait = load.columns(g_ref, 1, up)
    down_wait = load.rows(g_ref, 5, down)
    attended = rows_from_heads(got_ref, 1)
    ready(proj_wait[0])
    mixed = stream_ref[...] + matmul(attended, square(proj))
    mixed_ref[...] = mixed
    inner = normalized(mixed)[0] * norm_ref[2:3, :] + norm_ref[3:4, :]
    run = down.shape[0] // 4
    result = mixed
    for k in range(4):
        ready(up_wait[k])
        u = matmul(inner, up[k].reshape(D, D))
        u_ref[:, k * D : (k + 1) * D] = u
        hidden = gelu_parts(u)[1]
        ready(down_wait[k])
        result = result + matmul(hidden, down[k * run : (k + 1) * run].reshape(D, D))
    full_ref[...] = result


def shorten_kernel(
    ids_ref, full_ref, tail_ref, norm_ref, g_ref, short_ref, packed_ref, pool, qkv, moved, sems
):
    load = Loader(ids_ref, sems)
    pool_wait = load.columns(g_ref, 9, pool)
    qkv_wait = load.columns(g_ref, 12, qkv)
    shift_rows(full_ref, tail_ref, moved)
    rows = short_ref.shape[0]
    short = jnp.zeros((rows, D), F32)
    for i in range(3):
        ready(pool_wait[i])
        short = short + matmul(load_thirds(moved, 6 + i, rows), pool[i].reshape(D, D))
    short_ref[...] = short
    inner = normalized(short)[0] * norm_ref[4:5, :] + norm_ref[5:6, :]
    parts = []
    for i in range(3):
        ready(qkv_wait[i])
        parts.append(matmul(inner, qkv[i].reshape(D, D)))
    rows_to_heads(jnp.concatenate(parts, axis=1), packed_ref, 3)


LANES = 128
LANE_BLOCKS = D // LANES


def shift_rows(full_ref, tail_ref, moved):
    rows = full_ref.shape[0]
    for k in range(LANE_BLOCKS):
        lanes = slice(k * LANES, (k + 1) * LANES)
        moved[k, 6:8, :] = tail_ref[:, lanes]
        moved[k, 8 : 8 + rows, :] = full_ref[:, lanes]


def load_thirds(buffer, start, rows):
    pieces = [buffer[k, pl.ds(start, rows, stride=3), :] for k in range(LANE_BLOCKS)]
    return jnp.concatenate(pieces, axis=1)


def store_thirds(buffer, start, value):
    rows = value.shape[0]
    for k in range(LANE_BLOCKS):
        buffer[k, pl.ds(start, rows, stride=3), :] = value[:, k * LANES : (k + 1) * LANES]


def to_blocks(value, buffer):
    for k in range(LANE_BLOCKS):
        buffer[k, : value.shape[0], :] = value[:, k * LANES : (k + 1) * LANES]


def from_blocks(buffer, rows):
    return jnp.concatenate([buffer[k, :rows, :] for k in range(LANE_BLOCKS)], axis=1)


def kept_cotangent(ids_ref, cot_ref):
    rows = cot_ref.shape[0]
    position = lax.broadcasted_iota(jnp.int32, cot_ref.shape, 0) + ids_ref[CHIP] * rows
    return jnp.where(position < ids_ref[LENGTH], cot_ref[...], 0.0)


def ffn_backward(grad, mixed, gain, u_of, curves, up_of, down_of, proj_of, halves, size):
    normed, scale = normalized(mixed)
    halves.whole(normed)
    base = halves.at
    halves.at += 4 * D
    halves.whole(grad)
    inner = jnp.zeros_like(mixed)
    each = D // 2
    for k in range(4):
        u = u_of(k)
        curve, hidden = curves(k, u)
        du = matmul(grad, down_of(k), NT) * gelu_slope(u, curve)
        halves.granules(du, size, base + k * each)
        halves.granules(hidden, size, base + 2 * D + k * each)
        inner = inner + matmul(du, up_of(k), NT)
    grad_mixed = grad + normalized_grad(inner, gain, normed, scale)
    return grad_mixed, matmul(grad_mixed, proj_of(), NT)


def middle_kernel(size, *refs):
    (ids_ref, short_ref, got_ref, norm_ref, full_ref, cot_ref, g_ref), refs = refs[:7], refs[7:]
    late_ref, refs = refs[0], refs[1:]
    (act_ref, grad_ref, mixed_ref, keep_ref, send_ref), refs = refs[:5], refs[5:]
    proj, up, down, pool, kept, act, sems = refs
    load = Loader(ids_ref, sems)
    proj_wait = load.columns(g_ref, 15, proj)
    up_wait = load.columns(late_ref, 0, up)
    down_wait = load.rows(late_ref, 4, down)
    pool_wait = load.columns(g_ref, 16, pool)
    to_blocks(kept_cotangent(ids_ref, cot_ref), kept)
    to_blocks(full_ref[...], act)
    attended = rows_from_heads(got_ref, 1)
    run = down.shape[0] // 4
    rows = short_ref.shape[0]
    up_of = lambda k: up[k].reshape(D, D)
    down_of = lambda k: down[k * run : (k + 1) * run].reshape(D, D)
    ready(proj_wait[0])
    mixed = short_ref[...] + matmul(attended, square(proj))
    gain = norm_ref[6:7, :]
    inner = normalized(mixed)[0] * gain + norm_ref[7:8, :]
    for wait in up_wait:
        ready(wait)
    us = [matmul(inner, up_of(k)) for k in range(4)]
    gelus = [gelu_parts(u) for u in us]
    for wait in down_wait:
        ready(wait)
    result = mixed
    for k in range(4):
        result = result + matmul(gelus[k][1], down_of(k))
    grad = jnp.zeros((rows, D), F32)
    groups = []
    for i in range(3):
        ready(pool_wait[i])
        tap = pool[i].reshape(D, D)
        store_thirds(act, i, load_thirds(act, i, rows) + matmul(result, tap))
        groups.append(load_thirds(kept, i, rows))
        grad = grad + matmul(groups[i], tap, NT)
    act_ref[...] = from_blocks(act, 3 * rows)
    halves = Halves(ids_ref, keep_ref, send_ref)
    grad_mixed, grad_attended = ffn_backward(
        grad,
        mixed,
        gain,
        lambda k: us[k],
        lambda k, u: gelus[k],
        up_of,
        down_of,
        lambda: square(proj),
        halves,
        size,
    )
    rows_to_heads(grad_attended, grad_ref, 1)
    mixed_ref[...] = grad_mixed
    halves.whole(attended)
    halves.halved(grad_mixed[:, : D // 2], grad_mixed[:, D // 2 :])
    halves.whole(result)
    wide = jnp.concatenate(groups, axis=1)
    halves.halved(wide[:, : 3 * D // 2], wide[:, 3 * D // 2 :])


def lengthen_grad_kernel(
    ids_ref,
    got_ref,
    short_ref,
    mixed_ref,
    norm_ref,
    full_ref,
    tail_ref,
    g_ref,
    shifted_ref,
    keep_ref,
    send_ref,
    pool,
    qkv,
    moved,
    back,
    sems,
):
    load = Loader(ids_ref, sems)
    qkv_wait = load.columns(g_ref, 12, qkv)
    pool_wait = load.columns(g_ref, 9, pool)
    dqkv = rows_from_heads(got_ref, 3)
    rows = short_ref.shape[0]
    normed, scale = normalized(short_ref[...])
    inner = jnp.zeros((rows, D), F32)
    for i in range(3):
        ready(qkv_wait[i])
        inner = inner + matmul(dqkv[:, i * D : (i + 1) * D], qkv[i].reshape(D, D), NT)
    grad = mixed_ref[...] + normalized_grad(inner, norm_ref[4:5, :], normed, scale)
    for i in range(3):
        ready(pool_wait[i])
        store_thirds(back, i, matmul(grad, pool[i].reshape(D, D), NT))
    shifted_ref[...] = from_blocks(back, 3 * rows)
    shift_rows(full_ref, tail_ref, moved)
    halves = Halves(ids_ref, keep_ref, send_ref)
    halves.whole(normed)
    halves.halved(dqkv[:, : 3 * D // 2], dqkv[:, 3 * D // 2 :])
    for i in range(3):
        halves.whole(load_thirds(moved, 6 + i, rows))
    halves.halved(grad[:, : D // 2], grad[:, D // 2 :])


def first_dense_grad_kernel(
    size,
    ids_ref,
    shifted_ref,
    next_ref,
    cot_ref,
    mixed_in_ref,
    u_ref,
    got_ref,
    norm_ref,
    g_ref,
    grad_ref,
    mixed_ref,
    keep_ref,
    send_ref,
    proj,
    up,
    down,
    moved,
    sems,
):
    load = Loader(ids_ref, sems)
    down_wait = load.rows(g_ref, 5, down)
    up_wait = load.columns(g_ref, 1, up)
    proj_wait = load.columns(g_ref, 0, proj)
    rows = cot_ref.shape[0]
    moved[:rows, :] = shifted_ref[...]
    moved[rows : rows + 2, :] = next_ref[...]
    grad = kept_cotangent(ids_ref, cot_ref) + moved[2 : 2 + rows, :]
    run = down.shape[0] // 4

    def up_of(k):
        ready(up_wait[k])
        return up[k].reshape(D, D)

    def down_of(k):
        ready(down_wait[k])
        return down[k * run : (k + 1) * run].reshape(D, D)

    def proj_of():
        ready(proj_wait[0])
        return square(proj)

    halves = Halves(ids_ref, keep_ref, send_ref)
    grad_mixed, grad_attended = ffn_backward(
        grad,
        mixed_in_ref[...],
        norm_ref[2:3, :],
        lambda k: u_ref[:, k * D : (k + 1) * D],
        lambda k, u: gelu_parts(u),
        up_of,
        down_of,
        proj_of,
        halves,
        size,
    )
    rows_to_heads(grad_attended, grad_ref, 1)
    mixed_ref[...] = grad_mixed
    halves.whole(rows_from_heads(got_ref, 1))
    halves.halved(grad_mixed[:, : D // 2], grad_mixed[:, D // 2 :])


def input_grad_kernel(
    ids_ref, got_ref, stream_ref, mixed_ref, norm_ref, g_ref, out_ref, qkv, sems
):
    load = Loader(ids_ref, sems)
    qkv_wait = load.columns(g_ref, 0, qkv)
    dqkv = rows_from_heads(got_ref, 3)
    normed, scale = normalized(stream_ref[...])
    inner = jnp.zeros_like(normed)
    for i in range(3):
        ready(qkv_wait[i])
        inner = inner + matmul(dqkv[:, i * D : (i + 1) * D], qkv[i].reshape(D, D), NT)
    out_ref[...] = mixed_ref[...] + normalized_grad(inner, norm_ref[0:1, :], normed, scale)


class Factors:
    def __init__(self, keep_ref, got_ref):
        self.keep_ref, self.got_ref = keep_ref, got_ref
        self.at = 0

    def take(self, width):
        lanes = slice(self.at, self.at + width)
        self.at += width
        return jnp.concatenate([self.keep_ref[:, lanes], self.got_ref[:, lanes]], axis=0)


def side_halves(ids_ref, value):
    width = value.shape[1] // 2
    zero = ids_ref[SIDE] == 0
    first, second = value[:, :width], value[:, width:]
    return pick(zero, first, second), pick(zero, second, first)


def place_of(ids_ref, depth, rank, ranks):
    distance = depth ^ ids_ref[DEPTH]
    return ((distance & 1) * 2 + (distance >> 1)) * ranks + rank


def place_by_column(ids_ref, ref, rows, block, ranks):
    for depth in range(4):
        for column in range(2):
            for rank in range(ranks):
                chip = (depth * 2 + column) * ranks + rank
                place = place_of(ids_ref, depth, rank, ranks)
                ref[column ^ ids_ref[COLUMN], place, rows, :] = block(chip)


def packed_rows(rows):
    count = rows.shape[0] // 4
    return jnp.concatenate([rows[i * count : (i + 1) * count] for i in range(4)], axis=1)


def place_blocks(ids_ref, ref, at, product, each, ranks):
    rows = slice(at, at + each)
    place_by_column(
        ids_ref, ref, rows, lambda chip: product[chip * each : (chip + 1) * each], ranks
    )
    return at + each


def place_sums(ids_ref, ref, at, value, ranks):
    total = jnp.broadcast_to(jnp.sum(value, axis=0, keepdims=True), (8, value.shape[1]))
    place_by_column(ids_ref, ref, slice(at, at + 8), lambda chip: total, ranks)
    return at + 8


def place_packed(ids_ref, ref, at, product, each, ranks):
    rows = slice(at, at + each // 4)
    place_by_column(
        ids_ref,
        ref,
        rows,
        lambda chip: packed_rows(product[chip * each : (chip + 1) * each]),
        ranks,
    )
    return at + each // 4


def place_by_side(ids_ref, refs, at, products, each, ranks):
    zero = ids_ref[COLUMN] == 0
    for depth in range(4):
        for rank in range(ranks):
            first = ((depth * 2) * ranks + rank) * each
            second = ((depth * 2 + 1) * ranks + rank) * each
            place = place_of(ids_ref, depth, rank, ranks)
            for side in range(2):
                far = side ^ ids_ref[SIDE]
                one = products[side][first : first + each]
                two = products[side][second : second + each]
                refs[0][place, far, at : at + each, :] = pick(zero, one, two)
                refs[1][place, far, at : at + each, :] = pick(zero, two, one)
    return at + each


def dense_products_kernel(ranks, size, each, ids_ref, keep_ref, got_ref, *refs):
    up_refs, down_refs = refs[:2], refs[2:]
    factors = Factors(keep_ref, got_ref)
    normed, du, hidden, grad = (factors.take(w * D) for w in (1, 2, 2, 1))
    attended, grad_mixed = factors.take(D), factors.take(D // 2)
    for ref, half, narrow in zip(
        up_refs, side_halves(ids_ref, du), side_halves(ids_ref, grad_mixed)
    ):
        at = place_blocks(ids_ref, ref, 0, outer(normed, half), each, ranks)
        at = place_sums(ids_ref, ref, at, half, ranks)
        place_packed(ids_ref, ref, at, outer(attended, narrow), each, ranks)
    product = outer(hidden, grad).reshape(D // each, 2, size // 2, D)
    sides = [product[:, side].reshape(-1, D) for side in range(2)]
    place_by_side(ids_ref, down_refs, 0, sides, size // 2, ranks)


def shorten_products_kernel(
    ranks, each, ids_ref, keep_ref, got_ref, up_keep_ref, up_got_ref, *refs
):
    factors = Factors(keep_ref, got_ref)
    normed, dqkv = factors.take(D), factors.take(3 * D // 2)
    shifted = [factors.take(D) for _ in range(3)]
    grad = factors.take(D // 2)
    factors = Factors(up_keep_ref, up_got_ref)
    factors.at = 15 * D // 2
    short, groups = factors.take(D), factors.take(3 * D // 2)
    for ref, half, narrow, wide in zip(
        refs,
        side_halves(ids_ref, dqkv),
        side_halves(ids_ref, grad),
        side_halves(ids_ref, groups),
    ):
        at = place_blocks(ids_ref, ref, 0, outer(normed, half), each, ranks)
        at = place_sums(ids_ref, ref, at, half, ranks)
        taps = jnp.concatenate([outer(rows, narrow) for rows in shifted], axis=1)
        at = place_blocks(ids_ref, ref, at, taps, each, ranks)
        place_blocks(ids_ref, ref, at, outer(short, wide), each, ranks)


PER_US = 1.1e+08
SMEM = pl.BlockSpec(memory_space=pltpu.SMEM)
VMEM = pl.BlockSpec(memory_space=pltpu.VMEM)
ANY = pl.BlockSpec(memory_space=pl.ANY)


def attend_outs(rows, half_rows):
    width = 3 * HEAD_DIM
    return [
        shape(rows // (2 * half_rows), half_rows, 2 * HEAD_DIM),
        shape(HEAD_DIM, rows),
        shape(8, rows),
        jax.ShapeDtypeStruct((rows, width), BF16),
        jax.ShapeDtypeStruct((rows, width), BF16),
        jax.ShapeDtypeStruct((rows, width), BF16),
    ]


def shape(*dims):
    return jax.ShapeDtypeStruct(dims, F32)


def call(time, kernel, outs, scratch, ids, args, weights=(), copies=0):
    scratch = list(scratch)
    if copies:
        scratch.append(pltpu.SemaphoreType.DMA((copies,)))
    return pl.pallas_call(
        kernel,
        out_shape=list(outs),
        in_specs=[SMEM] + [VMEM] * len(args) + [ANY] * len(weights),
        out_specs=[VMEM] * len(outs),
        scratch_shapes=scratch,
        compiler_params=pltpu.CompilerParams(vmem_limit_bytes=VMEM_LIMIT),
        cost_estimate=pl.CostEstimate(
            flops=int(time * PER_US), bytes_accessed=0, transcendentals=0
        ),
    )(ids, *args, *weights)


def query_step(rows):
    return math.gcd(rows, 256)


def bit_count(size):
    return size.bit_length() - 1


def swap_with(value, axis, size, mask):
    return lax.ppermute(value, axis, [(i, i ^ mask) for i in range(size)])


def by_bit(bit, own, other):
    return jnp.where(bit == 0, jnp.stack([own, other]), jnp.stack([other, own]))


class Layout:
    def __init__(self, groups, ranks, cores):
        self.groups = groups
        self.ranks = ranks
        self.cores = cores
        self.chips = HEADS * ranks
        self.devices = self.chips * cores
        self.chip_axes = ("z", "x", "r") if ranks > 1 else ("z", "x")

    def chip(self):
        return lax.axis_index(("z", "x", "r"))

    def swap_chip(self, value, mask):
        return swap_with(value, self.chip_axes, self.chips, mask)

    def swap_core(self, value):
        return swap_with(value, "s", 2, 1)

    def exchange_cores(self, value):
        core = lax.axis_index("s")
        own = lax.dynamic_index_in_dim(value, core, 0, keepdims=False)
        away = lax.dynamic_index_in_dim(value, 1 - core, 0, keepdims=False)
        return by_bit(core, own, self.swap_core(away))

    def shift_chip(self, value, distance):
        chips = range(self.chips)
        route = [(i - distance, i) for i in chips if i - distance in chips]
        return lax.ppermute(value, self.chip_axes, route)

    def gather_chips(self, value, masks):
        held = value[None]
        for mask in masks[:-1]:
            held = jnp.concatenate([held, self.swap_chip(held, mask)], axis=0)
        return [held, self.swap_chip(held, masks[-1])]

    def distances(self, masks):
        found = [0]
        for mask in masks:
            found = found + [d ^ mask for d in found]
        return found

    def heads_to_rows(self, value):
        value = value.reshape((HEADS, self.ranks) + value.shape[1:])
        mine = lax.dynamic_index_in_dim(value, lax.axis_index("r"), 1, keepdims=False)
        return lax.all_to_all(mine, ("z", "x"), 0, 0, tiled=True)

    def rows_to_heads(self, value):
        got = lax.all_to_all(value, ("z", "x"), 0, 0, tiled=True)
        if self.ranks > 1:
            got = lax.all_gather(got, "r", axis=1, tiled=False)
            got = got.reshape((self.chips,) + value.shape[1:])
        return got

    def join_sides(self, value):
        return by_bit(lax.axis_index("b") % 2, value, swap_with(value, "b", self.groups, 1))

    def join_cores(self, value, each):
        core = lax.axis_index("s")
        both = value[:, 2 * each :]

        def rows_of(owner):
            rows = lax.dynamic_slice_in_dim(value, owner * each, each, 1)
            return jnp.concatenate([rows, both], axis=1)

        return by_bit(core, rows_of(core), self.swap_core(rows_of(1 - core)))

    def sum_batch(self, value):
        for place in range(bit_count(self.groups)):
            value = value + swap_with(value, "b", self.groups, 1 << place)
        return value


class Reduction:
    def __init__(self, layout, batch_first, keep, send):
        self.layout = layout
        self.batch_first = batch_first
        self.keep, self.send = keep, send
        self.stage = 0

    def step(self):
        groups, ranks = self.layout.groups, self.layout.ranks
        axes = (("b", groups, 1), ("x", 2, 1), ("z", 4, 1), ("z", 4, 2))
        if not self.batch_first:
            axes = (axes[1], axes[0]) + axes[2:]
        got = swap_with(self.send, *axes[self.stage])
        if self.stage == 0:
            stay, away = (0, 1) if self.batch_first else ((slice(None), 0), (slice(None), 1))
        else:
            count = got.shape[0] // 2
            stay, away = slice(0, count), slice(count, None)
        if self.stage < 3:
            self.keep, self.send = self.keep[stay] + got[stay], self.keep[away] + got[away]
        else:
            self.keep = self.last(self.keep + got)
        self.stage += 1

    def last(self, value):
        if self.layout.ranks > 1:
            rank = lax.axis_index("r")
            keep = lax.dynamic_index_in_dim(value, rank, 0, keepdims=False)
            send = lax.dynamic_index_in_dim(value, 1 - rank, 0, keepdims=False)
            value = keep + swap_with(send, "r", 2, 1)
        else:
            value = value[0]
        for place in range(1, bit_count(self.layout.groups)):
            value = value + swap_with(value, "b", self.layout.groups, 1 << place)
        return value

    def finish(self):
        while self.stage < 4:
            self.step()
        return self.keep


def tied(value, *reductions):
    value, kept = lax.optimization_barrier((value, [r.keep for r in reductions]))
    for r, keep in zip(reductions, kept):
        r.keep = keep
    return value


def column_blocks(mat):
    return [mat[:, i * D : (i + 1) * D] for i in range(mat.shape[1] // D)]


def update(grad, weight, velocity, average, rate):
    momentum = momentum_decay * velocity + grad
    updated = weight - rate * (grad + momentum_decay * momentum)
    smooth = average_decay * average + (1.0 - average_decay) * updated
    return (momentum, smooth, updated)


def with_norm(product, columns, gain, shift, weight):
    grad = gain * product + shift * columns
    return grad, jnp.sum(weight * product, axis=1), jnp.sum(weight * columns, axis=1)


def shards(layout, rate, args):
    inputs, lengths, cotangent = args[:3]
    weights, velocities, averages = args[3:9], args[9:15], args[15:21]
    qkv_w, proj_w, up_w, down_w, pool_w, norm_w = weights
    half = inputs.shape[1]
    rows = 2 * half
    short_half, short_rows = half // 3, rows // 3
    each = qkv_w.shape[1]
    ff_each = down_w.shape[1]
    owners, chips, ranks = layout.devices, layout.chips, layout.ranks
    chip = layout.chip()
    core = lax.axis_index("s")
    side = lax.axis_index("b") % 2
    owner = chip * layout.cores + core
    length = lengths[core]
    places = [chip, core, side, lax.axis_index("x"), lax.axis_index("z")]
    ids = jnp.stack(places + [length, length // 3]).astype(jnp.int32)
    seq = chips * rows
    short_seq = seq // 3
    bits = bit_count(chips)

    norm_local = jnp.transpose(norm_w, (0, 2, 1)).reshape(8, each)
    norm_lanes = lax.dynamic_update_slice(
        jnp.zeros((8, D), F32), norm_local, (0, owner * each)
    )
    carried = jnp.concatenate([inputs, jnp.broadcast_to(norm_lanes, (2, 8, D))], axis=1)
    carried = layout.exchange_cores(carried)
    stream = carried[:, :half].reshape(rows, D)
    masks_a = tuple(1 << i for i in reversed(range(bits)))
    masks_b = (1,) + tuple(1 << i for i in reversed(range(1, bits)))
    distances = (layout.distances(masks_a), layout.distances(masks_b))
    blocks = layout.gather_chips(carried[0], masks_a) + layout.gather_chips(carried[1], masks_b)

    head_cols = jnp.transpose(qkv_w[0].reshape(each, 3, HEADS, HEAD_DIM), (2, 0, 1, 3))
    head_cols = head_cols.reshape(HEADS, each, 3 * HEAD_DIM)
    head_cols = jnp.repeat(head_cols, ranks * layout.cores, axis=0)
    wide_axes = layout.chip_axes + ("s",)
    head_w = lax.all_to_all(head_cols, wide_axes, 0, 0, tiled=True)
    head_w = head_w.reshape(D, 3 * HEAD_DIM)

    units = lambda pieces: jnp.concatenate(pieces, axis=0).reshape(-1, each, D)
    packed = units(
        [proj_w[0]]
        + column_blocks(up_w[0])
        + [down_w[0]]
        + column_blocks(pool_w[0])
        + column_blocks(qkv_w[1])
        + [proj_w[1]]
        + column_blocks(pool_w[1])
    )
    gathered = lax.all_gather(packed, wide_axes, axis=0, tiled=False)
    second = units(column_blocks(up_w[1]) + [down_w[1]])
    second = lax.all_gather(second, wide_axes, axis=0, tiled=False)
    last = units(column_blocks(qkv_w[0]))
    last = lax.all_gather(last, wide_axes, axis=0, tiled=False)

    cos, sin, cos_t, sin_t = rope_tables(seq)
    tables = (cos, sin)
    tables_t = (cos_t, sin_t)
    short_tables = (cos[:short_seq], sin[:short_seq])
    short_tables_t = (cos_t[:, :short_seq], sin_t[:, :short_seq])
    step = query_step(seq)
    short_step = query_step(short_seq)
    vmem = lambda *dims: pltpu.VMEM(dims, F32)
    column_buffer = lambda count: vmem(count, owners, each, D)
    row_buffer = vmem(owners, 4, each, D)
    blocks_of = lambda count: vmem(LANE_BLOCKS, count, LANES)

    outs = call(
        10,
        functools.partial(first_attend_kernel, half, step, distances),
        attend_outs(seq, half) + [shape(8, D)],
        [vmem(seq, 3 * HEAD_DIM)],
        ids,
        [*blocks, head_w, *tables],
    )
    saved0, norm = (outs[3], outs[4], outs[5], outs[1], outs[2]), outs[6]
    got0 = layout.heads_to_rows(outs[0])
    full, mixed0, u0 = call(
        8,
        first_dense_kernel,
        [shape(rows, D), shape(rows, D), shape(rows, 4 * D)],
        [column_buffer(1), column_buffer(4), row_buffer],
        ids,
        [stream, got0, norm],
        [gathered],
        9,
    )

    tail = layout.shift_chip(full[-2:], 1)
    shortened, to_send = call(
        5,
        shorten_kernel,
        [shape(short_rows, D), shape(HEADS, short_half, 6 * HEAD_DIM)],
        [column_buffer(3), column_buffer(3), blocks_of(rows + 16)],
        ids,
        [full, tail, norm],
        [gathered],
        6,
    )
    outs = call(
        3,
        functools.partial(second_attend_kernel, short_half, short_step),
        attend_outs(short_seq, short_half),
        [vmem(short_seq, 3 * HEAD_DIM)],
        ids,
        [layout.rows_to_heads(to_send), *short_tables],
    )
    saved1 = (outs[3], outs[4], outs[5], outs[1], outs[2])
    got1 = layout.heads_to_rows(outs[0])
    cot = layout.exchange_cores(cotangent).reshape(rows, D)
    middle_wide = 10 * D
    activations, grad_att1, grad_mixed1, keep_a, send_a = call(
        13,
        functools.partial(middle_kernel, ff_each),
        [
            shape(rows, D),
            shape(HEADS, short_half, 2 * HEAD_DIM),
            shape(short_rows, D),
            shape(short_rows, middle_wide),
            shape(short_rows, middle_wide),
        ],
        [column_buffer(1), column_buffer(4), row_buffer, column_buffer(3)]
        + [blocks_of(rows + 8), blocks_of(rows + 8)],
        ids,
        [shortened, got1, norm, full, cot],
        [gathered, second],
        12,
    )

    depth = 4 * ranks
    pair = 2 * each
    up_rows = pair + 8
    up_out = shape(2, depth, up_rows + each // 2, D)
    down_out = shape(depth, 2, ff_each // 2, D)
    got_a = layout.swap_core(send_a)
    up_keep, up_send, down_keep, down_send = call(
        6,
        functools.partial(dense_products_kernel, ranks, ff_each, pair),
        [up_out, up_out, down_out, down_out],
        [],
        ids,
        [keep_a, got_a],
    )
    red_up1 = Reduction(layout, True, up_keep, up_send)
    red_down1 = Reduction(layout, False, down_keep, down_send)

    scratch = lambda count: [
        vmem(count, HEAD_DIM),
        vmem(count, 2 * HEAD_DIM),
        vmem(count, 2 * HEAD_DIM),
        vmem(HEAD_DIM, count),
        vmem(count, 3 * HEAD_DIM),
    ]
    got = layout.rows_to_heads(grad_att1)
    got = tied(got, red_up1, red_down1)
    (to_send,) = call(
        4,
        functools.partial(second_grad_kernel, short_half, short_step),
        [shape(chips, short_half, 6 * HEAD_DIM)],
        scratch(short_seq),
        ids,
        [*saved1, got, *short_tables, *short_tables_t],
    )
    got = layout.heads_to_rows(to_send)
    got, red_down1.send = lax.optimization_barrier((got, red_down1.send))
    grad_shifted, keep_b, send_b = call(
        6.5,
        lengthen_grad_kernel,
        [shape(rows, D), shape(short_rows, 6 * D), shape(short_rows, 6 * D)],
        [column_buffer(3), column_buffer(3), blocks_of(rows + 16), blocks_of(rows + 8)],
        ids,
        [got, shortened, grad_mixed1, norm, full, tail],
        [gathered],
        6,
    )
    head = layout.shift_chip(grad_shifted[:2], -1)
    pool_out = shape(2, depth, up_rows + 2 * pair, 3 * D // 4)
    pool_keep, pool_send = call(
        7,
        functools.partial(shorten_products_kernel, ranks, pair),
        [pool_out, pool_out],
        [],
        ids,
        [keep_b, layout.swap_core(send_b), keep_a, got_a],
    )
    red_pool = Reduction(layout, True, pool_keep, pool_send)
    red_up1.step()
    head = tied(head, red_up1)
    head = tied(head, red_pool)
    first_wide = 15 * D // 2
    grad_att0, grad_mixed0, keep_c, send_c = call(
        12.5,
        functools.partial(first_dense_grad_kernel, ff_each),
        [
            shape(HEADS, half, 2 * HEAD_DIM),
            shape(rows, D),
            shape(rows, first_wide),
            shape(rows, first_wide),
        ],
        [column_buffer(1), column_buffer(4), row_buffer, vmem(rows + 8, D)],
        ids,
        [grad_shifted, head, cot, mixed0, u0, got0, norm],
        [gathered],
        9,
    )
    up_keep, up_send, down_keep, down_send = call(
        9,
        functools.partial(dense_products_kernel, ranks, ff_each, pair),
        [up_out, up_out, down_out, down_out],
        [],
        ids,
        [keep_c, layout.swap_core(send_c)],
    )
    red_up0 = Reduction(layout, True, up_keep, up_send)
    red_down0 = Reduction(layout, False, down_keep, down_send)
    got = layout.rows_to_heads(grad_att0)
    got = tied(got, red_up0, red_down0)
    got = tied(got, red_up1, red_down1)
    red_up1.step()
    red_down1.step()
    to_send, product = call(
        16,
        functools.partial(first_grad_kernel, half, step, distances),
        [shape(chips, half, 6 * HEAD_DIM), shape(owners, each + 8, 3 * HEAD_DIM)],
        scratch(seq) + [pltpu.VMEM((seq, D), BF16), pltpu.VMEM((seq, D), BF16)],
        ids,
        [*blocks, *saved0, got, *tables, *tables_t],
    )
    red_pool.step()
    to_send = tied(to_send, red_pool)
    got = layout.heads_to_rows(to_send)
    got, product = lax.optimization_barrier((got, product))
    (input_grad,) = call(
        5,
        input_grad_kernel,
        [shape(rows, D)],
        [column_buffer(3)],
        ids,
        [got, stream, grad_mixed0, norm],
        [last],
        3,
    )
    input_grad = layout.exchange_cores(input_grad.reshape(2, half, D))
    activations = layout.exchange_cores(activations.reshape(2, half, D))

    product = product.reshape(HEADS, ranks, layout.cores, each + 8, 3 * HEAD_DIM)
    product = lax.dynamic_index_in_dim(product, lax.axis_index("r"), 1, keepdims=False)
    keep = lax.dynamic_index_in_dim(product, core, 1, keepdims=False)
    away = lax.dynamic_index_in_dim(product, 1 - core, 1, keepdims=False)
    product = layout.sum_batch(keep + layout.swap_core(away))
    product = lax.all_to_all(product, ("z", "x"), 0, 0, tiled=True)
    product = jnp.transpose(
        product.reshape(HEADS, each + 8, 3, HEAD_DIM), (1, 2, 0, 3)
    ).reshape(each + 8, 3 * D)

    def up_columns(joined):
        value = joined.reshape(2, 2, each + 8, D // ff_each, ff_each)
        return jnp.transpose(value, (2, 1, 3, 0, 4)).reshape(each + 8, 4 * D)

    def plain_columns(joined):
        return jnp.transpose(joined, (2, 0, 1, 3)).reshape(joined.shape[2], -1)

    def packed_columns(value):
        value = value.reshape(2, each // 2, 4, D // 4)
        value = jnp.transpose(value, (0, 2, 1, 3)).reshape(2, pair, D // 4)
        return plain_columns(layout.join_cores(value, each))

    joined = layout.join_sides(
        jnp.concatenate([red_up1.finish(), red_down1.finish()], axis=0)
    )
    up_g1 = up_columns(layout.join_cores(joined[:, :up_rows], each))
    proj_g1 = packed_columns(joined[:, up_rows : up_rows + each // 2])
    down_g1 = joined[:, up_rows + each // 2 :].reshape(ff_each, D)
    joined = layout.join_sides(red_pool.finish())
    qkv_g1 = plain_columns(layout.join_cores(joined[:, :up_rows], each))
    taps = layout.join_cores(joined[:, up_rows : up_rows + pair], each)
    taps = taps.reshape(2, 2, each, 3, D // 4)
    pool_g0 = jnp.transpose(taps, (2, 3, 0, 1, 4)).reshape(each, 3 * D)
    pool_g1 = plain_columns(layout.join_cores(joined[:, up_rows + pair :], each))
    joined = layout.join_sides(
        jnp.concatenate([red_up0.finish(), red_down0.finish()], axis=0)
    )
    up_g0 = up_columns(layout.join_cores(joined[:, :up_rows], each))
    proj_g0 = packed_columns(joined[:, up_rows : up_rows + each // 2])
    down_g0 = joined[:, up_rows + each // 2 :].reshape(ff_each, D)

    def own(block, number):
        return norm_w[block][:, number : number + 1]

    qkv_g0, own0, own1 = with_norm(
        product[:each], product[each : each + 1], own(0, 0), own(0, 1), qkv_w[0]
    )
    up_g0, own2, own3 = with_norm(
        up_g0[:each], up_g0[each : each + 1], own(0, 2), own(0, 3), up_w[0]
    )
    qkv_g1, own4, own5 = with_norm(
        qkv_g1[:each], qkv_g1[each : each + 1], own(1, 0), own(1, 1), qkv_w[1]
    )
    up_g1, own6, own7 = with_norm(
        up_g1[:each], up_g1[each : each + 1], own(1, 2), own(1, 3), up_w[1]
    )
    norm_g0 = jnp.stack([own0, own1, own2, own3], axis=1)
    norm_g1 = jnp.stack([own4, own5, own6, own7], axis=1)
    grads = [
        jnp.stack(pair)
        for pair in (
            (qkv_g0, qkv_g1),
            (proj_g0, proj_g1),
            (up_g0, up_g1),
            (down_g0, down_g1),
            (pool_g0, pool_g1),
            (norm_g0, norm_g1),
        )
    ]
    results = [
        update(grads[i], weights[i], velocities[i], averages[i], rate) for i in range(6)
    ]
    return (
        (activations, input_grad)
        + tuple(grads)
        + tuple(r[0] for r in results)
        + tuple(r[1] for r in results)
        + tuple(r[2] for r in results)
    )


def solution(mesh):
    groups, wide = mesh.shape["batch"], mesh.shape["wide"]

    def program(*args):
        cores = args[0].shape[0] // groups
        ranks = wide // (HEADS * cores)
        layout = Layout(groups, ranks, cores)
        rate = 0.5 / math.sqrt(math.prod(args[0].shape))
        dims = (groups, 4, 2, ranks, cores)
        fine = Mesh(mesh.devices.reshape(dims), ("b", "z", "x", "r", "s"))
        rows = ("z", "x", "r", "s")
        stream = P("b", rows, None)
        weight = P(None, rows, None)
        return jax.shard_map(
            lambda *local: shards(layout, rate, local),
            mesh=fine,
            in_specs=(stream, P("b"), stream) + (weight,) * 18,
            out_specs=(stream, stream) + (weight,) * 24,
            check_vma=False,
        )(*args)

    return program
```
